32 devices in a mesh: slide: 2 (over y), tile: 16 (over z, x, core).
Axes of the slice: x: 2, y: 2, z: 4, core: 2. Of those that a mesh axis runs over, the one named last changes fastest.
Arguments:
- fine_level: bfloat16 [2, 128, 256, 256], P('slide', 'tile'), may hold values from -6 to 6
- coarse_level: bfloat16 [2, 64, 128, 256], P('slide', 'tile'), may hold values from -6 to 6
- fine_kernel: bfloat16 [256, 9, 128], replicated, may hold values from -0.125 to 0.125
- coarse_kernel: bfloat16 [256, 9, 128], replicated, may hold values from -0.125 to 0.125
- fine_gain: float32 [128], replicated, may hold values from 0.25 to 1.75
- fine_offset: float32 [128], replicated, may hold values from -3 to 3
- coarse_gain: float32 [128], replicated, may hold values from 0.25 to 1.75
- coarse_offset: float32 [128], replicated, may hold values from -3 to 3
- class_kernel: bfloat16 [8, 128], replicated
- class_offset: float32 [8], replicated, may hold values from -4 to 4
- tissue_labels: int32 [2, 128, 256], P('slide', 'tile'), may hold values from -1 to 7, as said below
Outputs:
- loss: float32 [], replicated
- head_grads: float32 [12, 128], replicated
- conv_grads: float32 [256, 2, 9, 128], P('tile')
The draws below stay inside these ranges and needn't reach their ends.
Inputs may be any that keep to these rules, and one draw needn't show every extreme that they name: `tissue_labels`: -1 marks a pixel without tissue, other values are classes.
All inputs are finite; a program needn't handle non-finite values.
Results may differ from the reference program's by a relative error of at most 0.0033.
Values may be sent and summed in bfloat16 or wider, within the bound.
A program may use at most 128 MiB of HBM per device.

```python
import jax
import jax.numpy as jnp
from jax import lax

FPN_CH = 256
HEAD_CH = 128
GROUPS = 32
CLASSES = 8
COLS = 256
SLIDES = 2
ROWS = 128


def draw_class_kernel(key, part):
    first_key = jax.random.fold_in(jax.random.fold_in(key, 71), 0)
    base = jax.random.normal(first_key, (CLASSES, HEAD_CH), jnp.float32) / jnp.sqrt(jnp.float32(HEAD_CH))
    return base.astype(jnp.bfloat16)


def draw_tissue_labels(key, part):
    first_key, second_key = jax.random.split(jax.random.fold_in(key, 53))
    shape = (SLIDES, ROWS, COLS)
    draws = jax.random.randint(first_key, shape, 0, 1000, dtype=jnp.int32)
    classes = jax.random.randint(second_key, shape, 0, CLASSES, dtype=jnp.int32)
    row_index = lax.broadcasted_iota(jnp.int32, shape, 1)
    threshold = 250 + 500 * row_index // ROWS
    return jnp.where(draws < threshold, classes, -1).astype(jnp.int32)


def strengthened(result, stream_key, source, target, blocks, factor):
    def block_of(axis_at):
        return (jnp.arange(result.shape[axis_at]) // (result.shape[axis_at] // blocks)).reshape((-1,) + (1,) * (result.ndim - 1 - axis_at))

    one_side = jax.random.permutation(stream_key, blocks)[block_of(target)]
    other_side = (block_of(target) + blocks // 2) % blocks
    return jnp.where((block_of(source) == one_side) | (block_of(source) == other_side), factor * result, result)


def level_of(rng, extent, cuts, smallest, top_value):
    level = 1.0
    for axis_at, shards_of in cuts:
        steps = jax.random.uniform(jax.random.fold_in(jax.random.fold_in(rng, 6), axis_at), (shards_of,), jnp.float32, smallest / len(cuts), top_value / len(cuts))
        level = level * jnp.repeat(jnp.exp(steps), extent[axis_at] // shards_of).reshape((-1,) + (1,) * (len(extent) - 1 - axis_at))
    return level


def noise(stream_key, shape, scale, limit, cuts=(), kind=jnp.bfloat16):
    values = scale * jax.random.normal(stream_key, shape, jnp.float32)
    if cuts:
        values = values * level_of(stream_key, shape, cuts, -0.22, 0.18)
    return jnp.clip(values, -limit, limit).astype(kind)


def gaussian_with(key, extent, scale, limit, cuts, heavy, kind=jnp.bfloat16):
    entries = scale * jax.random.normal(key, extent, jnp.float32)
    if cuts:
        entries = entries * level_of(key, extent, cuts, -0.22, 0.18)
    return jnp.clip(strengthened(entries, jax.random.fold_in(key, 3), *heavy), -limit, limit).astype(kind)


def setup_inputs(seed: int = 0) -> dict:
    key_of = jax.random.split(jax.random.key(seed), 12)
    return {
        "fine_level": gaussian_with(key_of[0], (SLIDES, ROWS, COLS, FPN_CH), 1.0, 6.0, ((0, 2), (1, 16)), (1, 3, 16, 2.0)),
        "coarse_level": gaussian_with(key_of[1], (SLIDES, ROWS // 2, COLS // 2, FPN_CH), 1.0, 6.0, ((0, 2), (1, 16)), (1, 3, 16, 2.0)),
        "fine_kernel": noise(key_of[2], (FPN_CH, 9, HEAD_CH), (9 * FPN_CH) ** -0.5, 0.125),
        "coarse_kernel": noise(key_of[3], (FPN_CH, 9, HEAD_CH), (9 * FPN_CH) ** -0.5, 0.125),
        "fine_gain": jnp.clip(1.0 + 0.15 * jax.random.normal(key_of[4], (HEAD_CH,), jnp.float32), 0.25, 1.75),
        "fine_offset": noise(key_of[5], (HEAD_CH,), 0.5, 3.0, (), jnp.float32),
        "coarse_gain": jnp.clip(1.0 + 0.15 * jax.random.normal(key_of[6], (HEAD_CH,), jnp.float32), 0.25, 1.75),
        "coarse_offset": noise(key_of[7], (HEAD_CH,), 0.5, 3.0, (), jnp.float32),
        "class_kernel": draw_class_kernel(jax.random.fold_in(key_of[11], 71), 0),
        "class_offset": noise(key_of[9], (CLASSES,), 1.0, 4.0, (), jnp.float32),
        "tissue_labels": draw_tissue_labels(jax.random.fold_in(key_of[11], 71), 0),
    }


epsilon = 1e-05

def shifted(padded, height, width, position):
    row_step = position // 3
    col_step = position % 3
    return padded[row_step:row_step + height, col_step:col_step + width].reshape(height * width, -1)

def convolve(padded, kernel, height, width):
    total = jnp.zeros((height * width, kernel.shape[2]), jnp.float32)
    for position in range(9):
        total = total + jnp.dot(shifted(padded, height, width, position), kernel[:, position, :], preferred_element_type=jnp.float32)
    return total

def group_sums(values, groups):
    return values.reshape(values.shape[0], groups, -1).sum(axis=(0, 2))

def spread(per_group, channels):
    return jnp.repeat(per_group, channels // per_group.shape[0])

def kernel_grads(padded, upstream, height, width):
    taps = [lax.dot_general(shifted(padded, height, width, position), upstream, (((0,), (0,)), ((), ())), preferred_element_type=jnp.float32) for position in range(9)]
    return jnp.stack(taps, 1)

def one_slide(level_fine, level_coarse, labels, fine_kernel, coarse_kernel, fine_gain, fine_offset, coarse_gain, coarse_offset, class_kernel, class_offset, total):
    height, width = (level_fine.shape[0], level_fine.shape[1])
    channels = fine_kernel.shape[2]
    states = []
    for level, kernel, gain, offset in ((level_fine, fine_kernel, fine_gain, fine_offset), (level_coarse, coarse_kernel, coarse_gain, coarse_offset)):
        rows_here, cols_here = (level.shape[0], level.shape[1])
        padded = jnp.pad(level, ((1, 1), (1, 1), (0, 0)))
        conv_out = convolve(padded, kernel, rows_here, cols_here)
        number = rows_here * cols_here * (channels // GROUPS)
        mean = group_sums(conv_out, GROUPS) / number
        variance = group_sums(conv_out * conv_out, GROUPS) / number - mean * mean
        scale = spread(lax.rsqrt(variance + epsilon), channels)
        normed = (conv_out - spread(mean, channels)) * scale
        pre_act = normed * gain + offset
        states.append((padded, normed, scale, pre_act, gain, number, rows_here, cols_here))
    act_fine = jnp.maximum(states[0][3], 0.0).reshape(height, width, channels)
    act_coarse = jnp.maximum(states[1][3], 0.0).reshape(height // 2, width // 2, channels)
    upsampled = jnp.repeat(jnp.repeat(act_coarse, 2, 0), 2, 1)
    merged = (act_fine + upsampled).astype(jnp.bfloat16).reshape(height * width, channels)
    logits = lax.dot_general(class_kernel, merged, (((1,), (1,)), ((), ())), preferred_element_type=jnp.float32) + class_offset[:, None]
    flat_labels = labels.reshape(-1)
    tissue = (flat_labels >= 0).astype(jnp.float32)
    onehot = (flat_labels[None, :] == jnp.arange(CLASSES, dtype=jnp.int32)[:, None]).astype(jnp.float32)
    top = lax.optimization_barrier(jnp.max(logits, axis=0))
    lse = top + jnp.log(lax.optimization_barrier(jnp.sum(jnp.exp(logits - top[None, :]), axis=0)))
    loss_sum = jnp.sum((lse - lax.optimization_barrier(jnp.sum(onehot * logits, axis=0))) * tissue)
    dlogits = ((jnp.exp(logits - lse[None, :]) - onehot) * tissue[None, :] / total).astype(jnp.bfloat16)
    class_grad = jnp.dot(dlogits, merged, preferred_element_type=jnp.float32)
    dmerged = lax.dot_general(dlogits, class_kernel, (((0,), (0,)), ((), ())), preferred_element_type=jnp.float32)
    dact_fine = dmerged
    dact_coarse = dmerged.reshape(height // 2, 2, width // 2, 2, channels).sum(axis=(1, 3)).reshape(-1, channels)
    norm_rows = []
    conv_rows = []
    for state, upstream in ((states[0], dact_fine), (states[1], dact_coarse)):
        padded, normed, scale, pre_act, gain, number, rows_here, cols_here = state
        dpre = upstream * (pre_act > 0).astype(jnp.float32)
        norm_rows.append(lax.optimization_barrier(jnp.sum(dpre * normed, axis=0)))
        norm_rows.append(lax.optimization_barrier(jnp.sum(dpre, axis=0)))
        dnorm = dpre * gain
        first = spread(group_sums(dnorm, GROUPS) / number, channels)
        second = spread(group_sums(dnorm * normed, GROUPS) / number, channels)
        dconv = ((dnorm - first - normed * second) * scale).astype(jnp.bfloat16)
        conv_rows.append(kernel_grads(padded, dconv, rows_here, cols_here))
    head = jnp.concatenate([jnp.stack(norm_rows, 0), class_grad], 0)
    return (loss_sum, head, jnp.stack(conv_rows, 1))

def reference(fine_level, coarse_level, fine_kernel, coarse_kernel, fine_gain, fine_offset, coarse_gain, coarse_offset, class_kernel, class_offset, tissue_labels):
    total = jnp.sum((tissue_labels >= 0).astype(jnp.float32))

    def run(index):
        return one_slide(fine_level[index], coarse_level[index], tissue_labels[index], fine_kernel, coarse_kernel, fine_gain, fine_offset, coarse_gain, coarse_offset, class_kernel, class_offset, total)
    loss_sums, heads, convs = lax.map(run, jnp.arange(SLIDES, dtype=jnp.int32))
    return (jnp.sum(loss_sums) / total, lax.optimization_barrier(jnp.sum(heads, axis=0)), lax.optimization_barrier(jnp.sum(convs, axis=0)))
```

```python
import functools
import types

import jax
import jax.numpy as jnp
from jax import lax
from jax.experimental import pallas as pl
from jax.experimental.pallas import tpu as pltpu
from jax.sharding import PartitionSpec as P

GROUPS = 32
EPSILON = 1e-05
F32 = jnp.float32
BF16 = jnp.bfloat16
MESH = pl.DeviceIdType.MESH
VMEM = pl.BlockSpec(memory_space=pltpu.VMEM)
ANY = pl.BlockSpec(memory_space=pl.ANY)
LIMIT = 60 * 1024 * 1024
HIGH = lax.Precision.HIGHEST


def call(body, out_shape, scratch, args):
    return pl.pallas_call(
        body,
        out_shape=out_shape,
        in_specs=[ANY] * len(args),
        out_specs=jax.tree.map(lambda _: VMEM, out_shape),
        scratch_shapes=scratch,
        compiler_params=pltpu.CompilerParams(
            vmem_limit_bytes=LIMIT, collective_id=0, has_side_effects=True
        ),
    )(*args)


def store_kernel(classes, rows, grads, loss_out, head_out, grads_out, loss, sems):
    copies = [
        pltpu.make_async_copy(source, target, sems.at[at])
        for at, (source, target) in enumerate(
            ((grads, grads_out), (rows.at[pl.ds(0, 4 + classes)], head_out), (loss, loss_out))
        )
    ]
    for copy in copies[:2]:
        copy.start()
    loss[...] = rows[4 + classes : 5 + classes, 0:1]
    copies[2].start()
    for copy in copies:
        copy.wait()


def store(rows, grads, classes):
    return pl.pallas_call(
        functools.partial(store_kernel, classes),
        out_shape=(
            shape_of((1, 1)),
            shape_of((4 + classes, rows.shape[1])),
            shape_of(grads.shape),
        ),
        in_specs=[VMEM, VMEM],
        out_specs=(ANY, ANY, ANY),
        scratch_shapes=[pltpu.VMEM((1, 1), F32), dma_sems(3)],
    )(*(pltpu.with_memory_space_constraint(value, pltpu.VMEM) for value in (rows, grads)))


def shape_of(dims, dtype=F32):
    return jax.ShapeDtypeStruct(dims, dtype)


def greet(peers, meanwhile):
    barrier = pltpu.get_barrier_semaphore()
    for peer in peers:
        pl.semaphore_signal(barrier, inc=1, device_id=peer, device_id_type=MESH)
    meanwhile()
    pl.semaphore_wait(barrier, len(peers))


def ring_peers(axis, size):
    me = lax.axis_index(axis)
    return [{axis: lax.rem(me + d, size)} for d in range(1, size)]


class Spread:
    def __init__(self, axis, size, source, gather, send_sem, recv_sem):
        me = lax.axis_index(axis)
        self.copies = [
            pltpu.make_async_remote_copy(
                src_ref=source,
                dst_ref=gather.at[me],
                send_sem=send_sem,
                recv_sem=recv_sem,
                device_id={axis: lax.rem(me + d, size)},
                device_id_type=MESH,
            )
            for d in range(1, size)
        ]
        others = gather.at[pl.ds(0, size - 1)]
        self.ends = [pltpu.make_async_copy(others, others, sem) for sem in (send_sem, recv_sem)]

    def start(self):
        for copy in self.copies:
            copy.start()

    def wait(self):
        if self.copies:
            for end in self.ends:
                end.wait()


def ordered_sum(gather, size):
    total = gather[0]
    for index in range(1, size):
        total = total + gather[index]
    return total


def dma_sems(*dims):
    return pltpu.SemaphoreType.DMA(dims)


def column_of(shape, width):
    return lax.rem(lax.broadcasted_iota(jnp.int32, shape, 0), width)


def from_left(values, width):
    moved = pltpu.roll(values, 1, axis=0)
    return jnp.where(column_of(values.shape, width) == 0, 0.0, moved)


def from_right(values, width):
    moved = pltpu.roll(values, values.shape[0] - 1, axis=0)
    return jnp.where(column_of(values.shape, width) == width - 1, 0.0, moved)


def stage_plan(bits, order):
    left = list(reversed(range(bits)))
    plan = []
    for bit in order:
        place = left.index(bit)
        left = [other for other in left if other != bit]
        plan.append((bit, place, len(left)))
    return plan


def at_bits(places, count):
    index = [slice(None)] * count
    for place, value in places:
        index[place] = value
    return tuple(index)


def order_of(bits, turn):
    order = list(range(bits))
    if turn and bits > 2:
        order[1], order[2] = order[2], order[1]
    return order


def lanes_of(shape, dim=1):
    return lax.broadcasted_iota(jnp.int32, shape, dim)


def packed_groups(rows, channels):
    shape = (channels, channels)
    member = lanes_of(shape, 0) // (channels // GROUPS) == lax.rem(lanes_of(shape), GROUPS)
    sums = jnp.dot(rows, member.astype(F32), preferred_element_type=F32, precision=HIGH)
    own = lanes_of(rows.shape) // GROUPS == lanes_of(rows.shape, 0)
    return jnp.sum(jnp.where(own, sums, 0.0), axis=0, keepdims=True)


def unpacked_groups(row, channels):
    shape = (channels, channels)
    member = lax.rem(lanes_of(shape, 0), GROUPS) == lanes_of(shape) // (channels // GROUPS)
    own = lanes_of((8, channels)) // GROUPS == lanes_of((8, channels), 0)
    rows = jnp.where(own, jnp.broadcast_to(row, (8, channels)), 0.0)
    return jnp.dot(rows, member.astype(F32), preferred_element_type=F32, precision=HIGH)


PACK = 2
PIECES = 6
GRAD, SEND, RECV, KEPT = range(4)


def conv_rows(firsts, count, padded, taps, out, sums, at):
    width, depth = padded.shape[1], padded.shape[2]
    channels = taps.shape[2]
    span = count * width
    total = None
    for a in range(3):
        block = jnp.concatenate(
            [padded[pl.ds(first + a, count)].reshape(span, depth) for first in firsts], axis=0
        )
        side = jnp.concatenate([taps[3 * a + b] for b in range(3)], axis=1)
        term = jnp.dot(block, side, preferred_element_type=F32)
        total = term if total is None else total + term
    value = (
        from_left(total[:, :channels], width)
        + total[:, channels : 2 * channels]
        + from_right(total[:, 2 * channels :], width)
    )
    for index, first in enumerate(firsts):
        here = first * width if isinstance(first, int) else pl.multiple_of(first * width, width)
        out[pl.ds(here, span), :] = value[index * span : (index + 1) * span]
    sums[at : at + 1] += jnp.sum(value, axis=0, keepdims=True)
    sums[at + 1 : at + 2] += jnp.sum(value * value, axis=0, keepdims=True)


def step_kernel(tiles, slides, bits, numbers, names, keys, *refs):
    ref = types.SimpleNamespace(**dict(zip(names, refs)))
    ref.parts = dict(zip(keys, refs[len(names) :]))
    fine, coarse, labels = ref.far_fine, ref.far_coarse, ref.labels
    fine_pad, coarse_pad = ref.fine_pad, ref.coarse_pad
    fine_conv, coarse_conv = ref.fine_conv, ref.coarse_conv
    sums, rows, class_kernel = ref.sums, ref.rows, ref.class_kernel
    me, slide = lax.axis_index("tile"), lax.axis_index("slide")
    height, width, _ = fine.shape
    channels = fine_conv.shape[1]
    classes = class_kernel.shape[0]
    targets = dict(fine=fine_pad.at[pl.ds(1, height)], coarse=coarse_pad.at[pl.ds(1, height // 2)])
    loads = {}
    for at, name in enumerate(names):
        if name.startswith("far_"):
            name = name[4:]
            loads[name] = pltpu.make_async_copy(
                refs[at], targets.get(name, getattr(ref, name, None)), ref.load_sem.at[at]
            )

    def prepare():
        for copy in loads.values():
            copy.start()
        for name, copy in loads.items():
            if not name.startswith(("fine", "coarse")) or name.endswith(("gain", "offset")):
                copy.wait()
        tissue_here = (labels[...] >= 0).astype(F32)
        ref.count[...] = jnp.broadcast_to(
            jnp.sum(tissue_here, axis=(0, 1), keepdims=True), ref.count.shape
        )
        sums[...] = jnp.zeros_like(sums)

    greet(ring_peers("tile", tiles) + ring_peers("slide", slides), prepare)

    def edge_copies(peer, down):
        return [
            pltpu.make_async_remote_copy(
                src_ref=source.at[source.shape[0] - 1 if down else 0],
                dst_ref=target.at[0 if down else target.shape[0] - 1],
                send_sem=ref.edge_send.at[int(down), at],
                recv_sem=ref.edge_recv.at[int(down), at],
                device_id={"tile": peer},
                device_id_type=MESH,
            )
            for at, (source, target) in enumerate(((fine, fine_pad), (coarse, coarse_pad)))
        ]

    fine_gain, fine_offset = ref.fine_gain[...], ref.fine_offset[...]
    coarse_gain, coarse_offset = ref.coarse_gain[...], ref.coarse_offset[...]
    down = edge_copies(lax.rem(me + 1, tiles), True)
    up = edge_copies(lax.rem(me + tiles - 1, tiles), False)

    @pl.when(me < tiles - 1)
    def _():
        for copy in down:
            copy.start()

    @pl.when(me > 0)
    def _():
        for copy in up:
            copy.start()

    def tile_copies(at, source, gather):
        return Spread(
            "tile", tiles, source, gather, ref.tile_send.at[at], ref.tile_recv.at[at]
        )

    def slide_copies(at, source, gather):
        return Spread(
            "slide", slides, source, gather, ref.slide_send.at[at], ref.slide_recv.at[at]
        )

    counts = tile_copies(0, ref.count, ref.count_gather)
    counts.start()
    ref.count_gather[me] = ref.count[...]

    @pl.when(me == 0)
    def _():
        for padded in (fine_pad, coarse_pad):
            padded[0] = jnp.zeros(padded.shape[1:], BF16)

    @pl.when(me == tiles - 1)
    def _():
        for padded in (fine_pad, coarse_pad):
            padded[padded.shape[0] - 1] = jnp.zeros(padded.shape[1:], BF16)

    fine_steps, coarse_steps = height // PACK, height // 2 // PACK
    levels = (
        (fine_pad, ref.fine_taps, fine_conv, ref.fine_turned, height),
        (coarse_pad, ref.coarse_taps, coarse_conv, ref.coarse_turned, height // 2),
    )

    def turn(padded, turned, row):
        span = padded.shape[1]
        turned[:, row * span : (row + 1) * span] = padded[row].T

    with jax.named_scope("inner_conv"):
        for at, (padded, taps, out, turned, high) in enumerate(levels):
            for name in (("fine", "fine_taps"), ("coarse", "coarse_taps"))[at]:
                loads[name].wait()

            @pl.loop(0, (high - 2) // PACK)
            def _(step):
                conv_rows([1 + PACK * step], PACK, padded, taps, out, sums, 2 * at)

    with jax.named_scope("inner_turn"):
        for padded, _, _, turned, high in levels:
            for row in range(1, high + 1):
                turn(padded, turned, row)

    scope = jax.named_scope("edge_wait")
    scope.__enter__()

    @pl.when(me < tiles - 1)
    def _():
        for copy in down:
            copy.wait_send()
        for copy in up:
            copy.wait_recv()

    @pl.when(me > 0)
    def _():
        for copy in up:
            copy.wait_send()
        for copy in down:
            copy.wait_recv()

    scope.__exit__(None, None, None)
    with jax.named_scope("edge_conv"):
        for at, (padded, taps, out, _, high) in enumerate(levels):
            conv_rows([0, high - 1], 1, padded, taps, out, sums, 2 * at)

    ref.stat[...] = packed_groups(sums[...], channels)
    stat_copies = tile_copies(1, ref.stat, ref.stat_gather)
    stat_copies.start()
    counts.wait()
    ref.slide_count[...] = ordered_sum(ref.count_gather, tiles)
    total_copies = slide_copies(0, ref.slide_count, ref.total_gather)
    total_copies.start()
    ref.stat_gather[me] = ref.stat[...]
    ref.total_gather[slide] = ref.slide_count[...]

    for padded, _, _, turned, high in levels:
        turn(padded, turned, 0)
        turn(padded, turned, high + 1)

    scope = jax.named_scope("stat_wait")
    scope.__enter__()
    stat_copies.wait()
    total_copies.wait()
    total = ordered_sum(ref.total_gather, slides)
    count = total[0:1, 0:1]
    scope.__exit__(None, None, None)
    group_sums = unpacked_groups(ordered_sum(ref.stat_gather, tiles), channels)

    def terms_of(at, number):
        mean = group_sums[at : at + 1] / number
        variance = group_sums[at + 1 : at + 2] / number - mean * mean
        return mean, lax.rsqrt(variance + EPSILON)

    fine_mean, fine_scale = terms_of(0, numbers[0])
    coarse_mean, coarse_scale = terms_of(2, numbers[1])

    size, half = 2 * width, width // 2
    square = (classes, classes)
    offset = jnp.sum(
        jnp.where(
            lanes_of(square) == lanes_of(square, 0),
            jnp.broadcast_to(ref.class_offset[...], square),
            0.0,
        ),
        axis=1,
        keepdims=True,
    )
    rows[...] = jnp.zeros_like(rows)
    widen, fold = ref.widen, ref.fold
    fine_dpre, coarse_dpre = ref.fine_dpre, ref.coarse_dpre

    scope = jax.named_scope("head")
    scope.__enter__()

    @pl.loop(0, height // 2)
    def _(step):
        fine_at = pl.ds(pl.multiple_of(step * size, size), size)
        coarse_at = pl.ds(pl.multiple_of(step * half, half), half)
        fine_normed = (fine_conv[fine_at, :] - fine_mean) * fine_scale
        fine_pre = fine_normed * fine_gain + fine_offset
        coarse_normed = (coarse_conv[coarse_at, :] - coarse_mean) * coarse_scale
        coarse_pre = coarse_normed * coarse_gain + coarse_offset
        coarse_act = jnp.maximum(coarse_pre, 0.0)
        widen[pl.ds(0, half, stride=2), :] = coarse_act
        widen[pl.ds(1, half, stride=2), :] = coarse_act
        upsampled = widen[...]
        merged = (
            jnp.maximum(fine_pre, 0.0) + jnp.concatenate([upsampled, upsampled], axis=0)
        ).astype(BF16)
        logits = (
            lax.dot_general(
                class_kernel[...], merged, (((1,), (1,)), ((), ())), preferred_element_type=F32
            )
            + offset
        )
        label = jnp.concatenate(
            [labels[pl.ds(2 * step, 1), :], labels[pl.ds(2 * step + 1, 1), :]], axis=1
        )
        onehot = (lanes_of((classes, size), 0) == label).astype(F32)
        tissue = (label >= 0).astype(F32)
        top = jnp.max(logits, axis=0, keepdims=True)
        lse = top + jnp.log(jnp.sum(jnp.exp(logits - top), axis=0, keepdims=True))
        picked = jnp.sum(onehot * logits, axis=0, keepdims=True)
        loss = jnp.sum((lse - picked) * tissue, axis=1, keepdims=True)
        dlogits = ((jnp.exp(logits - lse) - onehot) * tissue / count).astype(BF16)
        dmerged = lax.dot_general(
            dlogits, class_kernel[...], (((0,), (0,)), ((), ())), preferred_element_type=F32
        )
        fine_d = jnp.where(fine_pre > 0, dmerged, 0.0)
        fine_dpre[fine_at, :] = fine_d
        fold[...] = dmerged[:width] + dmerged[width:]
        blocks = fold[pl.ds(0, half, stride=2), :] + fold[pl.ds(1, half, stride=2), :]
        coarse_d = jnp.where(coarse_pre > 0, blocks, 0.0)
        coarse_dpre[coarse_at, :] = coarse_d
        rows[0:1] += jnp.sum(fine_d * fine_normed, axis=0, keepdims=True)
        rows[1:2] += jnp.sum(fine_d, axis=0, keepdims=True)
        rows[2:3] += jnp.sum(coarse_d * coarse_normed, axis=0, keepdims=True)
        rows[3:4] += jnp.sum(coarse_d, axis=0, keepdims=True)
        rows[4 : 4 + classes] += jnp.dot(dlogits, merged, preferred_element_type=F32)
        rows[4 + classes : 5 + classes] += jnp.broadcast_to(loss, (1, channels))

    scope.__exit__(None, None, None)
    scope = jax.named_scope("back_wait")
    scope.__enter__()
    gains = jnp.concatenate([fine_gain, fine_gain, coarse_gain, coarse_gain] * 2, axis=0)
    ref.back[...] = packed_groups(rows[0:8] * gains, channels)
    back_copies = tile_copies(2, ref.back, ref.back_gather)
    back_copies.start()
    ref.back_gather[me] = ref.back[...]
    ref.row_sums[0] = rows[...]
    back_copies.wait()
    scope.__exit__(None, None, None)
    back = unpacked_groups(ordered_sum(ref.back_gather, tiles), channels)

    def upstream(conv, dpre, mean, scale, gain, at, number, span, shifted, steps):
        first = back[at + 1 : at + 2] / number
        second = back[at : at + 1] / number
        block = PACK * span

        @pl.loop(0, steps)
        def _(step):
            here = pl.ds(pl.multiple_of(step * block, block), block)
            normed = (conv[here, :] - mean) * scale
            dconv = (dpre[here, :] * gain - first - normed * second) * scale
            shifted[here, :] = jnp.concatenate(
                [
                    from_right(dconv, span).astype(BF16),
                    dconv.astype(BF16),
                    from_left(dconv, span).astype(BF16),
                ],
                axis=1,
            )

    mine = [lax.rem(me // (2**bit), 2) for bit in range(bits)]
    partners = [{"tile": me + (1 - 2 * mine[bit]) * (2**bit)} for bit in range(bits)]
    plans = [stage_plan(bits, order_of(bits, piece % 2)) for piece in range(PIECES)]
    final = ref.final
    across = 3 * channels
    spans = [((piece + 3) % PIECES * across, across) for piece in range(PIECES)]

    def buffer(piece, stage, kind):
        return ref.parts[kind, piece, stage]

    def stage_copy(piece, stage):
        bit, place, left = plans[piece][stage]
        if stage == 0:
            source = ref.parts[GRAD, piece, 0].at[at_bits([(place, 1 - mine[bit])], left + 1)]
        else:
            source = buffer(piece, stage, SEND)
        return pltpu.make_async_remote_copy(
            src_ref=source,
            dst_ref=buffer(piece, stage, RECV),
            send_sem=ref.stage_send.at[piece, stage],
            recv_sem=ref.stage_recv.at[piece, stage],
            device_id=partners[bit],
            device_id_type=MESH,
        )

    def piece_copies(piece):
        lanes = pl.ds(*spans[piece])
        return [
            pltpu.make_async_remote_copy(
                src_ref=final.at[slide, :, lanes],
                dst_ref=final.at[slide, :, lanes],
                send_sem=ref.piece_send.at[piece, d - 1],
                recv_sem=ref.piece_recv.at[piece, d - 1],
                device_id={"slide": lax.rem(slide + d, slides)},
                device_id_type=MESH,
            )
            for d in range(1, slides)
        ]

    done = [0] * PIECES

    def advance(piece):
        stage = done[piece]
        if stage == bits:
            return
        done[piece] += 1
        bit, place, left = plans[piece][stage]
        stage_copy(piece, stage).wait()
        if stage == 0:
            kept = ref.parts[GRAD, piece, 0].at[at_bits([(place, mine[bit])], left + 1)]
        else:
            kept = buffer(piece, stage, KEPT)
        came = buffer(piece, stage, RECV)
        if stage == bits - 1:
            final[slide, :, pl.ds(*spans[piece])] = kept[...] + came[...].astype(F32)
            for copy in piece_copies(piece):
                copy.start()
            return
        later, spot, _ = plans[piece][stage + 1]

        def part(value):
            chosen = at_bits([(spot, value)], left)
            return kept[chosen] + came[chosen].astype(F32)

        buffer(piece, stage + 1, SEND)[...] = part(1 - mine[later]).astype(BF16)
        stage_copy(piece, stage + 1).start()
        buffer(piece, stage + 1, KEPT)[...] = part(mine[later])

    def product(turned, shifted, a, span):
        pixels = shifted.shape[0]
        return jnp.dot(
            turned[:, a * span : a * span + pixels], shifted[...], preferred_element_type=F32
        )

    def row_copy(stage):
        return pltpu.make_async_remote_copy(
            src_ref=ref.row_sums.at[stage],
            dst_ref=ref.row_gather.at[stage],
            send_sem=ref.row_send.at[stage],
            recv_sem=ref.row_recv.at[stage],
            device_id=partners[stage],
            device_id_type=MESH,
        )

    head_copies = slide_copies(1, ref.row_sums.at[bits], ref.head_gather)

    def advance_rows(stage):
        row_copy(stage).wait()
        ref.row_sums[stage + 1] = ref.row_sums[stage] + ref.row_gather[stage]
        if stage + 1 < bits:
            row_copy(stage + 1).start()
        else:
            head_copies.start()
            ref.head_gather[slide] = ref.row_sums[bits]

    def begin(piece, turned, shifted, a, span):
        out = ref.parts[GRAD, piece, 0]
        out[...] = product(turned, shifted, a, span).reshape(out.shape)
        stage_copy(piece, 0).start()

    scope = jax.named_scope("grads")
    scope.__enter__()
    row_copy(0).start()
    upstream(coarse_conv, coarse_dpre, coarse_mean, coarse_scale, coarse_gain, 2, numbers[1],
             half, ref.coarse_shifted, coarse_steps)
    for a in range(3):
        begin(a, ref.coarse_turned, ref.coarse_shifted, a, half)
    upstream(fine_conv, fine_dpre, fine_mean, fine_scale, fine_gain, 0, numbers[0],
             width, ref.fine_shifted, fine_steps)
    advance(0)
    begin(3, ref.fine_turned, ref.fine_shifted, 0, width)
    advance(1)
    begin(4, ref.fine_turned, ref.fine_shifted, 1, width)
    advance(2)
    begin(5, ref.fine_turned, ref.fine_shifted, 2, width)
    scope.__exit__(None, None, None)
    scope = jax.named_scope("exchange")
    scope.__enter__()
    for stage in range(bits):
        for piece in range(PIECES // 2):
            advance(piece)
        advance_rows(stage)
        for piece in range(PIECES // 2, PIECES):
            advance(piece)
    head_copies.wait()
    row_total = ordered_sum(ref.head_gather, slides)
    ref.heads[...] = row_total
    ref.heads[4 + classes : 5 + classes] = row_total[4 + classes : 5 + classes] / count
    for piece in range(PIECES):
        for copy in piece_copies(piece):
            copy.wait()
        level, a = spans[piece][0] // across // 3, spans[piece][0] // across % 3
        whole = ordered_sum(final.at[:, :, pl.ds(*spans[piece])], slides)
        for b in range(3):
            ref.grads[pl.ds(6 * a + 2 * b + level, whole.shape[0], stride=18), :] = whole[
                :, b * channels : (b + 1) * channels
            ]
    scope.__exit__(None, None, None)


def per_device(
    fine_level,
    coarse_level,
    fine_kernel,
    coarse_kernel,
    fine_gain,
    fine_offset,
    coarse_gain,
    coarse_offset,
    class_kernel,
    class_offset,
    tissue_labels,
):
    tiles, slides = lax.axis_size("tile"), lax.axis_size("slide")
    bits = tiles.bit_length() - 1
    in_channels, _, channels = fine_kernel.shape
    classes = class_kernel.shape[0]
    fine, coarse, labels = fine_level[0], coarse_level[0], tissue_labels[0]
    height, width = fine.shape[0], fine.shape[1]
    fine_number = height * tiles * width * (channels // GROUPS)
    numbers = (float(fine_number), float(fine_number // 4))
    pixels, half = height * width, width // 2
    slide_ends = max(slides - 1, 1)
    chunk = in_channels // tiles
    row_count = -(-(5 + classes) // 8) * 8

    inputs = dict(
        fine=fine,
        fine_taps=fine_kernel.transpose(1, 0, 2),
        labels=labels,
        coarse=coarse,
        coarse_taps=coarse_kernel.transpose(1, 0, 2),
        fine_gain=fine_gain[None, :],
        fine_offset=fine_offset[None, :],
        coarse_gain=coarse_gain[None, :],
        coarse_offset=coarse_offset[None, :],
        class_kernel=class_kernel,
        class_offset=class_offset[None, :],
    )
    outputs = dict(
        heads=pltpu.VMEM((row_count, channels), F32),
        grads=pltpu.VMEM((chunk * 18, channels), F32),
    )
    line = (1, channels)
    scratch = {
        name: pltpu.VMEM(value.shape, value.dtype)
        for name, value in inputs.items()
        if name not in ("fine", "coarse")
    }
    scratch |= dict(
        final=pltpu.VMEM((slides, chunk, 18 * channels), F32),
        head_gather=pltpu.VMEM((slides, row_count, channels), F32),
        load_sem=dma_sems(len(inputs)),
        fine_pad=pltpu.VMEM((height + 2, width, in_channels), BF16),
        coarse_pad=pltpu.VMEM((height // 2 + 2, half, in_channels), BF16),
        fine_conv=pltpu.VMEM((pixels, channels), F32),
        coarse_conv=pltpu.VMEM((pixels // 4, channels), F32),
        fine_dpre=pltpu.VMEM((pixels, channels), F32),
        coarse_dpre=pltpu.VMEM((pixels // 4, channels), F32),
        fine_turned=pltpu.VMEM((in_channels, (height + 2) * width), BF16),
        coarse_turned=pltpu.VMEM((in_channels, (height // 2 + 2) * half), BF16),
        fine_shifted=pltpu.VMEM((pixels, 3 * channels), BF16),
        coarse_shifted=pltpu.VMEM((pixels // 4, 3 * channels), BF16),
        widen=pltpu.VMEM((width, channels), F32),
        fold=pltpu.VMEM((width, channels), F32),
        sums=pltpu.VMEM((8, channels), F32),
        rows=pltpu.VMEM((row_count, channels), F32),
        row_sums=pltpu.VMEM((bits + 1, row_count, channels), F32),
        row_gather=pltpu.VMEM((bits, row_count, channels), F32),
        row_send=dma_sems(bits),
        row_recv=dma_sems(bits),
        count=pltpu.VMEM(line, F32),
        stat=pltpu.VMEM(line, F32),
        back=pltpu.VMEM(line, F32),
        slide_count=pltpu.VMEM(line, F32),
        count_gather=pltpu.VMEM((tiles,) + line, F32),
        stat_gather=pltpu.VMEM((tiles,) + line, F32),
        back_gather=pltpu.VMEM((tiles,) + line, F32),
        total_gather=pltpu.VMEM((slides,) + line, F32),
        edge_send=dma_sems(2, 2),
        edge_recv=dma_sems(2, 2),
        tile_send=dma_sems(3),
        tile_recv=dma_sems(3),
        slide_send=dma_sems(2),
        slide_recv=dma_sems(2),
        piece_send=dma_sems(PIECES, slide_ends),
        piece_recv=dma_sems(PIECES, slide_ends),
        stage_send=dma_sems(PIECES, bits),
        stage_recv=dma_sems(PIECES, bits),
    )
    parts = {}
    span = 3 * channels
    for piece in range(PIECES):
        parts[GRAD, piece, 0] = pltpu.VMEM((2,) * bits + (chunk, span), F32)
        plan = stage_plan(bits, order_of(bits, piece % 2))
        for stage, (_, _, left) in enumerate(plan):
            below = (2,) * left + (chunk, span)
            parts[RECV, piece, stage] = pltpu.VMEM(below, BF16 if stage else F32)
            if stage:
                parts[SEND, piece, stage] = pltpu.VMEM(below, BF16)
                parts[KEPT, piece, stage] = pltpu.VMEM(below, F32)
    names = ["far_" + name for name in inputs] + list(outputs) + list(scratch)
    results = call(
        functools.partial(step_kernel, tiles, slides, bits, numbers, names, list(parts)),
        tuple(outputs.values()),
        list(scratch.values()) + list(parts.values()),
        tuple(inputs.values()),
    )
    loss, head, grads = store(*results, classes)
    return (loss[0, 0], head, grads.reshape(chunk, 9, 2, channels).transpose(0, 2, 1, 3))


def solution(mesh):
    return jax.shard_map(
        per_device,
        mesh=mesh,
        in_specs=(
            P("slide", "tile", None, None),
            P("slide", "tile", None, None),
            P(),
            P(),
            P(),
            P(),
            P(),
            P(),
            P(),
            P(),
            P("slide", "tile", None),
        ),
        out_specs=(P(), P(), P("tile", None, None, None)),
        check_vma=False,
    )
```

```python
import functools
import types

import jax
import jax.numpy as jnp
from jax import lax
from jax.experimental import pallas as pl
from jax.experimental.pallas import tpu as pltpu
from jax.sharding import PartitionSpec as P

GROUPS = 32
EPSILON = 1e-05
F32 = jnp.float32
BF16 = jnp.bfloat16
MESH = pl.DeviceIdType.MESH
VMEM = pl.BlockSpec(memory_space=pltpu.VMEM)
ANY = pl.BlockSpec(memory_space=pl.ANY)
LIMIT = 60 * 1024 * 1024
HIGH = lax.Precision.HIGHEST


def call(body, out_shape, scratch, args):
    return pl.pallas_call(
        body,
        out_shape=out_shape,
        in_specs=[ANY] * len(args),
        out_specs=jax.tree.map(lambda _: VMEM, out_shape),
        scratch_shapes=scratch,
        compiler_params=pltpu.CompilerParams(
            vmem_limit_bytes=LIMIT, collective_id=0, has_side_effects=True
        ),
    )(*args)


def store_kernel(classes, rows, grads, loss_out, head_out, grads_out, loss, sems):
    copies = [
        pltpu.make_async_copy(source, target, sems.at[at])
        for at, (source, target) in enumerate(
            ((grads, grads_out), (rows.at[pl.ds(0, 4 + classes)], head_out), (loss, loss_out))
        )
    ]
    for copy in copies[:2]:
        copy.start()
    loss[...] = rows[4 + classes : 5 + classes, 0:1]
    copies[2].start()
    for copy in copies:
        copy.wait()


def store(rows, grads, classes):
    return pl.pallas_call(
        functools.partial(store_kernel, classes),
        out_shape=(
            shape_of((1, 1)),
            shape_of((4 + classes, rows.shape[1])),
            shape_of(grads.shape),
        ),
        in_specs=[VMEM, VMEM],
        out_specs=(ANY, ANY, ANY),
        scratch_shapes=[pltpu.VMEM((1, 1), F32), dma_sems(3)],
    )(*(pltpu.with_memory_space_constraint(value, pltpu.VMEM) for value in (rows, grads)))


def shape_of(dims, dtype=F32):
    return jax.ShapeDtypeStruct(dims, dtype)


def greet(peers, meanwhile):
    barrier = pltpu.get_barrier_semaphore()
    for peer in peers:
        pl.semaphore_signal(barrier, inc=1, device_id=peer, device_id_type=MESH)
    meanwhile()
    pl.semaphore_wait(barrier, len(peers))


def ring_peers(axis, size):
    me = lax.axis_index(axis)
    return [{axis: lax.rem(me + d, size)} for d in range(1, size)]


class Spread:
    def __init__(self, axis, size, source, gather, send_sem, recv_sem):
        me = lax.axis_index(axis)
        self.copies = [
            pltpu.make_async_remote_copy(
                src_ref=source,
                dst_ref=gather.at[me],
                send_sem=send_sem,
                recv_sem=recv_sem,
                device_id={axis: lax.rem(me + d, size)},
                device_id_type=MESH,
            )
            for d in range(1, size)
        ]
        others = gather.at[pl.ds(0, size - 1)]
        self.ends = [pltpu.make_async_copy(others, others, sem) for sem in (send_sem, recv_sem)]

    def start(self):
        for copy in self.copies:
            copy.start()

    def wait(self):
        if self.copies:
            for end in self.ends:
                end.wait()


def ordered_sum(gather, size):
    total = gather[0]
    for index in range(1, size):
        total = total + gather[index]
    return total


def dma_sems(*dims):
    return pltpu.SemaphoreType.DMA(dims)


def column_of(shape, width):
    return lax.rem(lax.broadcasted_iota(jnp.int32, shape, 0), width)


def from_left(values, width):
    moved = pltpu.roll(values, 1, axis=0)
    return jnp.where(column_of(values.shape, width) == 0, 0.0, moved)


def from_right(values, width):
    moved = pltpu.roll(values, values.shape[0] - 1, axis=0)
    return jnp.where(column_of(values.shape, width) == width - 1, 0.0, moved)


def stage_plan(bits, order):
    left = list(reversed(range(bits)))
    plan = []
    for bit in order:
        place = left.index(bit)
        left = [other for other in left if other != bit]
        plan.append((bit, place, len(left)))
    return plan


def at_bits(places, count):
    index = [slice(None)] * count
    for place, value in places:
        index[place] = value
    return tuple(index)


def order_of(bits, turn):
    order = list(range(bits))
    if turn and bits > 2:
        order[1], order[2] = order[2], order[1]
    return order


def lanes_of(shape, dim=1):
    return lax.broadcasted_iota(jnp.int32, shape, dim)


def packed_groups(rows, channels):
    shape = (channels, channels)
    member = lanes_of(shape, 0) // (channels // GROUPS) == lax.rem(lanes_of(shape), GROUPS)
    sums = jnp.dot(rows, member.astype(F32), preferred_element_type=F32, precision=HIGH)
    own = lanes_of(rows.shape) // GROUPS == lanes_of(rows.shape, 0)
    return jnp.sum(jnp.where(own, sums, 0.0), axis=0, keepdims=True)


def unpacked_groups(row, channels):
    shape = (channels, channels)
    member = lax.rem(lanes_of(shape, 0), GROUPS) == lanes_of(shape) // (channels // GROUPS)
    own = lanes_of((8, channels)) // GROUPS == lanes_of((8, channels), 0)
    rows = jnp.where(own, jnp.broadcast_to(row, (8, channels)), 0.0)
    return jnp.dot(rows, member.astype(F32), preferred_element_type=F32, precision=HIGH)


PACK = 2
PIECES = 6
GRAD, SEND, RECV, KEPT, FORM, COME = range(6)


def shifts_of(values, width):
    return jnp.concatenate(
        [from_right(values, width), values, from_left(values, width)], axis=1
    ).astype(BF16)


def ones_of(rows, channels, width):
    column = column_of((rows, channels), width)
    lane = lanes_of((rows, channels))
    outside = ((lane == 0) & (column == width - 1)) | ((lane == 2) & (column == 0)) | (lane > 2)
    return jnp.where(outside, 0.0, 1.0).astype(BF16)


def conv_rows(firsts, count, padded, taps, out, wide, sums, at):
    width, depth = padded.shape[1], padded.shape[2]
    channels = taps.shape[2]
    span = count * width
    total = None
    for a in range(3):
        block = jnp.concatenate(
            [padded[pl.ds(first + a, count)].reshape(span, depth) for first in firsts], axis=0
        )
        side = jnp.concatenate([taps[3 * a + b] for b in range(3)], axis=1)
        term = jnp.dot(block, side, preferred_element_type=F32)
        total = term if total is None else total + term
    value = (
        from_left(total[:, :channels], width)
        + total[:, channels : 2 * channels]
        + from_right(total[:, 2 * channels :], width)
    )
    for index, first in enumerate(firsts):
        here = first * width if isinstance(first, int) else pl.multiple_of(first * width, width)
        part = value[index * span : (index + 1) * span]
        out[pl.ds(here, span), :] = part
        wide[pl.ds(here, span), : 3 * channels] = shifts_of(part, width)
    sums[at : at + 1] += jnp.sum(value, axis=0, keepdims=True)
    sums[at + 1 : at + 2] += jnp.sum(value * value, axis=0, keepdims=True)


def step_kernel(tiles, slides, bits, numbers, names, keys, *refs):
    ref = types.SimpleNamespace(**dict(zip(names, refs)))
    ref.parts = dict(zip(keys, refs[len(names) :]))
    fine, coarse, labels = ref.far_fine, ref.far_coarse, ref.labels
    fine_pad, coarse_pad = ref.fine_pad, ref.coarse_pad
    fine_conv, coarse_conv = ref.fine_conv, ref.coarse_conv
    sums, rows, class_kernel = ref.sums, ref.rows, ref.class_kernel
    me, slide = lax.axis_index("tile"), lax.axis_index("slide")
    height, width, _ = fine.shape
    channels = fine_conv.shape[1]
    classes = class_kernel.shape[0]
    targets = dict(fine=fine_pad.at[pl.ds(1, height)], coarse=coarse_pad.at[pl.ds(1, height // 2)])
    loads = {}
    for at, name in enumerate(names):
        if name.startswith("far_"):
            name = name[4:]
            loads[name] = pltpu.make_async_copy(
                refs[at], targets.get(name, getattr(ref, name, None)), ref.load_sem.at[at]
            )

    def prepare():
        for copy in loads.values():
            copy.start()
        for name, copy in loads.items():
            if not name.startswith(("fine", "coarse")) or name.endswith(("gain", "offset")):
                copy.wait()
        tissue_here = (labels[...] >= 0).astype(F32)
        ref.count[...] = jnp.broadcast_to(
            jnp.sum(tissue_here, axis=(0, 1), keepdims=True), ref.count.shape
        )
        sums[...] = jnp.zeros_like(sums)

    greet(ring_peers("tile", tiles) + ring_peers("slide", slides), prepare)

    def edge_copies(peer, down):
        return [
            pltpu.make_async_remote_copy(
                src_ref=source.at[source.shape[0] - 1 if down else 0],
                dst_ref=target.at[0 if down else target.shape[0] - 1],
                send_sem=ref.edge_send.at[int(down), at],
                recv_sem=ref.edge_recv.at[int(down), at],
                device_id={"tile": peer},
                device_id_type=MESH,
            )
            for at, (source, target) in enumerate(((fine, fine_pad), (coarse, coarse_pad)))
        ]

    fine_gain, fine_offset = ref.fine_gain[...], ref.fine_offset[...]
    coarse_gain, coarse_offset = ref.coarse_gain[...], ref.coarse_offset[...]
    down = edge_copies(lax.rem(me + 1, tiles), True)
    up = edge_copies(lax.rem(me + tiles - 1, tiles), False)

    @pl.when(me < tiles - 1)
    def _():
        for copy in down:
            copy.start()

    @pl.when(me > 0)
    def _():
        for copy in up:
            copy.start()

    def tile_copies(at, source, gather):
        return Spread(
            "tile", tiles, source, gather, ref.tile_send.at[at], ref.tile_recv.at[at]
        )

    def slide_copies(at, source, gather):
        return Spread(
            "slide", slides, source, gather, ref.slide_send.at[at], ref.slide_recv.at[at]
        )

    counts = tile_copies(0, ref.count, ref.count_gather)
    counts.start()
    ref.count_gather[me] = ref.count[...]

    @pl.when(me == 0)
    def _():
        for padded in (fine_pad, coarse_pad):
            padded[0] = jnp.zeros(padded.shape[1:], BF16)

    @pl.when(me == tiles - 1)
    def _():
        for padded in (fine_pad, coarse_pad):
            padded[padded.shape[0] - 1] = jnp.zeros(padded.shape[1:], BF16)

    size, half = 2 * width, width // 2
    levels = (
        (fine_pad, ref.fine_taps, fine_conv, ref.fine_wide, ref.fine_turned, height),
        (coarse_pad, ref.coarse_taps, coarse_conv, ref.coarse_wide, ref.coarse_turned, height // 2),
    )

    def turn(padded, turned, row):
        span = padded.shape[1]
        turned[:, row * span : (row + 1) * span] = padded[row].T

    with jax.named_scope("inner_conv"):
        for at, (padded, taps, out, wide, _, high) in enumerate(levels):
            for name in (("fine", "fine_taps"), ("coarse", "coarse_taps"))[at]:
                loads[name].wait()

            @pl.loop(0, (high - 2) // PACK)
            def _(step):
                conv_rows([1 + PACK * step], PACK, padded, taps, out, wide, sums, 2 * at)

    with jax.named_scope("inner_turn"):
        for padded, _, _, wide, turned, high in levels:
            for row in range(1, high + 1):
                turn(padded, turned, row)
            span = padded.shape[1]

            @pl.loop(0, high)
            def _(row):
                here = pl.ds(pl.multiple_of(row * span, span), span)
                wide[here, 3 * channels :] = ones_of(span, channels, span)

    scope = jax.named_scope("edge_wait")
    scope.__enter__()

    @pl.when(me < tiles - 1)
    def _():
        for copy in down:
            copy.wait_send()
        for copy in up:
            copy.wait_recv()

    @pl.when(me > 0)
    def _():
        for copy in up:
            copy.wait_send()
        for copy in down:
            copy.wait_recv()

    scope.__exit__(None, None, None)
    with jax.named_scope("edge_conv"):
        for at, (padded, taps, out, wide, _, high) in enumerate(levels):
            conv_rows([0, high - 1], 1, padded, taps, out, wide, sums, 2 * at)

    ref.stat[...] = packed_groups(sums[...], channels)
    stat_copies = tile_copies(1, ref.stat, ref.stat_gather)
    stat_copies.start()
    counts.wait()
    ref.slide_count[...] = ordered_sum(ref.count_gather, tiles)
    total_copies = slide_copies(0, ref.slide_count, ref.total_gather)
    total_copies.start()
    ref.stat_gather[me] = ref.stat[...]
    ref.total_gather[slide] = ref.slide_count[...]

    for padded, _, _, _, turned, high in levels:
        turn(padded, turned, 0)
        turn(padded, turned, high + 1)

    mine = [lax.rem(me // (2**bit), 2) for bit in range(bits)]
    partners = [{"tile": me + (1 - 2 * mine[bit]) * (2**bit)} for bit in range(bits)]
    plans = [stage_plan(bits, order_of(bits, piece % 2)) for piece in range(PIECES)]
    final = ref.final
    across = 3 * channels
    spans = [((piece + 3) % PIECES * across, across) for piece in range(PIECES)]

    def buffer(piece, stage, kind):
        return ref.parts[kind, piece, stage]

    def stage_copy(piece, stage):
        bit, place, left = plans[piece][stage]
        return pltpu.make_async_remote_copy(
            src_ref=buffer(piece, stage, SEND),
            dst_ref=buffer(piece, stage, RECV),
            send_sem=ref.stage_send.at[piece, stage],
            recv_sem=ref.stage_recv.at[piece, stage],
            device_id=partners[bit],
            device_id_type=MESH,
        )

    def piece_copies(piece):
        lanes = pl.ds(*spans[piece])
        return [
            pltpu.make_async_remote_copy(
                src_ref=final.at[slide, :, lanes],
                dst_ref=final.at[slide, :, lanes],
                send_sem=ref.piece_send.at[piece, d - 1],
                recv_sem=ref.piece_recv.at[piece, d - 1],
                device_id={"slide": lax.rem(slide + d, slides)},
                device_id_type=MESH,
            )
            for d in range(1, slides)
        ]

    def first_copy(piece, kind, target):
        bit, place, left = plans[piece][0]
        return pltpu.make_async_remote_copy(
            src_ref=buffer(piece, 0, kind).at[at_bits([(place, 1 - mine[bit])], left + 1)],
            dst_ref=buffer(piece, 0, target),
            send_sem=ref.first_send.at[int(kind == FORM), piece],
            recv_sem=ref.first_recv.at[int(kind == FORM), piece],
            device_id=partners[bit],
            device_id_type=MESH,
        )

    def pass_on(piece, stage, part):
        bit, spot, left = plans[piece][stage]
        buffer(piece, stage, SEND)[...] = part(at_bits([(spot, 1 - mine[bit])], left + 1)).astype(BF16)
        stage_copy(piece, stage).start()
        buffer(piece, stage, KEPT)[...] = part(at_bits([(spot, mine[bit])], left + 1))

    def combine(piece, factors):
        bit, place, left = plans[piece][0]
        first_copy(piece, GRAD, RECV).wait()
        first_copy(piece, FORM, COME).wait()
        at = at_bits([(place, mine[bit])], left + 1)
        own, form = buffer(piece, 0, GRAD).at[at], buffer(piece, 0, FORM).at[at]
        came, form_came = buffer(piece, 0, RECV), buffer(piece, 0, COME)

        def part(chosen):
            grad = own[chosen] + came[chosen]
            forms = form[chosen] + form_came[chosen]
            terms = []
            for b in range(3):
                here = slice(b * channels, (b + 1) * channels)
                terms.append(
                    factors[0] * grad[..., here]
                    + factors[1] * forms[..., here]
                    + factors[2] * forms[..., across + b : across + b + 1]
                )
            return jnp.concatenate(terms, axis=-1)

        pass_on(piece, 1, part)

    def advance(piece, stage):
        stage_copy(piece, stage).wait()
        kept, came = buffer(piece, stage, KEPT), buffer(piece, stage, RECV)

        def part(chosen):
            return kept[chosen] + came[chosen].astype(F32)

        if stage == bits - 1:
            final[slide, :, pl.ds(*spans[piece])] = part(...)
            for copy in piece_copies(piece):
                copy.start()
        else:
            pass_on(piece, stage + 1, part)

    def product(piece, kind, turned, values, a, span):
        out = buffer(piece, 0, kind)
        pixels = values.shape[0]
        out[...] = jnp.dot(
            turned[:, a * span : a * span + pixels], values[...], preferred_element_type=F32
        ).reshape(out.shape)
        first_copy(piece, kind, RECV if kind == GRAD else COME).start()

    def row_copy(stage):
        return pltpu.make_async_remote_copy(
            src_ref=ref.row_sums.at[stage],
            dst_ref=ref.row_gather.at[stage],
            send_sem=ref.row_send.at[stage],
            recv_sem=ref.row_recv.at[stage],
            device_id=partners[stage],
            device_id_type=MESH,
        )

    head_copies = slide_copies(1, ref.row_sums.at[bits], ref.head_gather)

    def advance_rows(stage):
        row_copy(stage).wait()
        ref.row_sums[stage + 1] = ref.row_sums[stage] + ref.row_gather[stage]
        if stage + 1 < bits:
            row_copy(stage + 1).start()
        else:
            head_copies.start()
            ref.head_gather[slide] = ref.row_sums[bits]

    with jax.named_scope("form_products"):
        for a in range(3):
            product(a, FORM, ref.coarse_turned, ref.coarse_wide, a, half)
        for a in range(3):
            product(3 + a, FORM, ref.fine_turned, ref.fine_wide, a, width)

    scope = jax.named_scope("stat_wait")
    scope.__enter__()
    stat_copies.wait()
    total_copies.wait()
    total = ordered_sum(ref.total_gather, slides)
    count = total[0:1, 0:1]
    scope.__exit__(None, None, None)
    group_sums = unpacked_groups(ordered_sum(ref.stat_gather, tiles), channels)

    def terms_of(at, number):
        mean = group_sums[at : at + 1] / number
        variance = group_sums[at + 1 : at + 2] / number - mean * mean
        return mean, lax.rsqrt(variance + EPSILON)

    fine_mean, fine_scale = terms_of(0, numbers[0])
    coarse_mean, coarse_scale = terms_of(2, numbers[1])

    square = (classes, classes)
    offset = jnp.sum(
        jnp.where(
            lanes_of(square) == lanes_of(square, 0),
            jnp.broadcast_to(ref.class_offset[...], square),
            0.0,
        ),
        axis=1,
        keepdims=True,
    )
    rows[...] = jnp.zeros_like(rows)
    widen, fold = ref.widen, ref.fold

    scope = jax.named_scope("head")
    scope.__enter__()

    @pl.loop(0, height // 2)
    def _(step):
        fine_at = pl.ds(pl.multiple_of(step * size, size), size)
        coarse_at = pl.ds(pl.multiple_of(step * half, half), half)
        fine_normed = (fine_conv[fine_at, :] - fine_mean) * fine_scale
        fine_pre = fine_normed * fine_gain + fine_offset
        coarse_normed = (coarse_conv[coarse_at, :] - coarse_mean) * coarse_scale
        coarse_pre = coarse_normed * coarse_gain + coarse_offset
        coarse_act = jnp.maximum(coarse_pre, 0.0)
        widen[pl.ds(0, half, stride=2), :] = coarse_act
        widen[pl.ds(1, half, stride=2), :] = coarse_act
        upsampled = widen[...]
        merged = (
            jnp.maximum(fine_pre, 0.0) + jnp.concatenate([upsampled, upsampled], axis=0)
        ).astype(BF16)
        logits = (
            lax.dot_general(
                class_kernel[...], merged, (((1,), (1,)), ((), ())), preferred_element_type=F32
            )
            + offset
        )
        label = jnp.concatenate(
            [labels[pl.ds(2 * step, 1), :], labels[pl.ds(2 * step + 1, 1), :]], axis=1
        )
        onehot = (lanes_of((classes, size), 0) == label).astype(F32)
        tissue = (label >= 0).astype(F32)
        top = jnp.max(logits, axis=0, keepdims=True)
        lse = top + jnp.log(jnp.sum(jnp.exp(logits - top), axis=0, keepdims=True))
        picked = jnp.sum(onehot * logits, axis=0, keepdims=True)
        loss = jnp.sum((lse - picked) * tissue, axis=1, keepdims=True)
        dlogits = ((jnp.exp(logits - lse) - onehot) * tissue / count).astype(BF16)
        dmerged = lax.dot_general(
            dlogits, class_kernel[...], (((0,), (0,)), ((), ())), preferred_element_type=F32
        )
        fine_d = jnp.where(fine_pre > 0, dmerged, 0.0)
        ref.fine_shifted[fine_at, :] = shifts_of(fine_d, width)
        fold[...] = dmerged[:width] + dmerged[width:]
        blocks = fold[pl.ds(0, half, stride=2), :] + fold[pl.ds(1, half, stride=2), :]
        coarse_d = jnp.where(coarse_pre > 0, blocks, 0.0)
        ref.coarse_shifted[coarse_at, :] = shifts_of(coarse_d, half)
        rows[0:1] += jnp.sum(fine_d * fine_normed, axis=0, keepdims=True)
        rows[1:2] += jnp.sum(fine_d, axis=0, keepdims=True)
        rows[2:3] += jnp.sum(coarse_d * coarse_normed, axis=0, keepdims=True)
        rows[3:4] += jnp.sum(coarse_d, axis=0, keepdims=True)
        rows[4 : 4 + classes] += jnp.dot(dlogits, merged, preferred_element_type=F32)
        rows[4 + classes : 5 + classes] += jnp.broadcast_to(loss, (1, channels))

    scope.__exit__(None, None, None)
    gains = jnp.concatenate([fine_gain, fine_gain, coarse_gain, coarse_gain] * 2, axis=0)
    ref.back[...] = packed_groups(rows[0:8] * gains, channels)
    back_copies = tile_copies(2, ref.back, ref.back_gather)
    back_copies.start()
    ref.back_gather[me] = ref.back[...]
    ref.row_sums[0] = rows[...]
    row_copy(0).start()
    with jax.named_scope("grad_products"):
        for a in range(3):
            product(a, GRAD, ref.coarse_turned, ref.coarse_shifted, a, half)
        for a in range(3):
            product(3 + a, GRAD, ref.fine_turned, ref.fine_shifted, a, width)
    with jax.named_scope("back_wait"):
        back_copies.wait()
    back = unpacked_groups(ordered_sum(ref.back_gather, tiles), channels)

    def factors_of(mean, scale, gain, at, number):
        first = back[at + 1 : at + 2] / number
        second = back[at : at + 1] / number * scale * scale
        return scale * gain, -second, second * mean - first * scale

    fine_factors = factors_of(fine_mean, fine_scale, fine_gain, 0, numbers[0])
    coarse_factors = factors_of(coarse_mean, coarse_scale, coarse_gain, 2, numbers[1])
    with jax.named_scope("combine"):
        for piece in range(PIECES):
            combine(piece, coarse_factors if piece < 3 else fine_factors)
    scope = jax.named_scope("exchange")
    scope.__enter__()
    advance_rows(0)
    for stage in range(1, bits):
        for piece in range(PIECES):
            advance(piece, stage)
        advance_rows(stage)
    head_copies.wait()
    row_total = ordered_sum(ref.head_gather, slides)
    ref.heads[...] = row_total
    ref.heads[4 + classes : 5 + classes] = row_total[4 + classes : 5 + classes] / count
    for piece in range(PIECES):
        for copy in piece_copies(piece):
            copy.wait()
        level, a = spans[piece][0] // across // 3, spans[piece][0] // across % 3
        whole = ordered_sum(final.at[:, :, pl.ds(*spans[piece])], slides)
        for b in range(3):
            ref.grads[pl.ds(6 * a + 2 * b + level, whole.shape[0], stride=18), :] = whole[
                :, b * channels : (b + 1) * channels
            ]
    scope.__exit__(None, None, None)


def per_device(
    fine_level,
    coarse_level,
    fine_kernel,
    coarse_kernel,
    fine_gain,
    fine_offset,
    coarse_gain,
    coarse_offset,
    class_kernel,
    class_offset,
    tissue_labels,
):
    tiles, slides = lax.axis_size("tile"), lax.axis_size("slide")
    bits = tiles.bit_length() - 1
    in_channels, _, channels = fine_kernel.shape
    classes = class_kernel.shape[0]
    fine, coarse, labels = fine_level[0], coarse_level[0], tissue_labels[0]
    height, width = fine.shape[0], fine.shape[1]
    fine_number = height * tiles * width * (channels // GROUPS)
    numbers = (float(fine_number), float(fine_number // 4))
    pixels, half = height * width, width // 2
    slide_ends = max(slides - 1, 1)
    chunk = in_channels // tiles
    row_count = -(-(5 + classes) // 8) * 8

    inputs = dict(
        fine=fine,
        fine_taps=fine_kernel.transpose(1, 0, 2),
        labels=labels,
        coarse=coarse,
        coarse_taps=coarse_kernel.transpose(1, 0, 2),
        fine_gain=fine_gain[None, :],
        fine_offset=fine_offset[None, :],
        coarse_gain=coarse_gain[None, :],
        coarse_offset=coarse_offset[None, :],
        class_kernel=class_kernel,
        class_offset=class_offset[None, :],
    )
    outputs = dict(
        heads=pltpu.VMEM((row_count, channels), F32),
        grads=pltpu.VMEM((chunk * 18, channels), F32),
    )
    line = (1, channels)
    scratch = {
        name: pltpu.VMEM(value.shape, value.dtype)
        for name, value in inputs.items()
        if name not in ("fine", "coarse")
    }
    scratch |= dict(
        final=pltpu.VMEM((slides, chunk, 18 * channels), F32),
        head_gather=pltpu.VMEM((slides, row_count, channels), F32),
        load_sem=dma_sems(len(inputs)),
        fine_pad=pltpu.VMEM((height + 2, width, in_channels), BF16),
        coarse_pad=pltpu.VMEM((height // 2 + 2, half, in_channels), BF16),
        fine_conv=pltpu.VMEM((pixels, channels), F32),
        coarse_conv=pltpu.VMEM((pixels // 4, channels), F32),
        fine_wide=pltpu.VMEM((pixels, 4 * channels), BF16),
        coarse_wide=pltpu.VMEM((pixels // 4, 4 * channels), BF16),
        fine_turned=pltpu.VMEM((in_channels, (height + 2) * width), BF16),
        coarse_turned=pltpu.VMEM((in_channels, (height // 2 + 2) * half), BF16),
        fine_shifted=pltpu.VMEM((pixels, 3 * channels), BF16),
        coarse_shifted=pltpu.VMEM((pixels // 4, 3 * channels), BF16),
        widen=pltpu.VMEM((width, channels), F32),
        fold=pltpu.VMEM((width, channels), F32),
        sums=pltpu.VMEM((8, channels), F32),
        rows=pltpu.VMEM((row_count, channels), F32),
        row_sums=pltpu.VMEM((bits + 1, row_count, channels), F32),
        row_gather=pltpu.VMEM((bits, row_count, channels), F32),
        row_send=dma_sems(bits),
        row_recv=dma_sems(bits),
        count=pltpu.VMEM(line, F32),
        stat=pltpu.VMEM(line, F32),
        back=pltpu.VMEM(line, F32),
        slide_count=pltpu.VMEM(line, F32),
        count_gather=pltpu.VMEM((tiles,) + line, F32),
        stat_gather=pltpu.VMEM((tiles,) + line, F32),
        back_gather=pltpu.VMEM((tiles,) + line, F32),
        total_gather=pltpu.VMEM((slides,) + line, F32),
        edge_send=dma_sems(2, 2),
        edge_recv=dma_sems(2, 2),
        tile_send=dma_sems(3),
        tile_recv=dma_sems(3),
        slide_send=dma_sems(2),
        slide_recv=dma_sems(2),
        piece_send=dma_sems(PIECES, slide_ends),
        piece_recv=dma_sems(PIECES, slide_ends),
        first_send=dma_sems(2, PIECES),
        first_recv=dma_sems(2, PIECES),
        stage_send=dma_sems(PIECES, bits),
        stage_recv=dma_sems(PIECES, bits),
    )
    parts = {}
    span = 3 * channels
    for piece in range(PIECES):
        parts[GRAD, piece, 0] = pltpu.VMEM((2,) * bits + (chunk, span), F32)
        plan = stage_plan(bits, order_of(bits, piece % 2))
        forms = (chunk, 4 * channels)
        parts[FORM, piece, 0] = pltpu.VMEM((2,) * bits + forms, F32)
        parts[COME, piece, 0] = pltpu.VMEM((2,) * (bits - 1) + forms, F32)
        for stage, (_, _, left) in enumerate(plan):
            below = (2,) * left + (chunk, span)
            parts[RECV, piece, stage] = pltpu.VMEM(below, BF16 if stage else F32)
            if stage:
                parts[SEND, piece, stage] = pltpu.VMEM(below, BF16)
                parts[KEPT, piece, stage] = pltpu.VMEM(below, F32)
    names = ["far_" + name for name in inputs] + list(outputs) + list(scratch)
    results = call(
        functools.partial(step_kernel, tiles, slides, bits, numbers, names, list(parts)),
        tuple(outputs.values()),
        list(scratch.values()) + list(parts.values()),
        tuple(inputs.values()),
    )
    loss, head, grads = store(*results, classes)
    return (loss[0, 0], head, grads.reshape(chunk, 9, 2, channels).transpose(0, 2, 1, 3))


def solution(mesh):
    return jax.shard_map(
        per_device,
        mesh=mesh,
        in_specs=(
            P("slide", "tile", None, None),
            P("slide", "tile", None, None),
            P(),
            P(),
            P(),
            P(),
            P(),
            P(),
            P(),
            P(),
            P("slide", "tile", None),
        ),
        out_specs=(P(), P(), P("tile", None, None, None)),
        check_vma=False,
    )
```

```python
import functools
import types

import jax
import jax.numpy as jnp
from jax import lax
from jax.experimental import pallas as pl
from jax.experimental.pallas import tpu as pltpu
from jax.sharding import PartitionSpec as P

GROUPS = 32
EPSILON = 1e-05
F32 = jnp.float32
BF16 = jnp.bfloat16
MESH = pl.DeviceIdType.MESH
VMEM = pl.BlockSpec(memory_space=pltpu.VMEM)
ANY = pl.BlockSpec(memory_space=pl.ANY)
LIMIT = 60 * 1024 * 1024
HIGH = lax.Precision.HIGHEST


def call(body, out_shape, scratch, args):
    return pl.pallas_call(
        body,
        out_shape=out_shape,
        in_specs=[ANY] * len(args),
        out_specs=jax.tree.map(lambda _: VMEM, out_shape),
        scratch_shapes=scratch,
        compiler_params=pltpu.CompilerParams(
            vmem_limit_bytes=LIMIT, collective_id=0, has_side_effects=True
        ),
    )(*args)


def store_kernel(classes, rows, grads, loss_out, head_out, grads_out, loss, sems):
    copies = [
        pltpu.make_async_copy(source, target, sems.at[at])
        for at, (source, target) in enumerate(
            ((grads, grads_out), (rows.at[pl.ds(0, 4 + classes)], head_out), (loss, loss_out))
        )
    ]
    for copy in copies[:2]:
        copy.start()
    loss[...] = rows[4 + classes : 5 + classes, 0:1]
    copies[2].start()
    for copy in copies:
        copy.wait()


def store(rows, grads, classes):
    return pl.pallas_call(
        functools.partial(store_kernel, classes),
        out_shape=(
            shape_of((1, 1)),
            shape_of((4 + classes, rows.shape[1])),
            shape_of(grads.shape),
        ),
        in_specs=[VMEM, VMEM],
        out_specs=(ANY, ANY, ANY),
        scratch_shapes=[pltpu.VMEM((1, 1), F32), dma_sems(3)],
    )(*(pltpu.with_memory_space_constraint(value, pltpu.VMEM) for value in (rows, grads)))


def shape_of(dims, dtype=F32):
    return jax.ShapeDtypeStruct(dims, dtype)


def greet(peers, meanwhile):
    barrier = pltpu.get_barrier_semaphore()
    for peer in peers:
        pl.semaphore_signal(barrier, inc=1, device_id=peer, device_id_type=MESH)
    meanwhile()
    pl.semaphore_wait(barrier, len(peers))


def others_of(axis, size):
    me = lax.axis_index(axis)
    return [lax.rem(me + d, size) for d in range(1, size)]


def ring_peers(axis, size):
    return [{axis: peer} for peer in others_of(axis, size)]


class Spread:
    def __init__(self, axis, peers, source, gather, send_sem, recv_sem):
        me = lax.axis_index(axis)
        self.copies = [
            pltpu.make_async_remote_copy(
                src_ref=source,
                dst_ref=gather.at[me],
                send_sem=send_sem,
                recv_sem=recv_sem,
                device_id={axis: peer},
                device_id_type=MESH,
            )
            for peer in peers
        ]
        others = gather.at[pl.ds(0, len(self.copies))]
        self.ends = [pltpu.make_async_copy(others, others, sem) for sem in (send_sem, recv_sem)]

    def start(self):
        for copy in self.copies:
            copy.start()

    def wait(self):
        if self.copies:
            for end in self.ends:
                end.wait()


def ordered_sum(gather, size):
    total = gather[0]
    for index in range(1, size):
        total = total + gather[index]
    return total


def dma_sems(*dims):
    return pltpu.SemaphoreType.DMA(dims)


def column_of(shape, width):
    return lax.rem(lax.broadcasted_iota(jnp.int32, shape, 0), width)


def from_left(values, width):
    moved = pltpu.roll(values, 1, axis=0)
    return jnp.where(column_of(values.shape, width) == 0, 0.0, moved)


def from_right(values, width):
    moved = pltpu.roll(values, values.shape[0] - 1, axis=0)
    return jnp.where(column_of(values.shape, width) == width - 1, 0.0, moved)


def stage_plan(bits, order):
    left = list(reversed(range(bits)))
    plan = []
    for bit in order:
        place = left.index(bit)
        left = [other for other in left if other != bit]
        plan.append((bit, place, len(left)))
    return plan


def at_bits(places, count):
    index = [slice(None)] * count
    for place, value in places:
        index[place] = value
    return tuple(index)


def order_of(bits, turn):
    order = list(range(bits))
    if turn and bits > 2:
        order[1], order[2] = order[2], order[1]
    return order


def lanes_of(shape, dim=1):
    return lax.broadcasted_iota(jnp.int32, shape, dim)


def group_sums_of(rows, channels):
    step = 1
    while step < channels // GROUPS:
        after, before = pltpu.roll(rows, channels - step, axis=1), pltpu.roll(rows, step, axis=1)
        rows = rows + jnp.where(lanes_of(rows.shape) // step % 2 == 0, after, before)
        step *= 2
    return rows


PACK = 2
PIECES = 6
GRAD, SEND, RECV, KEPT, FORM, COME, WINDOW, FSEND, FRECV, FKEPT, OTHER = range(11)


def shifts_of(values, width):
    return jnp.concatenate(
        [from_right(values, width), values, from_left(values, width)], axis=1
    ).astype(BF16)


def ones_of(rows, channels, width):
    column = column_of((rows, channels), width)
    lane = lanes_of((rows, channels))
    side = lax.rem(lane, 3)
    outside = ((side == 0) & (column == width - 1)) | ((side == 2) & (column == 0)) | (lane > 5)
    return jnp.where(outside, 0.0, 1.0).astype(BF16)


def split_sums(values):
    high = values.astype(BF16).astype(F32)
    return jnp.where(lanes_of(values.shape, values.ndim - 1) < 3, high, values - high)


def spread_sums(values, channels):
    shape = values.shape[:-1] + (channels,)
    return jnp.concatenate(
        [jnp.broadcast_to(values[..., b : b + 1], shape) for b in range(3)], axis=-1
    )


def three(row):
    return jnp.concatenate([row] * 3, axis=1)


def conv_terms(firsts, count, padded, taps, terms):
    width, depth = padded.shape[1], padded.shape[2]
    total = None
    for a in terms:
        block = jnp.concatenate(
            [padded[pl.ds(first + a, count)].reshape(count * width, depth) for first in firsts],
            axis=0,
        )
        side = jnp.concatenate([taps[3 * a + b] for b in range(3)], axis=1)
        term = jnp.dot(block, side, preferred_element_type=F32)
        total = term if total is None else total + term
    return total


def conv_finish(total, firsts, width, out, wide, sums, at):
    channels = out.shape[1]
    span = total.shape[0] // len(firsts)
    value = (
        from_left(total[:, :channels], width)
        + total[:, channels : 2 * channels]
        + from_right(total[:, 2 * channels :], width)
    )
    for index, first in enumerate(firsts):
        part = value[index * span : (index + 1) * span]
        out[pl.ds(first * width, span), :] = part
        wide[pl.ds(first * width, span), : 3 * channels] = shifts_of(part, width)
    sums[at : at + 1] += jnp.sum(value, axis=0, keepdims=True)
    sums[at + 1 : at + 2] += jnp.sum(value * value, axis=0, keepdims=True)


def step_kernel(tiles, slides, bits, numbers, names, keys, *refs):
    ref = types.SimpleNamespace(**dict(zip(names, refs)))
    ref.parts = dict(zip(keys, refs[len(names) :]))
    ref.begun = (ref.fine_begun, ref.coarse_begun)
    fine, coarse, labels = ref.far_fine, ref.far_coarse, ref.labels
    fine_pad, coarse_pad = ref.fine_pad, ref.coarse_pad
    fine_conv, coarse_conv = ref.fine_conv, ref.coarse_conv
    sums, rows, class_kernel = ref.sums, ref.rows, ref.class_kernel
    me, slide = lax.axis_index("tile"), lax.axis_index("slide")
    height, width, _ = fine.shape
    channels = fine_conv.shape[1]
    classes = class_kernel.shape[0]
    targets = dict(fine=fine_pad.at[pl.ds(1, height)], coarse=coarse_pad.at[pl.ds(1, height // 2)])
    loads = {}
    for at, name in enumerate(names):
        if name.startswith("far_"):
            name = name[4:]
            loads[name] = pltpu.make_async_copy(
                refs[at], targets.get(name, getattr(ref, name, None)), ref.load_sem.at[at]
            )

    def start_loads():
        for copy in loads.values():
            copy.start()

    def prepare():
        for name, copy in loads.items():
            if not name.startswith(("fine", "coarse")) or name.endswith(("gain", "offset")):
                copy.wait()
        tissue_here = (labels[...] >= 0).astype(F32)
        ref.count[...] = jnp.broadcast_to(
            jnp.sum(tissue_here, axis=(0, 1), keepdims=True), ref.count.shape
        )
        sums[...] = jnp.zeros_like(sums)

    with jax.named_scope("greet"):
        greet(ring_peers("tile", tiles) + ring_peers("slide", slides), start_loads)

    def edge_copies(peer, down):
        return [
            pltpu.make_async_remote_copy(
                src_ref=source.at[source.shape[0] - 1 if down else 0],
                dst_ref=target.at[0 if down else target.shape[0] - 1],
                send_sem=ref.edge_send.at[int(down), at],
                recv_sem=ref.edge_recv.at[int(down), at],
                device_id={"tile": peer},
                device_id_type=MESH,
            )
            for at, (source, target) in enumerate(((fine, fine_pad), (coarse, coarse_pad)))
        ]

    down = edge_copies(lax.rem(me + 1, tiles), True)
    up = edge_copies(lax.rem(me + tiles - 1, tiles), False)

    @pl.when(me < tiles - 1)
    def _():
        for copy in down:
            copy.start()

    @pl.when(me > 0)
    def _():
        for copy in up:
            copy.start()

    with jax.named_scope("prepare"):
        prepare()
    fine_gain, fine_offset = ref.fine_gain[...], ref.fine_offset[...]
    coarse_gain, coarse_offset = ref.coarse_gain[...], ref.coarse_offset[...]

    def tile_copies(at, source, gather):
        return Spread(
            "tile", others_of("tile", tiles), source, gather, ref.tile_send.at[at], ref.tile_recv.at[at]
        )

    def near_first(at, source, gather):
        beside = me + 1 - 2 * lax.rem(me, 2)
        near_copy = pltpu.make_async_remote_copy(
            src_ref=source,
            dst_ref=gather.at[me],
            send_sem=ref.near_send.at[at - 1],
            recv_sem=ref.near_recv.at[at - 1],
            device_id={"tile": beside},
            device_id_type=MESH,
        )
        base = me - lax.rem(me, 2)
        others = [
            lax.rem(base + d, tiles) for d in range(2, tiles)
        ]
        return near_copy, Spread(
            "tile", others, source, gather, ref.tile_send.at[at], ref.tile_recv.at[at]
        )

    def slide_copies(at, source, gather):
        return Spread(
            "slide", others_of("slide", slides), source, gather, ref.slide_send.at[at], ref.slide_recv.at[at]
        )

    counts = tile_copies(0, ref.count, ref.count_gather)
    counts.start()
    ref.count_gather[me] = ref.count[...]

    @pl.when(me == 0)
    def _():
        for padded in (fine_pad, coarse_pad):
            padded[0] = jnp.zeros(padded.shape[1:], BF16)

    @pl.when(me == tiles - 1)
    def _():
        for padded in (fine_pad, coarse_pad):
            padded[padded.shape[0] - 1] = jnp.zeros(padded.shape[1:], BF16)

    size, half = 2 * width, width // 2
    levels = (
        (fine_pad, ref.fine_taps, fine_conv, ref.fine_wide, ref.fine_turned, height),
        (coarse_pad, ref.coarse_taps, coarse_conv, ref.coarse_wide, ref.coarse_turned, height // 2),
    )

    def turn(padded, turned, row):
        span = padded.shape[1]
        turned[:, row * span : (row + 1) * span] = padded[row].T

    with jax.named_scope("inner_conv"):
        for at, (padded, taps, out, wide, _, high) in enumerate(levels):
            with jax.named_scope("load_wait"):
                for name in (("fine", "fine_taps"), ("coarse", "coarse_taps"))[at]:
                    loads[name].wait()

            for step in range((high - 2) // PACK):
                total = conv_terms([1 + PACK * step], PACK, padded, taps, range(3))
                conv_finish(total, [1 + PACK * step], padded.shape[1], out, wide, sums, 2 * at)
            span = padded.shape[1]
            ref.begun[at][:span] = conv_terms([0], 1, padded, taps, (1, 2))
            ref.begun[at][span:] = conv_terms([high - 1], 1, padded, taps, (0, 1))

    with jax.named_scope("inner_turn"):
        for padded, _, _, wide, turned, high in levels:
            for row in range(1, high + 1):
                turn(padded, turned, row)
            span = padded.shape[1]

            @pl.loop(0, high)
            def _(row):
                here = pl.ds(pl.multiple_of(row * span, span), span)
                wide[here, 3 * channels :] = ones_of(span, channels, span)

    mine = [lax.rem(me // (2**bit), 2) for bit in range(bits)]
    partners = [{"tile": me + (1 - 2 * mine[bit]) * (2**bit)} for bit in range(bits)]
    plans = [stage_plan(bits, order_of(bits, piece % 2)) for piece in range(PIECES)]
    final = ref.final
    across = 3 * channels
    spans = [((piece + 3) % PIECES * across, across) for piece in range(PIECES)]

    def buffer(piece, stage, kind):
        return ref.parts[kind, piece, stage]

    def stage_copy(piece, stage):
        bit, place, left = plans[piece][stage]
        return pltpu.make_async_remote_copy(
            src_ref=buffer(piece, stage, SEND),
            dst_ref=buffer(piece, stage, RECV),
            send_sem=ref.stage_send.at[piece, stage],
            recv_sem=ref.stage_recv.at[piece, stage],
            device_id=partners[bit],
            device_id_type=MESH,
        )

    def piece_copies(piece):
        lanes = pl.ds(*spans[piece])
        return [
            pltpu.make_async_remote_copy(
                src_ref=final.at[slide, :, lanes],
                dst_ref=final.at[slide, :, lanes],
                send_sem=ref.piece_send.at[piece, d - 1],
                recv_sem=ref.piece_recv.at[piece, d - 1],
                device_id={"slide": lax.rem(slide + d, slides)},
                device_id_type=MESH,
            )
            for d in range(1, slides)
        ]

    def first_copy(piece, kind, target):
        bit, place, left = plans[piece][0]
        return pltpu.make_async_remote_copy(
            src_ref=buffer(piece, 0, kind).at[at_bits([(place, 1 - mine[bit])], left + 1)],
            dst_ref=buffer(piece, 0, target),
            send_sem=ref.first_send.at[int(kind == FORM), piece],
            recv_sem=ref.first_recv.at[int(kind == FORM), piece],
            device_id=partners[bit],
            device_id_type=MESH,
        )

    def pass_on(piece, stage, part):
        bit, spot, left = plans[piece][stage]
        buffer(piece, stage, SEND)[...] = part(at_bits([(spot, 1 - mine[bit])], left + 1)).astype(BF16)
        stage_copy(piece, stage).start()
        buffer(piece, stage, KEPT)[...] = part(at_bits([(spot, mine[bit])], left + 1))

    def own_of(piece, kind):
        bit, place, left = plans[piece][0]
        return buffer(piece, 0, kind).at[at_bits([(place, mine[bit])], left + 1)]

    def add_forms(piece):
        first_copy(piece, FORM, COME).wait()
        forms = own_of(piece, FORM)[...] + buffer(piece, 0, COME)[...]
        buffer(piece, 0, COME)[...] = forms
        buffer(piece, 0, WINDOW)[...] = spread_sums(forms[..., across:], channels)

    def halves(piece, stage):
        bit, spot, left = plans[piece][stage]
        return [at_bits([(spot, value)], left + 1) for value in (1 - mine[bit], mine[bit])]

    def form_copy(piece):
        return pltpu.make_async_remote_copy(
            src_ref=buffer(piece, 1, FSEND),
            dst_ref=buffer(piece, 1, FRECV),
            send_sem=ref.form_send.at[piece],
            recv_sem=ref.form_recv.at[piece],
            device_id=partners[plans[piece][1][0]],
            device_id_type=MESH,
        )

    def send_forms(piece, mean):
        away, here = halves(piece, 1)
        forms, windows = buffer(piece, 0, COME), buffer(piece, 0, WINDOW)

        def centred(at):
            return forms[at][..., :across] - three(mean) * windows[at]

        send = buffer(piece, 1, FSEND)
        send[..., :across] = centred(away).astype(BF16)
        send[..., across:] = split_sums(forms[away][..., across:]).astype(BF16)
        form_copy(piece).start()
        buffer(piece, 1, FKEPT)[...] = centred(here)

    def close_forms(piece):
        form_copy(piece).wait()
        kept, came = buffer(piece, 1, FKEPT), buffer(piece, 1, FRECV)
        kept[...] = kept[...] + came[..., :across].astype(F32)
        sums_came = came[..., across:].astype(F32)
        ends = sums_came[..., :3] + sums_came[..., 3:6]
        buffer(piece, 1, OTHER)[...] = spread_sums(ends, channels)

    def centre_grads(piece, gain, near):
        first_copy(piece, GRAD, RECV).wait()
        own, came = own_of(piece, GRAD), buffer(piece, 0, RECV)
        windows = buffer(piece, 0, WINDOW)
        wide_gain, wide_near = three(gain), three(near)

        def part(at):
            return wide_gain * (own[at] + came[at]) - wide_near * windows[at]

        pass_on(piece, 1, part)

    def join(piece, factors):
        stage_copy(piece, 1).wait()
        kept, came = buffer(piece, 1, KEPT), buffer(piece, 1, RECV)
        forms, other = buffer(piece, 1, FKEPT), buffer(piece, 1, OTHER)
        windows = buffer(piece, 0, WINDOW).at[halves(piece, 1)[1]]
        wide = [three(factor) for factor in factors]

        def part(at):
            return (
                wide[0] * (kept[at] + came[at].astype(F32))
                + wide[1] * forms[at]
                + wide[2] * windows[at]
                + wide[3] * other[at]
            )

        pass_on(piece, 2, part)

    def advance(piece, stage):
        stage_copy(piece, stage).wait()
        kept, came = buffer(piece, stage, KEPT), buffer(piece, stage, RECV)

        def part(chosen):
            return kept[chosen] + came[chosen].astype(F32)

        if stage == bits - 1:
            final[slide, :, pl.ds(*spans[piece])] = part(...)
            for copy in piece_copies(piece):
                copy.start()
        else:
            pass_on(piece, stage + 1, part)

    def product(piece, kind, level, a, ranges, more=False):
        padded, _, _, wide, turned, _ = levels[level]
        values = (ref.coarse_shifted if level else ref.fine_shifted) if kind == GRAD else wide
        span = padded.shape[1]
        out = buffer(piece, 0, kind)
        left = [turned[:, (a + first) * span : (a + last) * span] for first, last in ranges]
        right = [values[first * span : last * span, :] for first, last in ranges]
        term = jnp.dot(
            jnp.concatenate(left, axis=1),
            jnp.concatenate(right, axis=0),
            preferred_element_type=F32,
        ).reshape(out.shape)
        out[...] = out[...] + term if more else term

    def send_first(piece, kind):
        first_copy(piece, kind, RECV if kind == GRAD else COME).start()

    def row_copy(stage):
        return pltpu.make_async_remote_copy(
            src_ref=ref.row_sums.at[stage],
            dst_ref=ref.row_gather.at[stage],
            send_sem=ref.row_send.at[stage],
            recv_sem=ref.row_recv.at[stage],
            device_id=partners[stage],
            device_id_type=MESH,
        )

    head_copies = slide_copies(1, ref.row_sums.at[bits], ref.head_gather)

    def advance_rows(stage):
        row_copy(stage).wait()
        ref.row_sums[stage + 1] = ref.row_sums[stage] + ref.row_gather[stage]
        if stage + 1 < bits:
            row_copy(stage + 1).start()
        else:
            head_copies.start()
            ref.head_gather[slide] = ref.row_sums[bits]

    with jax.named_scope("inner_forms"):
        for a in range(3):
            product(3 + a, FORM, 0, a, [(1, height - 1)])

    for at, (padded, taps, out, wide, _, high) in enumerate(levels):
        with jax.named_scope("edge_wait"):

            @pl.when(me < tiles - 1)
            def _():
                down[at].wait_send()
                up[at].wait_recv()

            @pl.when(me > 0)
            def _():
                up[at].wait_send()
                down[at].wait_recv()

        with jax.named_scope("edge_conv"):
            span = padded.shape[1]
            for first, a in ((0, 0), (high - 1, 2)):
                here = slice(span) if first == 0 else slice(span, 2 * span)
                total = ref.begun[at][here] + conv_terms([first], 1, padded, taps, (a,))
                conv_finish(total, [first], span, out, wide, sums, 2 * at)

    ref.stat[...] = sums[0:4]
    near_stat, stat_copies = near_first(1, ref.stat, ref.stat_gather)
    near_stat.start()
    ref.stat_gather[me] = ref.stat[...]
    stat_copies.start()
    counts.wait()
    ref.slide_count[...] = ordered_sum(ref.count_gather, tiles)
    total_copies = slide_copies(0, ref.slide_count, ref.total_gather)
    total_copies.start()
    ref.total_gather[slide] = ref.slide_count[...]

    for padded, _, _, _, turned, high in levels:
        turn(padded, turned, 0)
        turn(padded, turned, high + 1)

    def pair_of(gather, tile):
        return gather[tile] + gather[tile + 1 - 2 * lax.rem(tile, 2)]

    def near_centres(tile):
        pair = pair_of(ref.stat_gather, tile)
        return [
            pair[2 * at : 2 * at + 1] / (numbers[at] * 2 / tiles / (channels // GROUPS))
            for at in range(2)
        ]

    with jax.named_scope("form_products"):
        for a in range(3):
            product(a, FORM, 1, a, [(0, height // 2)])
            send_first(a, FORM)
        near_stat.wait()
        centres = near_centres(me)
        for a in range(3):
            product(3 + a, FORM, 0, a, [(0, 1), (height - 1, height)], more=True)
            send_first(3 + a, FORM)
            if a == 1:
                for piece in range(3):
                    add_forms(piece)
                    send_forms(piece, centres[1])
    with jax.named_scope("add_forms"):
        for piece in range(3, PIECES):
            add_forms(piece)
            send_forms(piece, centres[0])

    scope = jax.named_scope("stat_wait")
    scope.__enter__()
    stat_copies.wait()
    total_copies.wait()
    total = ordered_sum(ref.total_gather, slides)
    count = total[0:1, 0:1]
    scope.__exit__(None, None, None)
    group_sums = group_sums_of(ordered_sum(ref.stat_gather, tiles), channels)

    def terms_of(at, number):
        mean = group_sums[at : at + 1] / number
        variance = group_sums[at + 1 : at + 2] / number - mean * mean
        return mean, lax.rsqrt(variance + EPSILON)

    fine_mean, fine_scale = terms_of(0, numbers[0])
    coarse_mean, coarse_scale = terms_of(2, numbers[1])

    square = (classes, classes)
    offset = jnp.sum(
        jnp.where(
            lanes_of(square) == lanes_of(square, 0),
            jnp.broadcast_to(ref.class_offset[...], square),
            0.0,
        ),
        axis=1,
        keepdims=True,
    )
    rows[...] = jnp.zeros_like(rows)

    scope = jax.named_scope("head")
    scope.__enter__()

    for step in range(height // 2):
        widen, fold = ref.widen.at[step], ref.fold.at[step]
        fine_at = pl.ds(step * size, size)
        coarse_at = pl.ds(step * half, half)
        fine_normed = (fine_conv[fine_at, :] - fine_mean) * fine_scale
        fine_pre = fine_normed * fine_gain + fine_offset
        coarse_normed = (coarse_conv[coarse_at, :] - coarse_mean) * coarse_scale
        coarse_pre = coarse_normed * coarse_gain + coarse_offset
        coarse_act = jnp.maximum(coarse_pre, 0.0)
        widen[pl.ds(0, half, stride=2), :] = coarse_act
        widen[pl.ds(1, half, stride=2), :] = coarse_act
        upsampled = widen[...]
        merged = (
            jnp.maximum(fine_pre, 0.0) + jnp.concatenate([upsampled, upsampled], axis=0)
        ).astype(BF16)
        logits = (
            lax.dot_general(
                class_kernel[...], merged, (((1,), (1,)), ((), ())), preferred_element_type=F32
            )
            + offset
        )
        label = jnp.concatenate(
            [labels[pl.ds(2 * step, 1), :], labels[pl.ds(2 * step + 1, 1), :]], axis=1
        )
        onehot = (lanes_of((classes, size), 0) == label).astype(F32)
        tissue = (label >= 0).astype(F32)
        top = jnp.max(logits, axis=0, keepdims=True)
        lse = top + jnp.log(jnp.sum(jnp.exp(logits - top), axis=0, keepdims=True))
        picked = jnp.sum(onehot * logits, axis=0, keepdims=True)
        loss = jnp.sum((lse - picked) * tissue, axis=1, keepdims=True)
        dlogits = ((jnp.exp(logits - lse) - onehot) * tissue / count).astype(BF16)
        dmerged = lax.dot_general(
            dlogits, class_kernel[...], (((0,), (0,)), ((), ())), preferred_element_type=F32
        )
        fine_d = jnp.where(fine_pre > 0, dmerged, 0.0)
        ref.fine_shifted[fine_at, :] = shifts_of(fine_d, width)
        fold[...] = dmerged[:width] + dmerged[width:]
        blocks = fold[pl.ds(0, half, stride=2), :] + fold[pl.ds(1, half, stride=2), :]
        coarse_d = jnp.where(coarse_pre > 0, blocks, 0.0)
        ref.coarse_shifted[coarse_at, :] = shifts_of(coarse_d, half)
        rows[0:1] += jnp.sum(fine_d * fine_normed, axis=0, keepdims=True)
        rows[1:2] += jnp.sum(fine_d, axis=0, keepdims=True)
        rows[2:3] += jnp.sum(coarse_d * coarse_normed, axis=0, keepdims=True)
        rows[3:4] += jnp.sum(coarse_d, axis=0, keepdims=True)
        rows[4 : 4 + classes] += jnp.dot(dlogits, merged, preferred_element_type=F32)
        rows[4 + classes : 5 + classes] += jnp.broadcast_to(loss, (1, channels))

    scope.__exit__(None, None, None)
    gains = jnp.concatenate([fine_gain, fine_gain, coarse_gain, coarse_gain], axis=0)
    ref.back[...] = rows[0:4] * gains
    near_copy, back_copies = near_first(2, ref.back, ref.back_gather)
    near_copy.start()
    back_copies.start()
    ref.back_gather[me] = ref.back[...]
    ref.row_sums[0] = rows[...]
    row_copy(0).start()
    stats = ((fine_mean, fine_scale), (coarse_mean, coarse_scale))

    def near_means(tile):
        pair = pair_of(ref.back_gather, tile)
        sums_here = group_sums_of(pair, channels)
        return [
            sums_here[2 * at + 1 : 2 * at + 2] / (numbers[at] * 2 / tiles) for at in range(2)
        ]

    def grad_product(piece):
        level = 1 - piece // 3
        product(piece, GRAD, level, piece % 3, [(0, (height, height // 2)[level])])
        send_first(piece, GRAD)

    scope = jax.named_scope("grad_products")
    scope.__enter__()
    for piece in range(4):
        grad_product(piece)
    near_copy.wait()
    near = near_means(me)
    for piece in range(3):
        centre_grads(piece, coarse_gain, near[1])
    grad_product(4)
    centre_grads(3, fine_gain, near[0])
    grad_product(5)
    centre_grads(4, fine_gain, near[0])
    scope.__exit__(None, None, None)
    with jax.named_scope("close_forms"):
        for piece in range(3):
            close_forms(piece)
    with jax.named_scope("centre_grads"):
        centre_grads(5, fine_gain, near[0])
    advance_rows(0)
    with jax.named_scope("close_forms"):
        for piece in range(3, PIECES):
            close_forms(piece)
    with jax.named_scope("back_wait"):
        back_copies.wait()
    back = group_sums_of(ordered_sum(ref.back_gather, tiles), channels)
    peers = {
        bit: (near_means(partners[bit]["tile"]), near_centres(partners[bit]["tile"]))
        for bit in {plan[1][0] for plan in plans}
    }

    def factors_of(piece):
        at = 1 - piece // 3
        mean, scale = stats[at]
        first = back[2 * at + 1 : 2 * at + 2] / numbers[at]
        second = back[2 * at : 2 * at + 1] / numbers[at] * scale * scale
        peer_near, peer_centres = peers[plans[piece][1][0]]
        return (
            scale,
            -second,
            scale * (near[at] - first) - second * (centres[at] - mean),
            scale * (peer_near[at] - first) - second * (peer_centres[at] - mean),
        )

    with jax.named_scope("join"):
        for piece in range(3):
            join(piece, factors_of(piece))
    advance_rows(1)
    with jax.named_scope("join_fine"):
        for piece in range(3, PIECES):
            join(piece, factors_of(piece))
    for stage in range(2, bits):
        with jax.named_scope("stage%d" % stage):
            for piece in range(PIECES):
                advance(piece, stage)
        advance_rows(stage)
    scope = jax.named_scope("finish")
    scope.__enter__()
    head_copies.wait()
    row_total = ordered_sum(ref.head_gather, slides)
    ref.heads[...] = row_total
    ref.heads[4 + classes : 5 + classes] = row_total[4 + classes : 5 + classes] / count
    for piece in range(PIECES):
        for copy in piece_copies(piece):
            copy.wait()
        level, a = spans[piece][0] // across // 3, spans[piece][0] // across % 3
        whole = ordered_sum(final.at[:, :, pl.ds(*spans[piece])], slides)
        for b in range(3):
            ref.grads[pl.ds(6 * a + 2 * b + level, whole.shape[0], stride=18), :] = whole[
                :, b * channels : (b + 1) * channels
            ]
    scope.__exit__(None, None, None)


def per_device(
    fine_level,
    coarse_level,
    fine_kernel,
    coarse_kernel,
    fine_gain,
    fine_offset,
    coarse_gain,
    coarse_offset,
    class_kernel,
    class_offset,
    tissue_labels,
):
    tiles, slides = lax.axis_size("tile"), lax.axis_size("slide")
    bits = tiles.bit_length() - 1
    in_channels, _, channels = fine_kernel.shape
    classes = class_kernel.shape[0]
    fine, coarse, labels = fine_level[0], coarse_level[0], tissue_labels[0]
    height, width = fine.shape[0], fine.shape[1]
    fine_number = height * tiles * width * (channels // GROUPS)
    numbers = (float(fine_number), float(fine_number // 4))
    pixels, half = height * width, width // 2
    slide_ends = max(slides - 1, 1)
    chunk = in_channels // tiles
    row_count = -(-(5 + classes) // 8) * 8

    inputs = dict(
        fine=fine,
        fine_taps=fine_kernel.transpose(1, 0, 2),
        labels=labels,
        coarse=coarse,
        coarse_taps=coarse_kernel.transpose(1, 0, 2),
        fine_gain=fine_gain[None, :],
        fine_offset=fine_offset[None, :],
        coarse_gain=coarse_gain[None, :],
        coarse_offset=coarse_offset[None, :],
        class_kernel=class_kernel,
        class_offset=class_offset[None, :],
    )
    outputs = dict(
        heads=pltpu.VMEM((row_count, channels), F32),
        grads=pltpu.VMEM((chunk * 18, channels), F32),
    )
    line, lines = (1, channels), (4, channels)
    scratch = {
        name: pltpu.VMEM(value.shape, value.dtype)
        for name, value in inputs.items()
        if name not in ("fine", "coarse")
    }
    scratch |= dict(
        final=pltpu.VMEM((slides, chunk, 18 * channels), F32),
        head_gather=pltpu.VMEM((slides, row_count, channels), F32),
        load_sem=dma_sems(len(inputs)),
        fine_pad=pltpu.VMEM((height + 2, width, in_channels), BF16),
        coarse_pad=pltpu.VMEM((height // 2 + 2, half, in_channels), BF16),
        fine_conv=pltpu.VMEM((pixels, channels), F32),
        coarse_conv=pltpu.VMEM((pixels // 4, channels), F32),
        fine_begun=pltpu.VMEM((2 * width, 3 * channels), F32),
        coarse_begun=pltpu.VMEM((2 * half, 3 * channels), F32),
        fine_wide=pltpu.VMEM((pixels, 4 * channels), BF16),
        coarse_wide=pltpu.VMEM((pixels // 4, 4 * channels), BF16),
        fine_turned=pltpu.VMEM((in_channels, (height + 2) * width), BF16),
        coarse_turned=pltpu.VMEM((in_channels, (height // 2 + 2) * half), BF16),
        fine_shifted=pltpu.VMEM((pixels, 3 * channels), BF16),
        coarse_shifted=pltpu.VMEM((pixels // 4, 3 * channels), BF16),
        widen=pltpu.VMEM((height // 2, width, channels), F32),
        fold=pltpu.VMEM((height // 2, width, channels), F32),
        sums=pltpu.VMEM((8, channels), F32),
        rows=pltpu.VMEM((row_count, channels), F32),
        row_sums=pltpu.VMEM((bits + 1, row_count, channels), F32),
        row_gather=pltpu.VMEM((bits, row_count, channels), F32),
        row_send=dma_sems(bits),
        row_recv=dma_sems(bits),
        count=pltpu.VMEM(line, F32),
        stat=pltpu.VMEM(lines, F32),
        back=pltpu.VMEM(lines, F32),
        slide_count=pltpu.VMEM(line, F32),
        count_gather=pltpu.VMEM((tiles,) + line, F32),
        stat_gather=pltpu.VMEM((tiles,) + lines, F32),
        back_gather=pltpu.VMEM((tiles,) + lines, F32),
        total_gather=pltpu.VMEM((slides,) + line, F32),
        edge_send=dma_sems(2, 2),
        edge_recv=dma_sems(2, 2),
        near_send=dma_sems(2),
        near_recv=dma_sems(2),
        form_send=dma_sems(PIECES),
        form_recv=dma_sems(PIECES),
        tile_send=dma_sems(3),
        tile_recv=dma_sems(3),
        slide_send=dma_sems(2),
        slide_recv=dma_sems(2),
        piece_send=dma_sems(PIECES, slide_ends),
        piece_recv=dma_sems(PIECES, slide_ends),
        first_send=dma_sems(2, PIECES),
        first_recv=dma_sems(2, PIECES),
        stage_send=dma_sems(PIECES, bits),
        stage_recv=dma_sems(PIECES, bits),
    )
    parts = {}
    span = 3 * channels
    for piece in range(PIECES):
        parts[GRAD, piece, 0] = pltpu.VMEM((2,) * bits + (chunk, span), F32)
        plan = stage_plan(bits, order_of(bits, piece % 2))
        forms = (chunk, 4 * channels)
        parts[FORM, piece, 0] = pltpu.VMEM((2,) * bits + forms, F32)
        parts[WINDOW, piece, 0] = pltpu.VMEM((2,) * (bits - 1) + (chunk, span), F32)
        parts[COME, piece, 0] = pltpu.VMEM((2,) * (bits - 1) + forms, F32)
        for stage, (_, _, left) in enumerate(plan):
            below = (2,) * left + (chunk, span)
            parts[RECV, piece, stage] = pltpu.VMEM(below, BF16 if stage else F32)
            if stage == 1:
                wider = below[:-1] + (4 * channels,)
                parts[FSEND, piece, 1] = pltpu.VMEM(wider, BF16)
                parts[FRECV, piece, 1] = pltpu.VMEM(wider, BF16)
                parts[FKEPT, piece, 1] = pltpu.VMEM(below, F32)
                parts[OTHER, piece, 1] = pltpu.VMEM(below, F32)
            if stage:
                parts[SEND, piece, stage] = pltpu.VMEM(below, BF16)
                parts[KEPT, piece, stage] = pltpu.VMEM(below, F32)
    names = ["far_" + name for name in inputs] + list(outputs) + list(scratch)
    results = call(
        functools.partial(step_kernel, tiles, slides, bits, numbers, names, list(parts)),
        tuple(outputs.values()),
        list(scratch.values()) + list(parts.values()),
        tuple(inputs.values()),
    )
    loss, head, grads = store(*results, classes)
    return (loss[0, 0], head, grads.reshape(chunk, 9, 2, channels).transpose(0, 2, 1, 3))


def solution(mesh):
    return jax.shard_map(
        per_device,
        mesh=mesh,
        in_specs=(
            P("slide", "tile", None, None),
            P("slide", "tile", None, None),
            P(),
            P(),
            P(),
            P(),
            P(),
            P(),
            P(),
            P(),
            P("slide", "tile", None),
        ),
        out_specs=(P(), P(), P("tile", None, None, None)),
        check_vma=False,
    )
```

```python
import functools
import types

import jax
import jax.numpy as jnp
from jax import lax
from jax.experimental import pallas as pl
from jax.experimental.pallas import tpu as pltpu
from jax.sharding import PartitionSpec as P

GROUPS = 32
EPSILON = 1e-05
F32 = jnp.float32
BF16 = jnp.bfloat16
MESH = pl.DeviceIdType.MESH
VMEM = pl.BlockSpec(memory_space=pltpu.VMEM)
ANY = pl.BlockSpec(memory_space=pl.ANY)
LIMIT = 60 * 1024 * 1024
HIGH = lax.Precision.HIGHEST


def call(body, out_shape, scratch, args):
    return pl.pallas_call(
        body,
        out_shape=out_shape,
        in_specs=[ANY] * len(args),
        out_specs=jax.tree.map(lambda _: VMEM, out_shape),
        scratch_shapes=scratch,
        compiler_params=pltpu.CompilerParams(
            vmem_limit_bytes=LIMIT, collective_id=0, has_side_effects=True
        ),
    )(*args)


def store_kernel(classes, rows, grads, loss_out, head_out, grads_out, loss, sems):
    copies = [
        pltpu.make_async_copy(source, target, sems.at[at])
        for at, (source, target) in enumerate(
            ((grads, grads_out), (rows.at[pl.ds(0, 4 + classes)], head_out), (loss, loss_out))
        )
    ]
    for copy in copies[:2]:
        copy.start()
    loss[...] = rows[4 + classes : 5 + classes, 0:1]
    copies[2].start()
    for copy in copies:
        copy.wait()


def store(rows, grads, classes):
    return pl.pallas_call(
        functools.partial(store_kernel, classes),
        out_shape=(
            shape_of((1, 1)),
            shape_of((4 + classes, rows.shape[1])),
            shape_of(grads.shape),
        ),
        in_specs=[VMEM, VMEM],
        out_specs=(ANY, ANY, ANY),
        scratch_shapes=[pltpu.VMEM((1, 1), F32), dma_sems(3)],
    )(*(pltpu.with_memory_space_constraint(value, pltpu.VMEM) for value in (rows, grads)))


def shape_of(dims, dtype=F32):
    return jax.ShapeDtypeStruct(dims, dtype)


def greet(peers, meanwhile):
    barrier = pltpu.get_barrier_semaphore()
    for peer in peers:
        pl.semaphore_signal(barrier, inc=1, device_id=peer, device_id_type=MESH)
    meanwhile()
    pl.semaphore_wait(barrier, len(peers))


def others_of(axis, size):
    me = lax.axis_index(axis)
    return [lax.rem(me + d, size) for d in range(1, size)]


def ring_peers(axis, size):
    return [{axis: peer} for peer in others_of(axis, size)]


class Spread:
    def __init__(self, axis, peers, source, gather, send_sem, recv_sem):
        me = lax.axis_index(axis)
        self.copies = [
            pltpu.make_async_remote_copy(
                src_ref=source,
                dst_ref=gather.at[me],
                send_sem=send_sem,
                recv_sem=recv_sem,
                device_id={axis: peer},
                device_id_type=MESH,
            )
            for peer in peers
        ]
        others = gather.at[pl.ds(0, len(self.copies))]
        self.ends = [pltpu.make_async_copy(others, others, sem) for sem in (send_sem, recv_sem)]

    def start(self):
        for copy in self.copies:
            copy.start()

    def wait(self):
        if self.copies:
            for end in self.ends:
                end.wait()


def ordered_sum(gather, size):
    total = gather[0]
    for index in range(1, size):
        total = total + gather[index]
    return total


def dma_sems(*dims):
    return pltpu.SemaphoreType.DMA(dims)


def column_of(shape, width):
    return lax.rem(lax.broadcasted_iota(jnp.int32, shape, 0), width)


def from_left(values, width):
    moved = pltpu.roll(values, 1, axis=0)
    return jnp.where(column_of(values.shape, width) == 0, 0.0, moved)


def from_right(values, width):
    moved = pltpu.roll(values, values.shape[0] - 1, axis=0)
    return jnp.where(column_of(values.shape, width) == width - 1, 0.0, moved)


def stage_plan(bits, order):
    left = list(reversed(range(bits)))
    plan = []
    for bit in order:
        place = left.index(bit)
        left = [other for other in left if other != bit]
        plan.append((bit, place, len(left)))
    return plan


def at_bits(places, count):
    index = [slice(None)] * count
    for place, value in places:
        index[place] = value
    return tuple(index)


def order_of(bits, turn):
    order = list(range(bits))
    if turn and bits > 2:
        order[1], order[2] = order[2], order[1]
    return order


def lanes_of(shape, dim=1):
    return lax.broadcasted_iota(jnp.int32, shape, dim)


def group_sums_of(rows, channels):
    step = 1
    while step < channels // GROUPS:
        after, before = pltpu.roll(rows, channels - step, axis=1), pltpu.roll(rows, step, axis=1)
        rows = rows + jnp.where(lanes_of(rows.shape) // step % 2 == 0, after, before)
        step *= 2
    return rows


PACK = 2
PIECES = 6
EARLY = 6
GRAD, SEND, RECV, KEPT, FORM, COME, WINDOW, FSEND, FRECV, FKEPT, OTHER = range(11)


def shifts_of(values, width):
    return jnp.concatenate(
        [from_right(values, width), values, from_left(values, width)], axis=1
    ).astype(BF16)


def ones_of(rows, channels, width):
    column = column_of((rows, channels), width)
    lane = lanes_of((rows, channels))
    side = lax.rem(lane, 3)
    outside = ((side == 0) & (column == width - 1)) | ((side == 2) & (column == 0)) | (lane > 5)
    return jnp.where(outside, 0.0, 1.0).astype(BF16)


def split_sums(values):
    high = values.astype(BF16).astype(F32)
    return jnp.where(lanes_of(values.shape, values.ndim - 1) < 3, high, values - high)


def spread_sums(values, channels):
    shape = values.shape[:-1] + (channels,)
    return jnp.concatenate(
        [jnp.broadcast_to(values[..., b : b + 1], shape) for b in range(3)], axis=-1
    )


def three(row):
    return jnp.concatenate([row] * 3, axis=1)


def conv_terms(firsts, count, padded, taps, terms):
    width, depth = padded.shape[1], padded.shape[2]
    total = None
    for a in terms:
        block = jnp.concatenate(
            [padded[pl.ds(first + a, count)].reshape(count * width, depth) for first in firsts],
            axis=0,
        )
        side = jnp.concatenate([taps[3 * a + b] for b in range(3)], axis=1)
        term = jnp.dot(block, side, preferred_element_type=F32)
        total = term if total is None else total + term
    return total


def conv_finish(total, firsts, width, out, wide, sums, at):
    channels = out.shape[1]
    span = total.shape[0] // len(firsts)
    value = (
        from_left(total[:, :channels], width)
        + total[:, channels : 2 * channels]
        + from_right(total[:, 2 * channels :], width)
    )
    for index, first in enumerate(firsts):
        part = value[index * span : (index + 1) * span]
        out[pl.ds(first * width, span), :] = part
        wide[pl.ds(first * width, span), : 3 * channels] = shifts_of(part, width)
    sums[at : at + 1] += jnp.sum(value, axis=0, keepdims=True)
    sums[at + 1 : at + 2] += jnp.sum(value * value, axis=0, keepdims=True)


def step_kernel(tiles, slides, bits, numbers, names, keys, *refs):
    ref = types.SimpleNamespace(**dict(zip(names, refs)))
    ref.parts = dict(zip(keys, refs[len(names) :]))
    ref.begun = (ref.fine_begun, ref.coarse_begun)
    fine, coarse, labels = ref.far_fine, ref.far_coarse, ref.labels
    fine_pad, coarse_pad = ref.fine_pad, ref.coarse_pad
    fine_conv, coarse_conv = ref.fine_conv, ref.coarse_conv
    sums, rows, class_kernel = ref.sums, ref.rows, ref.class_kernel
    me, slide = lax.axis_index("tile"), lax.axis_index("slide")
    height, width, _ = fine.shape
    channels = fine_conv.shape[1]
    classes = class_kernel.shape[0]
    targets = dict(fine=fine_pad.at[pl.ds(1, height)], coarse=coarse_pad.at[pl.ds(1, height // 2)])
    loads = {}
    for at, name in enumerate(names):
        if name.startswith("far_"):
            name = name[4:]
            loads[name] = pltpu.make_async_copy(
                refs[at], targets.get(name, getattr(ref, name, None)), ref.load_sem.at[at]
            )

    def start_loads():
        for copy in loads.values():
            copy.start()

    def prepare():
        for name, copy in loads.items():
            if not name.startswith(("fine", "coarse")) or name.endswith(("gain", "offset")):
                copy.wait()
        tissue_here = (labels[...] >= 0).astype(F32)
        ref.count[...] = jnp.broadcast_to(
            jnp.sum(tissue_here, axis=(0, 1), keepdims=True), ref.count.shape
        )
        sums[...] = jnp.zeros_like(sums)

    with jax.named_scope("greet"):
        greet(ring_peers("tile", tiles) + ring_peers("slide", slides), start_loads)

    def edge_copies(peer, down):
        return [
            pltpu.make_async_remote_copy(
                src_ref=source.at[source.shape[0] - 1 if down else 0],
                dst_ref=target.at[0 if down else target.shape[0] - 1],
                send_sem=ref.edge_send.at[int(down), at],
                recv_sem=ref.edge_recv.at[int(down), at],
                device_id={"tile": peer},
                device_id_type=MESH,
            )
            for at, (source, target) in enumerate(((fine, fine_pad), (coarse, coarse_pad)))
        ]

    down = edge_copies(lax.rem(me + 1, tiles), True)
    up = edge_copies(lax.rem(me + tiles - 1, tiles), False)

    @pl.when(me < tiles - 1)
    def _():
        for copy in down:
            copy.start()

    @pl.when(me > 0)
    def _():
        for copy in up:
            copy.start()

    with jax.named_scope("prepare"):
        prepare()
    fine_gain, fine_offset = ref.fine_gain[...], ref.fine_offset[...]
    coarse_gain, coarse_offset = ref.coarse_gain[...], ref.coarse_offset[...]

    def tile_copies(at, source, gather):
        return Spread(
            "tile", others_of("tile", tiles), source, gather, ref.tile_send.at[at], ref.tile_recv.at[at]
        )

    def near_first(at, source, gather):
        beside = me + 1 - 2 * lax.rem(me, 2)
        near_copy = pltpu.make_async_remote_copy(
            src_ref=source,
            dst_ref=gather.at[me],
            send_sem=ref.near_send.at[at - 1],
            recv_sem=ref.near_recv.at[at - 1],
            device_id={"tile": beside},
            device_id_type=MESH,
        )
        signs = [1 - 2 * lax.rem(me // 2**bit, 2) for bit in range(bits)]
        others = [
            me + sum(signs[bit] * 2**bit for bit in range(bits) if d // 2**bit % 2)
            for d in range(tiles - 1, 1, -1)
        ]
        return near_copy, Spread(
            "tile", others, source, gather, ref.tile_send.at[at], ref.tile_recv.at[at]
        )

    def slide_copies(at, source, gather):
        return Spread(
            "slide", others_of("slide", slides), source, gather, ref.slide_send.at[at], ref.slide_recv.at[at]
        )

    counts = tile_copies(0, ref.count, ref.count_gather)
    counts.start()
    ref.count_gather[me] = ref.count[...]

    @pl.when(me == 0)
    def _():
        for padded in (fine_pad, coarse_pad):
            padded[0] = jnp.zeros(padded.shape[1:], BF16)

    @pl.when(me == tiles - 1)
    def _():
        for padded in (fine_pad, coarse_pad):
            padded[padded.shape[0] - 1] = jnp.zeros(padded.shape[1:], BF16)

    size, half = 2 * width, width // 2
    levels = (
        (fine_pad, ref.fine_taps, fine_conv, ref.fine_wide, ref.fine_turned, height),
        (coarse_pad, ref.coarse_taps, coarse_conv, ref.coarse_wide, ref.coarse_turned, height // 2),
    )

    def turn(padded, turned, row):
        span = padded.shape[1]
        turned[:, row * span : (row + 1) * span] = padded[row].T

    with jax.named_scope("inner_conv"):
        for at, (padded, taps, out, wide, _, high) in enumerate(levels):
            with jax.named_scope("load_wait"):
                for name in (("fine", "fine_taps"), ("coarse", "coarse_taps"))[at]:
                    loads[name].wait()

            for step in range((high - 2) // PACK):
                total = conv_terms([1 + PACK * step], PACK, padded, taps, range(3))
                conv_finish(total, [1 + PACK * step], padded.shape[1], out, wide, sums, 2 * at)
            span = padded.shape[1]
            ref.begun[at][:span] = conv_terms([0], 1, padded, taps, (1, 2))
            ref.begun[at][span:] = conv_terms([high - 1], 1, padded, taps, (0, 1))

    with jax.named_scope("inner_turn"):
        for padded, _, _, wide, turned, high in levels:
            for row in range(1, high + 1):
                turn(padded, turned, row)
            span = padded.shape[1]

            @pl.loop(0, high)
            def _(row):
                here = pl.ds(pl.multiple_of(row * span, span), span)
                wide[here, 3 * channels :] = ones_of(span, channels, span)

    mine = [lax.rem(me // (2**bit), 2) for bit in range(bits)]
    partners = [{"tile": me + (1 - 2 * mine[bit]) * (2**bit)} for bit in range(bits)]
    plans = [stage_plan(bits, order_of(bits, piece % 2)) for piece in range(PIECES)]
    final = ref.final
    across = 3 * channels
    spans = [((piece + 3) % PIECES * across, across) for piece in range(PIECES)]

    def buffer(piece, stage, kind):
        if kind in (SEND, FSEND):
            return ref.parts[kind, 0, stage].at[piece]
        return ref.parts[kind, piece, stage]

    def stage_copy(piece, stage):
        bit, place, left = plans[piece][stage]
        return pltpu.make_async_remote_copy(
            src_ref=buffer(piece, stage, SEND),
            dst_ref=buffer(piece, stage, RECV),
            send_sem=ref.stage_send.at[stage - 1],
            recv_sem=ref.stage_recv.at[piece, stage - 1],
            device_id=partners[bit],
            device_id_type=MESH,
        )

    def piece_copies(piece):
        lanes = pl.ds(*spans[piece])
        return [
            pltpu.make_async_remote_copy(
                src_ref=final.at[slide, :, lanes],
                dst_ref=final.at[slide, :, lanes],
                send_sem=ref.piece_send.at[0],
                recv_sem=ref.piece_recv.at[piece, d - 1],
                device_id={"slide": lax.rem(slide + d, slides)},
                device_id_type=MESH,
            )
            for d in range(1, slides)
        ]

    def first_copy(piece, kind, target):
        bit, place, left = plans[piece][0]
        return pltpu.make_async_remote_copy(
            src_ref=buffer(piece, 0, kind).at[at_bits([(place, 1 - mine[bit])], left + 1)],
            dst_ref=buffer(piece, 0, target),
            send_sem=ref.first_send.at[int(kind == FORM), piece],
            recv_sem=ref.first_recv.at[int(kind == FORM), piece],
            device_id=partners[bit],
            device_id_type=MESH,
        )

    def fill(piece, stage, part):
        bit, spot, left = plans[piece][stage]
        buffer(piece, stage, SEND)[...] = part(at_bits([(spot, 1 - mine[bit])], left + 1)).astype(BF16)
        buffer(piece, stage, KEPT)[...] = part(at_bits([(spot, mine[bit])], left + 1))

    def pass_on(piece, stage, part):
        fill(piece, stage, part)
        stage_copy(piece, stage).start()

    def own_of(piece, kind):
        bit, place, left = plans[piece][0]
        return buffer(piece, 0, kind).at[at_bits([(place, mine[bit])], left + 1)]

    def add_forms(piece):
        forms = own_of(piece, FORM)[...] + buffer(piece, 0, COME)[...]
        buffer(piece, 0, COME)[...] = forms
        buffer(piece, 0, WINDOW)[...] = spread_sums(forms[..., across:], channels)

    def halves(piece, stage):
        bit, spot, left = plans[piece][stage]
        return [at_bits([(spot, value)], left + 1) for value in (1 - mine[bit], mine[bit])]

    def form_copy(piece):
        return pltpu.make_async_remote_copy(
            src_ref=buffer(piece, 1, FSEND),
            dst_ref=buffer(piece, 1, FRECV),
            send_sem=ref.form_send.at[0],
            recv_sem=ref.form_recv.at[piece],
            device_id=partners[plans[piece][1][0]],
            device_id_type=MESH,
        )

    def centre_forms(piece, mean):
        away, here = halves(piece, 1)
        forms, windows = buffer(piece, 0, COME), buffer(piece, 0, WINDOW)

        def centred(at):
            return forms[at][..., :across] - three(mean) * windows[at]

        send = buffer(piece, 1, FSEND)
        send[..., :across] = centred(away).astype(BF16)
        send[..., across:] = split_sums(forms[away][..., across:]).astype(BF16)
        buffer(piece, 1, FKEPT)[...] = centred(here)

    def close_forms(piece):
        form_copy(piece).wait_recv()
        kept, came = buffer(piece, 1, FKEPT), buffer(piece, 1, FRECV)
        kept[...] = kept[...] + came[..., :across].astype(F32)
        sums_came = came[..., across:].astype(F32)
        ends = sums_came[..., :3] + sums_came[..., 3:6]
        buffer(piece, 1, OTHER)[...] = spread_sums(ends, channels)

    def centre_grads(piece, gain, near):
        own, came = own_of(piece, GRAD), buffer(piece, 0, RECV)
        windows = buffer(piece, 0, WINDOW)
        wide_gain, wide_near = three(gain), three(near)

        def part(at):
            return wide_gain * (own[at] + came[at]) - wide_near * windows[at]

        fill(piece, 1, part)

    def join(piece, factors):
        stage_copy(piece, 1).wait_recv()
        kept, came = buffer(piece, 1, KEPT), buffer(piece, 1, RECV)
        forms, other = buffer(piece, 1, FKEPT), buffer(piece, 1, OTHER)
        windows = buffer(piece, 0, WINDOW).at[halves(piece, 1)[1]]
        wide = [three(factor) for factor in factors]

        def part(at):
            return (
                wide[0] * (kept[at] + came[at].astype(F32))
                + wide[1] * forms[at]
                + wide[2] * windows[at]
                + wide[3] * other[at]
            )

        pass_on(piece, 2, part)

    def advance(piece, stage):
        stage_copy(piece, stage).wait_recv()
        kept, came = buffer(piece, stage, KEPT), buffer(piece, stage, RECV)

        def part(chosen):
            return kept[chosen] + came[chosen].astype(F32)

        if stage == bits - 1:
            final[slide, :, pl.ds(*spans[piece])] = part(...)
            for copy in piece_copies(piece):
                copy.start()
        else:
            pass_on(piece, stage + 1, part)

    def product(piece, kind, level, a, ranges, more=False):
        padded, _, _, wide, turned, _ = levels[level]
        values = (ref.coarse_shifted if level else ref.fine_shifted) if kind == GRAD else wide
        span = padded.shape[1]
        out = buffer(piece, 0, kind)
        left = [turned[:, (a + first) * span : (a + last) * span] for first, last in ranges]
        right = [values[first * span : last * span, :] for first, last in ranges]
        term = jnp.dot(
            jnp.concatenate(left, axis=1),
            jnp.concatenate(right, axis=0),
            preferred_element_type=F32,
        ).reshape(out.shape)
        out[...] = out[...] + term if more else term

    def send_first(piece, kind):
        first_copy(piece, kind, RECV if kind == GRAD else COME).start()

    def row_copy(stage):
        return pltpu.make_async_remote_copy(
            src_ref=ref.row_sums.at[stage],
            dst_ref=ref.row_gather.at[stage],
            send_sem=ref.row_send.at[stage],
            recv_sem=ref.row_recv.at[stage],
            device_id=partners[stage],
            device_id_type=MESH,
        )

    head_copies = slide_copies(1, ref.row_sums.at[bits], ref.head_gather)

    def advance_rows(stage):
        row_copy(stage).wait()
        ref.row_sums[stage + 1] = ref.row_sums[stage] + ref.row_gather[stage]
        if stage + 1 < bits:
            row_copy(stage + 1).start()
        else:
            head_copies.start()
            ref.head_gather[slide] = ref.row_sums[bits]

    with jax.named_scope("inner_forms"):
        for a in range(3):
            product(3 + a, FORM, 0, a, [(1, height - 1)])

    for at, (padded, taps, out, wide, _, high) in enumerate(levels):
        with jax.named_scope("edge_wait"):

            @pl.when(me < tiles - 1)
            def _():
                down[at].wait_send()
                up[at].wait_recv()

            @pl.when(me > 0)
            def _():
                up[at].wait_send()
                down[at].wait_recv()

        with jax.named_scope("edge_conv"):
            span = padded.shape[1]
            for first, a in ((0, 0), (high - 1, 2)):
                here = slice(span) if first == 0 else slice(span, 2 * span)
                total = ref.begun[at][here] + conv_terms([first], 1, padded, taps, (a,))
                conv_finish(total, [first], span, out, wide, sums, 2 * at)

    ref.stat[...] = sums[0:4]
    near_stat, stat_copies = near_first(1, ref.stat, ref.stat_gather)
    near_stat.start()
    ref.stat_gather[me] = ref.stat[...]
    stat_copies.start()
    counts.wait()
    ref.slide_count[...] = ordered_sum(ref.count_gather, tiles)
    total_copies = slide_copies(0, ref.slide_count, ref.total_gather)
    total_copies.start()
    ref.total_gather[slide] = ref.slide_count[...]

    for padded, _, _, _, turned, high in levels:
        turn(padded, turned, 0)
        turn(padded, turned, high + 1)

    def pair_of(gather, tile):
        return gather[tile] + gather[tile + 1 - 2 * lax.rem(tile, 2)]

    def near_centres(tile):
        pair = pair_of(ref.stat_gather, tile)
        return [
            pair[2 * at : 2 * at + 1] / (numbers[at] * 2 / tiles / (channels // GROUPS))
            for at in range(2)
        ]

    def forms_came(pieces):
        for piece in pieces:
            first_copy(piece, FORM, COME).wait()

    def send_forms(pieces):
        for piece in pieces:
            form_copy(piece).start()

    def form_product(piece):
        if piece < 3:
            product(piece, FORM, 1, piece, [(0, height // 2)])
        else:
            product(piece, FORM, 0, piece - 3, [(0, 1), (height - 1, height)], more=True)

    with jax.named_scope("form_products"):
        for pair in ((0, 1), (2, 3)):
            for piece in pair:
                form_product(piece)
            for piece in pair:
                send_first(piece, FORM)
        near_stat.wait()
        centres = near_centres(me)
        form_product(4)
        send_first(4, FORM)
        forms_came(range(2))
        form_product(5)
        for piece in range(2):
            add_forms(piece)
            centre_forms(piece, centres[1])
        send_first(5, FORM)
        send_forms(range(2))
        for piece in range(2, EARLY):
            forms_came([piece])
            add_forms(piece)
            centre_forms(piece, centres[1 - piece // 3])
            send_forms([piece])

    scope = jax.named_scope("stat_wait")
    scope.__enter__()
    stat_copies.wait()
    total_copies.wait()
    total = ordered_sum(ref.total_gather, slides)
    count = total[0:1, 0:1]
    scope.__exit__(None, None, None)
    group_sums = group_sums_of(ordered_sum(ref.stat_gather, tiles), channels)

    def terms_of(at, number):
        mean = group_sums[at : at + 1] / number
        variance = group_sums[at + 1 : at + 2] / number - mean * mean
        return mean, lax.rsqrt(variance + EPSILON)

    fine_mean, fine_scale = terms_of(0, numbers[0])
    coarse_mean, coarse_scale = terms_of(2, numbers[1])

    square = (classes, classes)
    offset = jnp.sum(
        jnp.where(
            lanes_of(square) == lanes_of(square, 0),
            jnp.broadcast_to(ref.class_offset[...], square),
            0.0,
        ),
        axis=1,
        keepdims=True,
    )
    rows[...] = jnp.zeros_like(rows)

    forms_came(range(EARLY, PIECES))
    scope = jax.named_scope("head")
    scope.__enter__()
    for piece in range(EARLY, PIECES):
        add_forms(piece)
        centre_forms(piece, centres[0])

    for step in range(height // 2):
        widen, fold = ref.widen.at[step], ref.fold.at[step]
        fine_at = pl.ds(step * size, size)
        coarse_at = pl.ds(step * half, half)
        fine_normed = (fine_conv[fine_at, :] - fine_mean) * fine_scale
        fine_pre = fine_normed * fine_gain + fine_offset
        coarse_normed = (coarse_conv[coarse_at, :] - coarse_mean) * coarse_scale
        coarse_pre = coarse_normed * coarse_gain + coarse_offset
        coarse_act = jnp.maximum(coarse_pre, 0.0)
        widen[pl.ds(0, half, stride=2), :] = coarse_act
        widen[pl.ds(1, half, stride=2), :] = coarse_act
        upsampled = widen[...]
        merged = (
            jnp.maximum(fine_pre, 0.0) + jnp.concatenate([upsampled, upsampled], axis=0)
        ).astype(BF16)
        logits = (
            lax.dot_general(
                class_kernel[...], merged, (((1,), (1,)), ((), ())), preferred_element_type=F32
            )
            + offset
        )
        label = jnp.concatenate(
            [labels[pl.ds(2 * step, 1), :], labels[pl.ds(2 * step + 1, 1), :]], axis=1
        )
        onehot = (lanes_of((classes, size), 0) == label).astype(F32)
        tissue = (label >= 0).astype(F32)
        top = jnp.max(logits, axis=0, keepdims=True)
        lse = top + jnp.log(jnp.sum(jnp.exp(logits - top), axis=0, keepdims=True))
        picked = jnp.sum(onehot * logits, axis=0, keepdims=True)
        loss = jnp.sum((lse - picked) * tissue, axis=1, keepdims=True)
        dlogits = ((jnp.exp(logits - lse) - onehot) * tissue / count).astype(BF16)
        dmerged = lax.dot_general(
            dlogits, class_kernel[...], (((0,), (0,)), ((), ())), preferred_element_type=F32
        )
        fine_d = jnp.where(fine_pre > 0, dmerged, 0.0)
        ref.fine_shifted[fine_at, :] = shifts_of(fine_d, width)
        fold[...] = dmerged[:width] + dmerged[width:]
        blocks = fold[pl.ds(0, half, stride=2), :] + fold[pl.ds(1, half, stride=2), :]
        coarse_d = jnp.where(coarse_pre > 0, blocks, 0.0)
        ref.coarse_shifted[coarse_at, :] = shifts_of(coarse_d, half)
        rows[0:1] += jnp.sum(fine_d * fine_normed, axis=0, keepdims=True)
        rows[1:2] += jnp.sum(fine_d, axis=0, keepdims=True)
        rows[2:3] += jnp.sum(coarse_d * coarse_normed, axis=0, keepdims=True)
        rows[3:4] += jnp.sum(coarse_d, axis=0, keepdims=True)
        rows[4 : 4 + classes] += jnp.dot(dlogits, merged, preferred_element_type=F32)
        rows[4 + classes : 5 + classes] += jnp.broadcast_to(loss, (1, channels))

    scope.__exit__(None, None, None)
    gains = jnp.concatenate([fine_gain, fine_gain, coarse_gain, coarse_gain], axis=0)
    ref.back[...] = rows[0:4] * gains
    near_copy, back_copies = near_first(2, ref.back, ref.back_gather)
    near_copy.start()
    back_copies.start()
    ref.back_gather[me] = ref.back[...]
    ref.row_sums[0] = rows[...]
    send_forms(range(EARLY, PIECES))
    row_copy(0).start()
    stats = ((fine_mean, fine_scale), (coarse_mean, coarse_scale))

    def near_means(tile):
        pair = pair_of(ref.back_gather, tile)
        sums_here = group_sums_of(pair, channels)
        return [
            sums_here[2 * at + 1 : 2 * at + 2] / (numbers[at] * 2 / tiles) for at in range(2)
        ]

    def grad_product(piece):
        level = 1 - piece // 3
        product(piece, GRAD, level, piece % 3, [(0, (height, height // 2)[level])])

    def grads_came(pieces):
        for piece in pieces:
            first_copy(piece, GRAD, RECV).wait()

    def centre(pieces):
        for piece in pieces:
            centre_grads(piece, *((coarse_gain, near[1]) if piece < 3 else (fine_gain, near[0])))

    def send(pieces):
        for piece in pieces:
            stage_copy(piece, 1).start()

    with jax.named_scope("grads_a"):
        for piece in range(4):
            grad_product(piece)
            send_first(piece, GRAD)
    with jax.named_scope("grads_wait"):
        near_copy.wait()
        near = near_means(me)
        grads_came(range(2))
    with jax.named_scope("grads_c"):
        grad_product(4)
        centre(range(2))
        send_first(4, GRAD)
        send(range(2))
        grads_came([2, 3])
    with jax.named_scope("grads_d"):
        grad_product(5)
        centre([2, 3])
        send_first(5, GRAD)
        send([2, 3])
        advance_rows(0)
    with jax.named_scope("close_a"):
        for piece in range(2):
            close_forms(piece)
        grads_came([4])
        centre([4])
        send([4])
        close_forms(2)
        grads_came([5])
        centre([5])
        send([5])
    with jax.named_scope("close_b"):
        for piece in range(3, PIECES):
            close_forms(piece)
    with jax.named_scope("back_wait"):
        back_copies.wait()
    back = group_sums_of(ordered_sum(ref.back_gather, tiles), channels)
    peers = {
        bit: (near_means(partners[bit]["tile"]), near_centres(partners[bit]["tile"]))
        for bit in {plan[1][0] for plan in plans}
    }

    def factors_of(piece):
        at = 1 - piece // 3
        mean, scale = stats[at]
        first = back[2 * at + 1 : 2 * at + 2] / numbers[at]
        second = back[2 * at : 2 * at + 1] / numbers[at] * scale * scale
        peer_near, peer_centres = peers[plans[piece][1][0]]
        return (
            scale,
            -second,
            scale * (near[at] - first) - second * (centres[at] - mean),
            scale * (peer_near[at] - first) - second * (peer_centres[at] - mean),
        )

    with jax.named_scope("join"):
        for piece in range(3):
            join(piece, factors_of(piece))
    with jax.named_scope("join_fine"):
        for piece in range(3, PIECES):
            join(piece, factors_of(piece))
    advance_rows(1)
    for stage in range(2, bits):
        with jax.named_scope("stage%d" % stage):
            for piece in range(PIECES):
                advance(piece, stage)
        advance_rows(stage)
    scope = jax.named_scope("finish")
    scope.__enter__()
    sent = [(ref.parts[SEND, 0, stage], ref.stage_send.at[stage - 1]) for stage in range(1, bits)]
    sent += [(ref.parts[FSEND, 0, 1], ref.form_send.at[0])]
    sent += [(final.at[pl.ds(0, slides - 1)], ref.piece_send.at[0])]
    for buffers, sem in sent:
        pltpu.make_async_copy(buffers, buffers, sem).wait()
    head_copies.wait()
    row_total = ordered_sum(ref.head_gather, slides)
    ref.heads[...] = row_total
    ref.heads[4 + classes : 5 + classes] = row_total[4 + classes : 5 + classes] / count
    for piece in range(PIECES):
        for copy in piece_copies(piece):
            copy.wait_recv()
        level, a = spans[piece][0] // across // 3, spans[piece][0] // across % 3
        whole = ordered_sum(final.at[:, :, pl.ds(*spans[piece])], slides)
        for b in range(3):
            ref.grads[pl.ds(6 * a + 2 * b + level, whole.shape[0], stride=18), :] = whole[
                :, b * channels : (b + 1) * channels
            ]
    scope.__exit__(None, None, None)


def per_device(
    fine_level,
    coarse_level,
    fine_kernel,
    coarse_kernel,
    fine_gain,
    fine_offset,
    coarse_gain,
    coarse_offset,
    class_kernel,
    class_offset,
    tissue_labels,
):
    tiles, slides = lax.axis_size("tile"), lax.axis_size("slide")
    bits = tiles.bit_length() - 1
    in_channels, _, channels = fine_kernel.shape
    classes = class_kernel.shape[0]
    fine, coarse, labels = fine_level[0], coarse_level[0], tissue_labels[0]
    height, width = fine.shape[0], fine.shape[1]
    fine_number = height * tiles * width * (channels // GROUPS)
    numbers = (float(fine_number), float(fine_number // 4))
    pixels, half = height * width, width // 2
    slide_ends = max(slides - 1, 1)
    chunk = in_channels // tiles
    row_count = -(-(5 + classes) // 8) * 8

    inputs = dict(
        fine=fine,
        fine_taps=fine_kernel.transpose(1, 0, 2),
        labels=labels,
        coarse=coarse,
        coarse_taps=coarse_kernel.transpose(1, 0, 2),
        fine_gain=fine_gain[None, :],
        fine_offset=fine_offset[None, :],
        coarse_gain=coarse_gain[None, :],
        coarse_offset=coarse_offset[None, :],
        class_kernel=class_kernel,
        class_offset=class_offset[None, :],
    )
    outputs = dict(
        heads=pltpu.VMEM((row_count, channels), F32),
        grads=pltpu.VMEM((chunk * 18, channels), F32),
    )
    line, lines = (1, channels), (4, channels)
    scratch = {
        name: pltpu.VMEM(value.shape, value.dtype)
        for name, value in inputs.items()
        if name not in ("fine", "coarse")
    }
    scratch |= dict(
        final=pltpu.VMEM((slides, chunk, 18 * channels), F32),
        head_gather=pltpu.VMEM((slides, row_count, channels), F32),
        load_sem=dma_sems(len(inputs)),
        fine_pad=pltpu.VMEM((height + 2, width, in_channels), BF16),
        coarse_pad=pltpu.VMEM((height // 2 + 2, half, in_channels), BF16),
        fine_conv=pltpu.VMEM((pixels, channels), F32),
        coarse_conv=pltpu.VMEM((pixels // 4, channels), F32),
        fine_begun=pltpu.VMEM((2 * width, 3 * channels), F32),
        coarse_begun=pltpu.VMEM((2 * half, 3 * channels), F32),
        fine_wide=pltpu.VMEM((pixels, 4 * channels), BF16),
        coarse_wide=pltpu.VMEM((pixels // 4, 4 * channels), BF16),
        fine_turned=pltpu.VMEM((in_channels, (height + 2) * width), BF16),
        coarse_turned=pltpu.VMEM((in_channels, (height // 2 + 2) * half), BF16),
        fine_shifted=pltpu.VMEM((pixels, 3 * channels), BF16),
        coarse_shifted=pltpu.VMEM((pixels // 4, 3 * channels), BF16),
        widen=pltpu.VMEM((height // 2, width, channels), F32),
        fold=pltpu.VMEM((height // 2, width, channels), F32),
        sums=pltpu.VMEM((8, channels), F32),
        rows=pltpu.VMEM((row_count, channels), F32),
        row_sums=pltpu.VMEM((bits + 1, row_count, channels), F32),
        row_gather=pltpu.VMEM((bits, row_count, channels), F32),
        row_send=dma_sems(bits),
        row_recv=dma_sems(bits),
        count=pltpu.VMEM(line, F32),
        stat=pltpu.VMEM(lines, F32),
        back=pltpu.VMEM(lines, F32),
        slide_count=pltpu.VMEM(line, F32),
        count_gather=pltpu.VMEM((tiles,) + line, F32),
        stat_gather=pltpu.VMEM((tiles,) + lines, F32),
        back_gather=pltpu.VMEM((tiles,) + lines, F32),
        total_gather=pltpu.VMEM((slides,) + line, F32),
        edge_send=dma_sems(2, 2),
        edge_recv=dma_sems(2, 2),
        near_send=dma_sems(2),
        near_recv=dma_sems(2),
        form_send=dma_sems(1),
        form_recv=dma_sems(PIECES),
        tile_send=dma_sems(3),
        tile_recv=dma_sems(3),
        slide_send=dma_sems(2),
        slide_recv=dma_sems(2),
        piece_send=dma_sems(1),
        piece_recv=dma_sems(PIECES, slide_ends),
        first_send=dma_sems(2, PIECES),
        first_recv=dma_sems(2, PIECES),
        stage_send=dma_sems(bits - 1),
        stage_recv=dma_sems(PIECES, bits - 1),
    )
    parts = {}
    span = 3 * channels
    for piece in range(PIECES):
        parts[GRAD, piece, 0] = pltpu.VMEM((2,) * bits + (chunk, span), F32)
        plan = stage_plan(bits, order_of(bits, piece % 2))
        forms = (chunk, 4 * channels)
        parts[FORM, piece, 0] = pltpu.VMEM((2,) * bits + forms, F32)
        parts[WINDOW, piece, 0] = pltpu.VMEM((2,) * (bits - 1) + (chunk, span), F32)
        parts[COME, piece, 0] = pltpu.VMEM((2,) * (bits - 1) + forms, F32)
        for stage, (_, _, left) in enumerate(plan):
            below = (2,) * left + (chunk, span)
            parts[RECV, piece, stage] = pltpu.VMEM(below, BF16 if stage else F32)
            if stage == 1:
                wider = below[:-1] + (4 * channels,)
                parts[FSEND, 0, 1] = pltpu.VMEM((PIECES,) + wider, BF16)
                parts[FRECV, piece, 1] = pltpu.VMEM(wider, BF16)
                parts[FKEPT, piece, 1] = pltpu.VMEM(below, F32)
                parts[OTHER, piece, 1] = pltpu.VMEM(below, F32)
            if stage:
                parts[SEND, 0, stage] = pltpu.VMEM((PIECES,) + below, BF16)
                parts[KEPT, piece, stage] = pltpu.VMEM(below, F32)
    names = ["far_" + name for name in inputs] + list(outputs) + list(scratch)
    results = call(
        functools.partial(step_kernel, tiles, slides, bits, numbers, names, list(parts)),
        tuple(outputs.values()),
        list(scratch.values()) + list(parts.values()),
        tuple(inputs.values()),
    )
    loss, head, grads = store(*results, classes)
    return (loss[0, 0], head, grads.reshape(chunk, 9, 2, channels).transpose(0, 2, 1, 3))


def solution(mesh):
    return jax.shard_map(
        per_device,
        mesh=mesh,
        in_specs=(
            P("slide", "tile", None, None),
            P("slide", "tile", None, None),
            P(),
            P(),
            P(),
            P(),
            P(),
            P(),
            P(),
            P(),
            P("slide", "tile", None),
        ),
        out_specs=(P(), P(), P("tile", None, None, None)),
        check_vma=False,
    )
```

```python
import functools
import types

import jax
import jax.numpy as jnp
from jax import lax
from jax.experimental import pallas as pl
from jax.experimental.pallas import tpu as pltpu
from jax.sharding import PartitionSpec as P

GROUPS = 32
EPSILON = 1e-05
F32 = jnp.float32
BF16 = jnp.bfloat16
MESH = pl.DeviceIdType.MESH
VMEM = pl.BlockSpec(memory_space=pltpu.VMEM)
ANY = pl.BlockSpec(memory_space=pl.ANY)
LIMIT = 60 * 1024 * 1024
HIGH = lax.Precision.HIGHEST


def call(body, out_shape, scratch, args):
    return pl.pallas_call(
        body,
        out_shape=out_shape,
        in_specs=[ANY] * len(args),
        out_specs=jax.tree.map(lambda _: VMEM, out_shape),
        scratch_shapes=scratch,
        compiler_params=pltpu.CompilerParams(
            vmem_limit_bytes=LIMIT, collective_id=0, has_side_effects=True
        ),
    )(*args)


def store_kernel(classes, rows, grads, loss_out, head_out, grads_out, loss, sems):
    copies = [
        pltpu.make_async_copy(source, target, sems.at[at])
        for at, (source, target) in enumerate(
            ((grads, grads_out), (rows.at[pl.ds(0, 4 + classes)], head_out), (loss, loss_out))
        )
    ]
    for copy in copies[:2]:
        copy.start()
    loss[...] = rows[4 + classes : 5 + classes, 0:1]
    copies[2].start()
    for copy in copies:
        copy.wait()


def store(rows, grads, classes):
    return pl.pallas_call(
        functools.partial(store_kernel, classes),
        out_shape=(
            shape_of((1, 1)),
            shape_of((4 + classes, rows.shape[1])),
            shape_of(grads.shape),
        ),
        in_specs=[VMEM, VMEM],
        out_specs=(ANY, ANY, ANY),
        scratch_shapes=[pltpu.VMEM((1, 1), F32), dma_sems(3)],
    )(*(pltpu.with_memory_space_constraint(value, pltpu.VMEM) for value in (rows, grads)))


def shape_of(dims, dtype=F32):
    return jax.ShapeDtypeStruct(dims, dtype)


def greet(peers, meanwhile):
    barrier = pltpu.get_barrier_semaphore()
    for peer in peers:
        pl.semaphore_signal(barrier, inc=1, device_id=peer, device_id_type=MESH)
    meanwhile()
    pl.semaphore_wait(barrier, len(peers))


def others_of(axis, size):
    me = lax.axis_index(axis)
    return [lax.rem(me + d, size) for d in range(1, size)]


def ring_peers(axis, size):
    return [{axis: peer} for peer in others_of(axis, size)]


class Spread:
    def __init__(self, axis, peers, source, gather, send_sem, recv_sem):
        me = lax.axis_index(axis)
        self.copies = [
            pltpu.make_async_remote_copy(
                src_ref=source,
                dst_ref=gather.at[me],
                send_sem=send_sem,
                recv_sem=recv_sem,
                device_id={axis: peer},
                device_id_type=MESH,
            )
            for peer in peers
        ]
        others = gather.at[pl.ds(0, len(self.copies))]
        self.ends = [pltpu.make_async_copy(others, others, sem) for sem in (send_sem, recv_sem)]

    def start(self):
        for copy in self.copies:
            copy.start()

    def wait(self):
        if self.copies:
            for end in self.ends:
                end.wait()


def ordered_sum(gather, size):
    total = gather[0]
    for index in range(1, size):
        total = total + gather[index]
    return total


def dma_sems(*dims):
    return pltpu.SemaphoreType.DMA(dims)


def column_of(shape, width):
    return lax.rem(lax.broadcasted_iota(jnp.int32, shape, 0), width)


def from_left(values, width):
    moved = pltpu.roll(values, 1, axis=0)
    return jnp.where(column_of(values.shape, width) == 0, 0.0, moved)


def from_right(values, width):
    moved = pltpu.roll(values, values.shape[0] - 1, axis=0)
    return jnp.where(column_of(values.shape, width) == width - 1, 0.0, moved)


def stage_plan(bits, order):
    left = list(reversed(range(bits)))
    plan = []
    for bit in order:
        place = left.index(bit)
        left = [other for other in left if other != bit]
        plan.append((bit, place, len(left)))
    return plan


def at_bits(places, count):
    index = [slice(None)] * count
    for place, value in places:
        index[place] = value
    return tuple(index)


def order_of(bits, turn):
    order = list(range(bits))
    if turn and bits > 2:
        order[1], order[2] = order[2], order[1]
    return order


def lanes_of(shape, dim=1):
    return lax.broadcasted_iota(jnp.int32, shape, dim)


def group_sums_of(rows, channels):
    step = 1
    while step < channels // GROUPS:
        after, before = pltpu.roll(rows, channels - step, axis=1), pltpu.roll(rows, step, axis=1)
        rows = rows + jnp.where(lanes_of(rows.shape) // step % 2 == 0, after, before)
        step *= 2
    return rows


PACK = 2
PIECES = 6
EARLY = 6
GRAD, SEND, RECV, KEPT, FORM, COME, WINDOW, FSEND, FRECV, FKEPT, OTHER = range(11)


def shifts_of(values, width):
    return jnp.concatenate(
        [from_right(values, width), values, from_left(values, width)], axis=1
    ).astype(BF16)


def ones_of(rows, channels, width):
    column = column_of((rows, channels), width)
    lane = lanes_of((rows, channels))
    side = lax.rem(lane, 3)
    outside = ((side == 0) & (column == width - 1)) | ((side == 2) & (column == 0)) | (lane > 5)
    return jnp.where(outside, 0.0, 1.0).astype(BF16)


def split_sums(values):
    high = values.astype(BF16).astype(F32)
    return jnp.where(lanes_of(values.shape, values.ndim - 1) < 3, high, values - high)


def spread_sums(values, channels):
    shape = values.shape[:-1] + (channels,)
    return jnp.concatenate(
        [jnp.broadcast_to(values[..., b : b + 1], shape) for b in range(3)], axis=-1
    )


def three(row):
    return jnp.concatenate([row] * 3, axis=1)


def conv_terms(firsts, count, padded, taps, terms):
    width, depth = padded.shape[1], padded.shape[2]
    total = None
    for a in terms:
        block = jnp.concatenate(
            [padded[pl.ds(first + a, count)].reshape(count * width, depth) for first in firsts],
            axis=0,
        )
        side = jnp.concatenate([taps[3 * a + b] for b in range(3)], axis=1)
        term = jnp.dot(block, side, preferred_element_type=F32)
        total = term if total is None else total + term
    return total


def conv_finish(total, firsts, width, out, wide, sums, at):
    channels = out.shape[1]
    span = total.shape[0] // len(firsts)
    value = (
        from_left(total[:, :channels], width)
        + total[:, channels : 2 * channels]
        + from_right(total[:, 2 * channels :], width)
    )
    for index, first in enumerate(firsts):
        part = value[index * span : (index + 1) * span]
        out[pl.ds(first * width, span), :] = part
        wide[pl.ds(first * width, span), : 3 * channels] = shifts_of(part, width)
    sums[at : at + 1] += jnp.sum(value, axis=0, keepdims=True)
    sums[at + 1 : at + 2] += jnp.sum(value * value, axis=0, keepdims=True)


def step_kernel(tiles, slides, bits, numbers, names, keys, *refs):
    ref = types.SimpleNamespace(**dict(zip(names, refs)))
    ref.parts = dict(zip(keys, refs[len(names) :]))
    ref.begun = (ref.fine_begun, ref.coarse_begun)
    fine, coarse, labels = ref.far_fine, ref.far_coarse, ref.labels
    fine_pad, coarse_pad = ref.fine_pad, ref.coarse_pad
    fine_conv, coarse_conv = ref.fine_conv, ref.coarse_conv
    sums, rows, class_kernel = ref.sums, ref.rows, ref.class_kernel
    me, slide = lax.axis_index("tile"), lax.axis_index("slide")
    height, width, _ = fine.shape
    channels = fine_conv.shape[1]
    classes = class_kernel.shape[0]
    targets = dict(fine=fine_pad.at[pl.ds(1, height)], coarse=coarse_pad.at[pl.ds(1, height // 2)])
    loads = {}
    for at, name in enumerate(names):
        if name.startswith("far_"):
            name = name[4:]
            loads[name] = pltpu.make_async_copy(
                refs[at], targets.get(name, getattr(ref, name, None)), ref.load_sem.at[at]
            )

    def start_loads():
        for copy in loads.values():
            copy.start()

    def prepare():
        for name, copy in loads.items():
            if not name.startswith(("fine", "coarse")) or name.endswith(("gain", "offset")):
                copy.wait()
        tissue_here = (labels[...] >= 0).astype(F32)
        ref.count[...] = jnp.broadcast_to(
            jnp.sum(tissue_here, axis=(0, 1), keepdims=True), ref.count.shape
        )
        sums[...] = jnp.zeros_like(sums)

    with jax.named_scope("greet"):
        greet(ring_peers("tile", tiles) + ring_peers("slide", slides), start_loads)

    def edge_copies(peer, down):
        return [
            pltpu.make_async_remote_copy(
                src_ref=source.at[source.shape[0] - 1 if down else 0],
                dst_ref=target.at[0 if down else target.shape[0] - 1],
                send_sem=ref.edge_send.at[int(down), at],
                recv_sem=ref.edge_recv.at[int(down), at],
                device_id={"tile": peer},
                device_id_type=MESH,
            )
            for at, (source, target) in enumerate(((fine, fine_pad), (coarse, coarse_pad)))
        ]

    down = edge_copies(lax.rem(me + 1, tiles), True)
    up = edge_copies(lax.rem(me + tiles - 1, tiles), False)

    @pl.when(me < tiles - 1)
    def _():
        for copy in down:
            copy.start()

    @pl.when(me > 0)
    def _():
        for copy in up:
            copy.start()

    with jax.named_scope("prepare"):
        prepare()
    fine_gain, fine_offset = ref.fine_gain[...], ref.fine_offset[...]
    coarse_gain, coarse_offset = ref.coarse_gain[...], ref.coarse_offset[...]

    def tile_copies(at, source, gather):
        return Spread(
            "tile", others_of("tile", tiles), source, gather, ref.tile_send.at[at], ref.tile_recv.at[at]
        )

    def near_first(at, source, gather):
        beside = me + 1 - 2 * lax.rem(me, 2)
        near_copy = pltpu.make_async_remote_copy(
            src_ref=source,
            dst_ref=gather.at[me],
            send_sem=ref.near_send.at[at - 1],
            recv_sem=ref.near_recv.at[at - 1],
            device_id={"tile": beside},
            device_id_type=MESH,
        )
        signs = [1 - 2 * lax.rem(me // 2**bit, 2) for bit in range(bits)]
        others = [
            me + sum(signs[bit] * 2**bit for bit in range(bits) if d // 2**bit % 2)
            for d in range(tiles - 1, 1, -1)
        ]
        return near_copy, Spread(
            "tile", others, source, gather, ref.tile_send.at[at], ref.tile_recv.at[at]
        )

    def slide_copies(at, source, gather):
        return Spread(
            "slide", others_of("slide", slides), source, gather, ref.slide_send.at[at], ref.slide_recv.at[at]
        )

    counts = tile_copies(0, ref.count, ref.count_gather)
    counts.start()
    ref.count_gather[me] = ref.count[...]

    @pl.when(me == 0)
    def _():
        for padded in (fine_pad, coarse_pad):
            padded[0] = jnp.zeros(padded.shape[1:], BF16)

    @pl.when(me == tiles - 1)
    def _():
        for padded in (fine_pad, coarse_pad):
            padded[padded.shape[0] - 1] = jnp.zeros(padded.shape[1:], BF16)

    size, half = 2 * width, width // 2
    levels = (
        (fine_pad, ref.fine_taps, fine_conv, ref.fine_wide, ref.fine_turned, height),
        (coarse_pad, ref.coarse_taps, coarse_conv, ref.coarse_wide, ref.coarse_turned, height // 2),
    )

    def turn(padded, turned, row):
        span = padded.shape[1]
        turned[:, row * span : (row + 1) * span] = padded[row].T

    with jax.named_scope("inner_conv"):
        for at, (padded, taps, out, wide, _, high) in enumerate(levels):
            with jax.named_scope("load_wait"):
                for name in (("fine", "fine_taps"), ("coarse", "coarse_taps"))[at]:
                    loads[name].wait()

            for step in range((high - 2) // PACK):
                total = conv_terms([1 + PACK * step], PACK, padded, taps, range(3))
                conv_finish(total, [1 + PACK * step], padded.shape[1], out, wide, sums, 2 * at)
            span = padded.shape[1]
            ref.begun[at][:span] = conv_terms([0], 1, padded, taps, (1, 2))
            ref.begun[at][span:] = conv_terms([high - 1], 1, padded, taps, (0, 1))

    with jax.named_scope("inner_turn"):
        for padded, _, _, wide, turned, high in levels:
            for row in range(1, high + 1):
                turn(padded, turned, row)
            span = padded.shape[1]

            @pl.loop(0, high)
            def _(row):
                here = pl.ds(pl.multiple_of(row * span, span), span)
                wide[here, 3 * channels :] = ones_of(span, channels, span)

    mine = [lax.rem(me // (2**bit), 2) for bit in range(bits)]
    partners = [{"tile": me + (1 - 2 * mine[bit]) * (2**bit)} for bit in range(bits)]
    plans = [stage_plan(bits, order_of(bits, piece % 2)) for piece in range(PIECES)]
    final = ref.final
    across = 3 * channels
    spans = [((piece + 3) % PIECES * across, across) for piece in range(PIECES)]

    def buffer(piece, stage, kind):
        if kind in (SEND, FSEND, COME) or (kind == RECV and stage == 0):
            return ref.parts[kind, 0, stage].at[piece]
        return ref.parts[kind, piece, stage]

    def stage_copy(piece, stage):
        bit, place, left = plans[piece][stage]
        return pltpu.make_async_remote_copy(
            src_ref=buffer(piece, stage, SEND),
            dst_ref=buffer(piece, stage, RECV),
            send_sem=ref.stage_send.at[stage - 1],
            recv_sem=ref.stage_recv.at[piece, stage - 1],
            device_id=partners[bit],
            device_id_type=MESH,
        )

    def piece_copies(piece):
        lanes = pl.ds(*spans[piece])
        return [
            pltpu.make_async_remote_copy(
                src_ref=final.at[slide, :, lanes],
                dst_ref=final.at[slide, :, lanes],
                send_sem=ref.piece_send.at[0],
                recv_sem=ref.piece_recv.at[piece, d - 1],
                device_id={"slide": lax.rem(slide + d, slides)},
                device_id_type=MESH,
            )
            for d in range(1, slides)
        ]

    def first_copy(piece, kind, target):
        bit, place, left = plans[piece][0]
        return pltpu.make_async_remote_copy(
            src_ref=buffer(piece, 0, kind).at[at_bits([(place, 1 - mine[bit])], left + 1)],
            dst_ref=buffer(piece, 0, target),
            send_sem=ref.first_send.at[int(kind == FORM)],
            recv_sem=ref.first_recv.at[int(kind == FORM), piece],
            device_id=partners[bit],
            device_id_type=MESH,
        )

    def fill(piece, stage, part):
        bit, spot, left = plans[piece][stage]
        buffer(piece, stage, SEND)[...] = part(at_bits([(spot, 1 - mine[bit])], left + 1)).astype(BF16)
        buffer(piece, stage, KEPT)[...] = part(at_bits([(spot, mine[bit])], left + 1))

    def pass_on(piece, stage, part):
        fill(piece, stage, part)
        stage_copy(piece, stage).start()

    def own_of(piece, kind):
        bit, place, left = plans[piece][0]
        return buffer(piece, 0, kind).at[at_bits([(place, mine[bit])], left + 1)]

    def halves(piece, stage):
        bit, spot, left = plans[piece][stage]
        return [at_bits([(spot, value)], left + 1) for value in (1 - mine[bit], mine[bit])]

    def form_copy(piece):
        return pltpu.make_async_remote_copy(
            src_ref=buffer(piece, 1, FSEND),
            dst_ref=buffer(piece, 1, FRECV),
            send_sem=ref.form_send.at[0],
            recv_sem=ref.form_recv.at[piece],
            device_id=partners[plans[piece][1][0]],
            device_id_type=MESH,
        )

    def centre_forms(piece, mean):
        away, here = halves(piece, 1)
        own, came = own_of(piece, FORM), buffer(piece, 0, COME)
        windows, send = buffer(piece, 0, WINDOW), buffer(piece, 1, FSEND)

        def centred(at):
            forms = own[at] + came[at]
            window = spread_sums(forms[..., across:], channels)
            windows[at] = window
            return forms[..., :across] - three(mean) * window, forms[..., across:]

        values, ends = centred(away)
        send[..., :across] = values.astype(BF16)
        send[..., across:] = split_sums(ends).astype(BF16)
        buffer(piece, 1, FKEPT)[...] = centred(here)[0]

    def close_forms(piece):
        form_copy(piece).wait_recv()
        kept, came = buffer(piece, 1, FKEPT), buffer(piece, 1, FRECV)
        kept[...] = kept[...] + came[..., :across].astype(F32)
        sums_came = came[..., across:].astype(F32)
        ends = sums_came[..., :3] + sums_came[..., 3:6]
        buffer(piece, 1, OTHER)[...] = spread_sums(ends, channels)

    def centre_grads(piece, gain, near):
        own, came = own_of(piece, GRAD), buffer(piece, 0, RECV)
        windows = buffer(piece, 0, WINDOW)
        wide_gain, wide_near = three(gain), three(near)

        def part(at):
            return wide_gain * (own[at] + came[at]) - wide_near * windows[at]

        fill(piece, 1, part)

    def join(piece, factors):
        stage_copy(piece, 1).wait_recv()
        kept, came = buffer(piece, 1, KEPT), buffer(piece, 1, RECV)
        forms, other = buffer(piece, 1, FKEPT), buffer(piece, 1, OTHER)
        windows = buffer(piece, 0, WINDOW).at[halves(piece, 1)[1]]
        wide = [three(factor) for factor in factors]

        def part(at):
            return (
                wide[0] * (kept[at] + came[at].astype(F32))
                + wide[1] * forms[at]
                + wide[2] * windows[at]
                + wide[3] * other[at]
            )

        pass_on(piece, 2, part)

    def advance(piece, stage):
        stage_copy(piece, stage).wait_recv()
        kept, came = buffer(piece, stage, KEPT), buffer(piece, stage, RECV)

        def part(chosen):
            return kept[chosen] + came[chosen].astype(F32)

        if stage == bits - 1:
            final[slide, :, pl.ds(*spans[piece])] = part(...)
            for copy in piece_copies(piece):
                copy.start()
        else:
            pass_on(piece, stage + 1, part)

    def product(piece, kind, level, a, ranges, more=False):
        padded, _, _, wide, turned, _ = levels[level]
        values = (ref.coarse_shifted if level else ref.fine_shifted) if kind == GRAD else wide
        span = padded.shape[1]
        out = buffer(piece, 0, kind)
        left = [turned[:, (a + first) * span : (a + last) * span] for first, last in ranges]
        right = [values[first * span : last * span, :] for first, last in ranges]
        term = jnp.dot(
            jnp.concatenate(left, axis=1),
            jnp.concatenate(right, axis=0),
            preferred_element_type=F32,
        ).reshape(out.shape)
        out[...] = out[...] + term if more else term

    def send_first(piece, kind):
        first_copy(piece, kind, RECV if kind == GRAD else COME).start()

    def row_copy(stage):
        return pltpu.make_async_remote_copy(
            src_ref=ref.row_sums.at[stage],
            dst_ref=ref.row_gather.at[stage],
            send_sem=ref.row_send.at[stage],
            recv_sem=ref.row_recv.at[stage],
            device_id=partners[stage],
            device_id_type=MESH,
        )

    head_copies = slide_copies(1, ref.row_sums.at[bits], ref.head_gather)

    def advance_rows(stage):
        row_copy(stage).wait()
        ref.row_sums[stage + 1] = ref.row_sums[stage] + ref.row_gather[stage]
        if stage + 1 < bits:
            row_copy(stage + 1).start()
        else:
            head_copies.start()
            ref.head_gather[slide] = ref.row_sums[bits]

    with jax.named_scope("inner_forms"):
        for a in range(3):
            product(3 + a, FORM, 0, a, [(1, height - 1)])

    for at, (padded, taps, out, wide, _, high) in enumerate(levels):
        with jax.named_scope("edge_wait"):

            @pl.when(me < tiles - 1)
            def _():
                down[at].wait_send()
                up[at].wait_recv()

            @pl.when(me > 0)
            def _():
                up[at].wait_send()
                down[at].wait_recv()

        with jax.named_scope("edge_conv"):
            span = padded.shape[1]
            for first, a in ((0, 0), (high - 1, 2)):
                here = slice(span) if first == 0 else slice(span, 2 * span)
                total = ref.begun[at][here] + conv_terms([first], 1, padded, taps, (a,))
                conv_finish(total, [first], span, out, wide, sums, 2 * at)

    ref.stat[...] = sums[0:4]
    near_stat, stat_copies = near_first(1, ref.stat, ref.stat_gather)
    near_stat.start()
    ref.stat_gather[me] = ref.stat[...]
    stat_copies.start()
    counts.wait()
    ref.slide_count[...] = ordered_sum(ref.count_gather, tiles)
    total_copies = slide_copies(0, ref.slide_count, ref.total_gather)
    total_copies.start()
    ref.total_gather[slide] = ref.slide_count[...]

    for padded, _, _, _, turned, high in levels:
        turn(padded, turned, 0)
        turn(padded, turned, high + 1)

    def pair_of(gather, tile):
        return gather[tile] + gather[tile + 1 - 2 * lax.rem(tile, 2)]

    def near_centres(tile):
        pair = pair_of(ref.stat_gather, tile)
        return [
            pair[2 * at : 2 * at + 1] / (numbers[at] * 2 / tiles / (channels // GROUPS))
            for at in range(2)
        ]

    def forms_came(pieces):
        for piece in pieces:
            first_copy(piece, FORM, COME).wait_recv()

    def send_forms(pieces):
        for piece in pieces:
            form_copy(piece).start()

    def form_product(piece):
        if piece < 3:
            product(piece, FORM, 1, piece, [(0, height // 2)])
        else:
            product(piece, FORM, 0, piece - 3, [(0, 1), (height - 1, height)], more=True)

    with jax.named_scope("form_products"):
        for pair in ((0, 1), (2, 3)):
            for piece in pair:
                form_product(piece)
            for piece in pair:
                send_first(piece, FORM)
        near_stat.wait()
        centres = near_centres(me)
        form_product(4)
        send_first(4, FORM)
        forms_came(range(2))
        form_product(5)
        for piece in range(2):
            centre_forms(piece, centres[1])
        send_first(5, FORM)
        send_forms(range(2))
        for piece in range(2, EARLY):
            forms_came([piece])
            centre_forms(piece, centres[1 - piece // 3])
            send_forms([piece])

    scope = jax.named_scope("stat_wait")
    scope.__enter__()
    stat_copies.wait()
    total_copies.wait()
    total = ordered_sum(ref.total_gather, slides)
    count = total[0:1, 0:1]
    scope.__exit__(None, None, None)
    group_sums = group_sums_of(ordered_sum(ref.stat_gather, tiles), channels)

    def terms_of(at, number):
        mean = group_sums[at : at + 1] / number
        variance = group_sums[at + 1 : at + 2] / number - mean * mean
        return mean, lax.rsqrt(variance + EPSILON)

    fine_mean, fine_scale = terms_of(0, numbers[0])
    coarse_mean, coarse_scale = terms_of(2, numbers[1])

    square = (classes, classes)
    offset = jnp.sum(
        jnp.where(
            lanes_of(square) == lanes_of(square, 0),
            jnp.broadcast_to(ref.class_offset[...], square),
            0.0,
        ),
        axis=1,
        keepdims=True,
    )
    rows[...] = jnp.zeros_like(rows)

    forms_came(range(EARLY, PIECES))
    scope = jax.named_scope("head")
    scope.__enter__()
    for piece in range(EARLY, PIECES):
        centre_forms(piece, centres[0])

    for step in range(height // 2):
        widen, fold = ref.widen.at[step], ref.fold.at[step]
        fine_at = pl.ds(step * size, size)
        coarse_at = pl.ds(step * half, half)
        fine_normed = (fine_conv[fine_at, :] - fine_mean) * fine_scale
        fine_pre = fine_normed * fine_gain + fine_offset
        coarse_normed = (coarse_conv[coarse_at, :] - coarse_mean) * coarse_scale
        coarse_pre = coarse_normed * coarse_gain + coarse_offset
        coarse_act = jnp.maximum(coarse_pre, 0.0)
        widen[pl.ds(0, half, stride=2), :] = coarse_act
        widen[pl.ds(1, half, stride=2), :] = coarse_act
        upsampled = widen[...]
        merged = (
            jnp.maximum(fine_pre, 0.0) + jnp.concatenate([upsampled, upsampled], axis=0)
        ).astype(BF16)
        logits = (
            lax.dot_general(
                class_kernel[...], merged, (((1,), (1,)), ((), ())), preferred_element_type=F32
            )
            + offset
        )
        label = jnp.concatenate(
            [labels[pl.ds(2 * step, 1), :], labels[pl.ds(2 * step + 1, 1), :]], axis=1
        )
        onehot = (lanes_of((classes, size), 0) == label).astype(F32)
        tissue = (label >= 0).astype(F32)
        top = jnp.max(logits, axis=0, keepdims=True)
        lse = top + jnp.log(jnp.sum(jnp.exp(logits - top), axis=0, keepdims=True))
        picked = jnp.sum(onehot * logits, axis=0, keepdims=True)
        loss = jnp.sum((lse - picked) * tissue, axis=1, keepdims=True)
        dlogits = ((jnp.exp(logits - lse) - onehot) * tissue / count).astype(BF16)
        dmerged = lax.dot_general(
            dlogits, class_kernel[...], (((0,), (0,)), ((), ())), preferred_element_type=F32
        )
        fine_d = jnp.where(fine_pre > 0, dmerged, 0.0)
        ref.fine_shifted[fine_at, :] = shifts_of(fine_d, width)
        fold[...] = dmerged[:width] + dmerged[width:]
        blocks = fold[pl.ds(0, half, stride=2), :] + fold[pl.ds(1, half, stride=2), :]
        coarse_d = jnp.where(coarse_pre > 0, blocks, 0.0)
        ref.coarse_shifted[coarse_at, :] = shifts_of(coarse_d, half)
        rows[0:1] += jnp.sum(fine_d * fine_normed, axis=0, keepdims=True)
        rows[1:2] += jnp.sum(fine_d, axis=0, keepdims=True)
        rows[2:3] += jnp.sum(coarse_d * coarse_normed, axis=0, keepdims=True)
        rows[3:4] += jnp.sum(coarse_d, axis=0, keepdims=True)
        rows[4 : 4 + classes] += jnp.dot(dlogits, merged, preferred_element_type=F32)
        rows[4 + classes : 5 + classes] += jnp.broadcast_to(loss, (1, channels))

    scope.__exit__(None, None, None)
    gains = jnp.concatenate([fine_gain, fine_gain, coarse_gain, coarse_gain], axis=0)
    ref.back[...] = rows[0:4] * gains
    near_copy, back_copies = near_first(2, ref.back, ref.back_gather)
    near_copy.start()
    back_copies.start()
    ref.back_gather[me] = ref.back[...]
    ref.row_sums[0] = rows[...]
    send_forms(range(EARLY, PIECES))
    row_copy(0).start()
    stats = ((fine_mean, fine_scale), (coarse_mean, coarse_scale))

    def near_means(tile):
        pair = pair_of(ref.back_gather, tile)
        sums_here = group_sums_of(pair, channels)
        return [
            sums_here[2 * at + 1 : 2 * at + 2] / (numbers[at] * 2 / tiles) for at in range(2)
        ]

    def grad_product(piece):
        level = 1 - piece // 3
        product(piece, GRAD, level, piece % 3, [(0, (height, height // 2)[level])])

    def grads_came(pieces):
        for piece in pieces:
            first_copy(piece, GRAD, RECV).wait_recv()

    def centre(pieces):
        for piece in pieces:
            centre_grads(piece, *((coarse_gain, near[1]) if piece < 3 else (fine_gain, near[0])))

    def send(pieces):
        for piece in pieces:
            stage_copy(piece, 1).start()

    with jax.named_scope("grads_a"):
        for piece in range(4):
            grad_product(piece)
            send_first(piece, GRAD)
    with jax.named_scope("grads_wait"):
        near_copy.wait()
        near = near_means(me)
        for piece in range(3):
            grads_came([piece])
            centre([piece])
            send([piece])
        advance_rows(0)
    with jax.named_scope("grads_c"):
        grad_product(4)
        send_first(4, GRAD)
        grads_came([3])
    with jax.named_scope("grads_d"):
        grad_product(5)
        centre([3])
        send_first(5, GRAD)
        send([3])
    with jax.named_scope("close_a"):
        for piece in range(2):
            close_forms(piece)
        grads_came([4])
        centre([4])
        send([4])
        close_forms(2)
        grads_came([5])
        centre([5])
        send([5])
    with jax.named_scope("close_b"):
        for piece in range(3, PIECES):
            close_forms(piece)
    advance_rows(1)
    with jax.named_scope("back_wait"):
        back_copies.wait()
    back = group_sums_of(ordered_sum(ref.back_gather, tiles), channels)
    peers = {
        bit: (near_means(partners[bit]["tile"]), near_centres(partners[bit]["tile"]))
        for bit in {plan[1][0] for plan in plans}
    }

    def factors_of(piece):
        at = 1 - piece // 3
        mean, scale = stats[at]
        first = back[2 * at + 1 : 2 * at + 2] / numbers[at]
        second = back[2 * at : 2 * at + 1] / numbers[at] * scale * scale
        peer_near, peer_centres = peers[plans[piece][1][0]]
        return (
            scale,
            -second,
            scale * (near[at] - first) - second * (centres[at] - mean),
            scale * (peer_near[at] - first) - second * (peer_centres[at] - mean),
        )

    with jax.named_scope("join"):
        for piece in range(3):
            join(piece, factors_of(piece))
    with jax.named_scope("join_fine"):
        for piece in range(3, PIECES):
            join(piece, factors_of(piece))
    advance_rows(2)
    for stage in range(2, bits):
        with jax.named_scope("stage%d" % stage):
            for piece in range(PIECES):
                advance(piece, stage)
                if stage > 2 and piece == 2:
                    advance_rows(stage)
    scope = jax.named_scope("finish")
    scope.__enter__()
    sent = [(ref.parts[SEND, 0, stage], ref.stage_send.at[stage - 1]) for stage in range(1, bits)]
    sent += [(ref.parts[FSEND, 0, 1], ref.form_send.at[0])]
    sent += [(ref.parts[RECV, 0, 0], ref.first_send.at[0])]
    sent += [(ref.parts[COME, 0, 0], ref.first_send.at[1])]
    sent += [(final.at[pl.ds(0, slides - 1)], ref.piece_send.at[0])]
    for buffers, sem in sent:
        pltpu.make_async_copy(buffers, buffers, sem).wait()
    head_copies.wait()
    row_total = ordered_sum(ref.head_gather, slides)
    ref.heads[...] = row_total
    ref.heads[4 + classes : 5 + classes] = row_total[4 + classes : 5 + classes] / count
    for piece in range(PIECES):
        for copy in piece_copies(piece):
            copy.wait_recv()
        level, a = spans[piece][0] // across // 3, spans[piece][0] // across % 3
        whole = ordered_sum(final.at[:, :, pl.ds(*spans[piece])], slides)
        for b in range(3):
            ref.grads[pl.ds(6 * a + 2 * b + level, whole.shape[0], stride=18), :] = whole[
                :, b * channels : (b + 1) * channels
            ]
    scope.__exit__(None, None, None)


def per_device(
    fine_level,
    coarse_level,
    fine_kernel,
    coarse_kernel,
    fine_gain,
    fine_offset,
    coarse_gain,
    coarse_offset,
    class_kernel,
    class_offset,
    tissue_labels,
):
    tiles, slides = lax.axis_size("tile"), lax.axis_size("slide")
    bits = tiles.bit_length() - 1
    in_channels, _, channels = fine_kernel.shape
    classes = class_kernel.shape[0]
    fine, coarse, labels = fine_level[0], coarse_level[0], tissue_labels[0]
    height, width = fine.shape[0], fine.shape[1]
    fine_number = height * tiles * width * (channels // GROUPS)
    numbers = (float(fine_number), float(fine_number // 4))
    pixels, half = height * width, width // 2
    slide_ends = max(slides - 1, 1)
    chunk = in_channels // tiles
    row_count = -(-(5 + classes) // 8) * 8

    inputs = dict(
        fine=fine,
        fine_taps=fine_kernel.transpose(1, 0, 2),
        labels=labels,
        coarse=coarse,
        coarse_taps=coarse_kernel.transpose(1, 0, 2),
        fine_gain=fine_gain[None, :],
        fine_offset=fine_offset[None, :],
        coarse_gain=coarse_gain[None, :],
        coarse_offset=coarse_offset[None, :],
        class_kernel=class_kernel,
        class_offset=class_offset[None, :],
    )
    outputs = dict(
        heads=pltpu.VMEM((row_count, channels), F32),
        grads=pltpu.VMEM((chunk * 18, channels), F32),
    )
    line, lines = (1, channels), (4, channels)
    scratch = {
        name: pltpu.VMEM(value.shape, value.dtype)
        for name, value in inputs.items()
        if name not in ("fine", "coarse")
    }
    scratch |= dict(
        final=pltpu.VMEM((slides, chunk, 18 * channels), F32),
        head_gather=pltpu.VMEM((slides, row_count, channels), F32),
        load_sem=dma_sems(len(inputs)),
        fine_pad=pltpu.VMEM((height + 2, width, in_channels), BF16),
        coarse_pad=pltpu.VMEM((height // 2 + 2, half, in_channels), BF16),
        fine_conv=pltpu.VMEM((pixels, channels), F32),
        coarse_conv=pltpu.VMEM((pixels // 4, channels), F32),
        fine_begun=pltpu.VMEM((2 * width, 3 * channels), F32),
        coarse_begun=pltpu.VMEM((2 * half, 3 * channels), F32),
        fine_wide=pltpu.VMEM((pixels, 4 * channels), BF16),
        coarse_wide=pltpu.VMEM((pixels // 4, 4 * channels), BF16),
        fine_turned=pltpu.VMEM((in_channels, (height + 2) * width), BF16),
        coarse_turned=pltpu.VMEM((in_channels, (height // 2 + 2) * half), BF16),
        fine_shifted=pltpu.VMEM((pixels, 3 * channels), BF16),
        coarse_shifted=pltpu.VMEM((pixels // 4, 3 * channels), BF16),
        widen=pltpu.VMEM((height // 2, width, channels), F32),
        fold=pltpu.VMEM((height // 2, width, channels), F32),
        sums=pltpu.VMEM((8, channels), F32),
        rows=pltpu.VMEM((row_count, channels), F32),
        row_sums=pltpu.VMEM((bits + 1, row_count, channels), F32),
        row_gather=pltpu.VMEM((bits, row_count, channels), F32),
        row_send=dma_sems(bits),
        row_recv=dma_sems(bits),
        count=pltpu.VMEM(line, F32),
        stat=pltpu.VMEM(lines, F32),
        back=pltpu.VMEM(lines, F32),
        slide_count=pltpu.VMEM(line, F32),
        count_gather=pltpu.VMEM((tiles,) + line, F32),
        stat_gather=pltpu.VMEM((tiles,) + lines, F32),
        back_gather=pltpu.VMEM((tiles,) + lines, F32),
        total_gather=pltpu.VMEM((slides,) + line, F32),
        edge_send=dma_sems(2, 2),
        edge_recv=dma_sems(2, 2),
        near_send=dma_sems(2),
        near_recv=dma_sems(2),
        form_send=dma_sems(1),
        form_recv=dma_sems(PIECES),
        tile_send=dma_sems(3),
        tile_recv=dma_sems(3),
        slide_send=dma_sems(2),
        slide_recv=dma_sems(2),
        piece_send=dma_sems(1),
        piece_recv=dma_sems(PIECES, slide_ends),
        first_send=dma_sems(2),
        first_recv=dma_sems(2, PIECES),
        stage_send=dma_sems(bits - 1),
        stage_recv=dma_sems(PIECES, bits - 1),
    )
    parts = {}
    span = 3 * channels
    for piece in range(PIECES):
        parts[GRAD, piece, 0] = pltpu.VMEM((2,) * bits + (chunk, span), F32)
        plan = stage_plan(bits, order_of(bits, piece % 2))
        forms = (chunk, 4 * channels)
        parts[FORM, piece, 0] = pltpu.VMEM((2,) * bits + forms, F32)
        parts[WINDOW, piece, 0] = pltpu.VMEM((2,) * (bits - 1) + (chunk, span), F32)
        parts[COME, 0, 0] = pltpu.VMEM((PIECES,) + (2,) * (bits - 1) + forms, F32)
        for stage, (_, _, left) in enumerate(plan):
            below = (2,) * left + (chunk, span)
            if stage:
                parts[RECV, piece, stage] = pltpu.VMEM(below, BF16)
            else:
                parts[RECV, 0, 0] = pltpu.VMEM((PIECES,) + below, F32)
            if stage == 1:
                wider = below[:-1] + (4 * channels,)
                parts[FSEND, 0, 1] = pltpu.VMEM((PIECES,) + wider, BF16)
                parts[FRECV, piece, 1] = pltpu.VMEM(wider, BF16)
                parts[FKEPT, piece, 1] = pltpu.VMEM(below, F32)
                parts[OTHER, piece, 1] = pltpu.VMEM(below, F32)
            if stage:
                parts[SEND, 0, stage] = pltpu.VMEM((PIECES,) + below, BF16)
                parts[KEPT, piece, stage] = pltpu.VMEM(below, F32)
    names = ["far_" + name for name in inputs] + list(outputs) + list(scratch)
    results = call(
        functools.partial(step_kernel, tiles, slides, bits, numbers, names, list(parts)),
        tuple(outputs.values()),
        list(scratch.values()) + list(parts.values()),
        tuple(inputs.values()),
    )
    loss, head, grads = store(*results, classes)
    return (loss[0, 0], head, grads.reshape(chunk, 9, 2, channels).transpose(0, 2, 1, 3))


def solution(mesh):
    return jax.shard_map(
        per_device,
        mesh=mesh,
        in_specs=(
            P("slide", "tile", None, None),
            P("slide", "tile", None, None),
            P(),
            P(),
            P(),
            P(),
            P(),
            P(),
            P(),
            P(),
            P("slide", "tile", None),
        ),
        out_specs=(P(), P(), P("tile", None, None, None)),
        check_vma=False,
    )
```

```python
import functools
import types

import jax
import jax.numpy as jnp
from jax import lax
from jax.experimental import pallas as pl
from jax.experimental.pallas import tpu as pltpu
from jax.sharding import PartitionSpec as P

GROUPS = 32
EPSILON = 1e-05
F32 = jnp.float32
BF16 = jnp.bfloat16
MESH = pl.DeviceIdType.MESH
VMEM = pl.BlockSpec(memory_space=pltpu.VMEM)
ANY = pl.BlockSpec(memory_space=pl.ANY)
LIMIT = 60 * 1024 * 1024
HIGH = lax.Precision.HIGHEST


def call(body, out_shape, scratch, args):
    return pl.pallas_call(
        body,
        out_shape=out_shape,
        in_specs=[ANY] * len(args),
        out_specs=jax.tree.map(lambda _: VMEM, out_shape),
        scratch_shapes=scratch,
        compiler_params=pltpu.CompilerParams(
            vmem_limit_bytes=LIMIT, collective_id=0, has_side_effects=True
        ),
    )(*args)


def store_kernel(classes, rows, grads, loss_out, head_out, grads_out, loss, sems):
    copies = [
        pltpu.make_async_copy(source, target, sems.at[at])
        for at, (source, target) in enumerate(
            ((grads, grads_out), (rows.at[pl.ds(0, 4 + classes)], head_out), (loss, loss_out))
        )
    ]
    for copy in copies[:2]:
        copy.start()
    loss[...] = rows[4 + classes : 5 + classes, 0:1]
    copies[2].start()
    for copy in copies:
        copy.wait()


def store(rows, grads, classes):
    return pl.pallas_call(
        functools.partial(store_kernel, classes),
        out_shape=(
            shape_of((1, 1)),
            shape_of((4 + classes, rows.shape[1])),
            shape_of(grads.shape),
        ),
        in_specs=[VMEM, VMEM],
        out_specs=(ANY, ANY, ANY),
        scratch_shapes=[pltpu.VMEM((1, 1), F32), dma_sems(3)],
    )(*(pltpu.with_memory_space_constraint(value, pltpu.VMEM) for value in (rows, grads)))


def shape_of(dims, dtype=F32):
    return jax.ShapeDtypeStruct(dims, dtype)


def greet(peers, meanwhile):
    barrier = pltpu.get_barrier_semaphore()
    for peer in peers:
        pl.semaphore_signal(barrier, inc=1, device_id=peer, device_id_type=MESH)
    meanwhile()
    pl.semaphore_wait(barrier, len(peers))


def others_of(axis, size):
    me = lax.axis_index(axis)
    return [lax.rem(me + d, size) for d in range(1, size)]


def ring_peers(axis, size):
    return [{axis: peer} for peer in others_of(axis, size)]


class Spread:
    def __init__(self, axis, peers, source, gather, send_sem, recv_sem):
        me = lax.axis_index(axis)
        self.copies = [
            pltpu.make_async_remote_copy(
                src_ref=source,
                dst_ref=gather.at[me],
                send_sem=send_sem,
                recv_sem=recv_sem,
                device_id={axis: peer},
                device_id_type=MESH,
            )
            for peer in peers
        ]
        others = gather.at[pl.ds(0, len(self.copies))]
        self.ends = [pltpu.make_async_copy(others, others, sem) for sem in (send_sem, recv_sem)]

    def start(self):
        for copy in self.copies:
            copy.start()

    def wait(self):
        if self.copies:
            for end in self.ends:
                end.wait()


def ordered_sum(gather, size):
    total = gather[0]
    for index in range(1, size):
        total = total + gather[index]
    return total


def dma_sems(*dims):
    return pltpu.SemaphoreType.DMA(dims)


def column_of(shape, width):
    return lax.rem(lax.broadcasted_iota(jnp.int32, shape, 0), width)


def from_left(values, width):
    moved = pltpu.roll(values, 1, axis=0)
    return jnp.where(column_of(values.shape, width) == 0, 0.0, moved)


def from_right(values, width):
    moved = pltpu.roll(values, values.shape[0] - 1, axis=0)
    return jnp.where(column_of(values.shape, width) == width - 1, 0.0, moved)


def stage_plan(bits, order):
    left = list(reversed(range(bits)))
    plan = []
    for bit in order:
        place = left.index(bit)
        left = [other for other in left if other != bit]
        plan.append((bit, place, len(left)))
    return plan


def at_bits(places, count):
    index = [slice(None)] * count
    for place, value in places:
        index[place] = value
    return tuple(index)


def order_of(bits, turn):
    order = list(range(bits))
    if turn and bits > 2:
        order[1], order[2] = order[2], order[1]
    return order


def lanes_of(shape, dim=1):
    return lax.broadcasted_iota(jnp.int32, shape, dim)


def group_sums_of(rows, channels):
    step = 1
    while step < channels // GROUPS:
        after, before = pltpu.roll(rows, channels - step, axis=1), pltpu.roll(rows, step, axis=1)
        rows = rows + jnp.where(lanes_of(rows.shape) // step % 2 == 0, after, before)
        step *= 2
    return rows


PACK = 2
PIECES = 6
EARLY = 6
GRAD, SEND, RECV, KEPT, FORM, COME, WINDOW, FSEND, FRECV, FKEPT, OTHER = range(11)


def shifts_of(values, width):
    return jnp.concatenate(
        [from_right(values, width), values, from_left(values, width)], axis=1
    ).astype(BF16)


def ones_of(rows, channels, width):
    column = column_of((rows, channels), width)
    lane = lanes_of((rows, channels))
    side = lax.rem(lane, 3)
    outside = ((side == 0) & (column == width - 1)) | ((side == 2) & (column == 0)) | (lane > 5)
    return jnp.where(outside, 0.0, 1.0).astype(BF16)


def split_sums(values):
    high = values.astype(BF16).astype(F32)
    return jnp.where(lanes_of(values.shape, values.ndim - 1) < 3, high, values - high)


def spread_sums(values, channels):
    shape = values.shape[:-1] + (channels,)
    return jnp.concatenate(
        [jnp.broadcast_to(values[..., b : b + 1], shape) for b in range(3)], axis=-1
    )


def three(row):
    return jnp.concatenate([row] * 3, axis=1)


def conv_terms(firsts, count, padded, taps, terms):
    width, depth = padded.shape[1], padded.shape[2]
    total = None
    for a in terms:
        block = jnp.concatenate(
            [padded[pl.ds(first + a, count)].reshape(count * width, depth) for first in firsts],
            axis=0,
        )
        side = jnp.concatenate([taps[3 * a + b] for b in range(3)], axis=1)
        term = jnp.dot(block, side, preferred_element_type=F32)
        total = term if total is None else total + term
    return total


def conv_finish(total, firsts, width, out, wide, sums, at):
    channels = out.shape[1]
    span = total.shape[0] // len(firsts)
    value = (
        from_left(total[:, :channels], width)
        + total[:, channels : 2 * channels]
        + from_right(total[:, 2 * channels :], width)
    )
    for index, first in enumerate(firsts):
        part = value[index * span : (index + 1) * span]
        out[pl.ds(first * width, span), :] = part
        wide[pl.ds(first * width, span), : 3 * channels] = shifts_of(part, width)
    sums[at : at + 1] += jnp.sum(value, axis=0, keepdims=True)
    sums[at + 1 : at + 2] += jnp.sum(value * value, axis=0, keepdims=True)


def step_kernel(tiles, slides, bits, numbers, names, keys, *refs):
    ref = types.SimpleNamespace(**dict(zip(names, refs)))
    ref.parts = dict(zip(keys, refs[len(names) :]))
    ref.begun = (ref.fine_begun, ref.coarse_begun)
    fine, coarse, labels = ref.far_fine, ref.far_coarse, ref.labels
    fine_pad, coarse_pad = ref.fine_pad, ref.coarse_pad
    fine_conv, coarse_conv = ref.fine_conv, ref.coarse_conv
    sums, rows, class_kernel = ref.sums, ref.rows, ref.class_kernel
    me, slide = lax.axis_index("tile"), lax.axis_index("slide")
    height, width, _ = fine.shape
    channels = fine_conv.shape[1]
    classes = class_kernel.shape[0]
    targets = dict(fine=fine_pad.at[pl.ds(1, height)], coarse=coarse_pad.at[pl.ds(1, height // 2)])
    loads = {}
    for at, name in enumerate(names):
        if name.startswith("far_"):
            name = name[4:]
            loads[name] = pltpu.make_async_copy(
                refs[at], targets.get(name, getattr(ref, name, None)), ref.load_sem.at[at]
            )

    def start_loads():
        for copy in loads.values():
            copy.start()

    def prepare():
        for name, copy in loads.items():
            if not name.startswith(("fine", "coarse")) or name.endswith(("gain", "offset")):
                copy.wait()
        tissue_here = (labels[...] >= 0).astype(F32)
        ref.count[...] = jnp.broadcast_to(
            jnp.sum(tissue_here, axis=(0, 1), keepdims=True), ref.count.shape
        )
        sums[...] = jnp.zeros_like(sums)

    with jax.named_scope("greet"):
        greet(ring_peers("tile", tiles) + ring_peers("slide", slides), start_loads)

    def edge_copies(peer, down):
        return [
            pltpu.make_async_remote_copy(
                src_ref=source.at[source.shape[0] - 1 if down else 0],
                dst_ref=target.at[0 if down else target.shape[0] - 1],
                send_sem=ref.edge_send.at[int(down), at],
                recv_sem=ref.edge_recv.at[int(down), at],
                device_id={"tile": peer},
                device_id_type=MESH,
            )
            for at, (source, target) in enumerate(((fine, fine_pad), (coarse, coarse_pad)))
        ]

    down = edge_copies(lax.rem(me + 1, tiles), True)
    up = edge_copies(lax.rem(me + tiles - 1, tiles), False)

    @pl.when(me < tiles - 1)
    def _():
        for copy in down:
            copy.start()

    @pl.when(me > 0)
    def _():
        for copy in up:
            copy.start()

    with jax.named_scope("prepare"):
        prepare()
    fine_gain, fine_offset = ref.fine_gain[...], ref.fine_offset[...]
    coarse_gain, coarse_offset = ref.coarse_gain[...], ref.coarse_offset[...]

    def tile_copies(at, source, gather):
        return Spread(
            "tile", others_of("tile", tiles), source, gather, ref.tile_send.at[at], ref.tile_recv.at[at]
        )

    def near_first(at, source, gather):
        beside = me + 1 - 2 * lax.rem(me, 2)
        near_copy = pltpu.make_async_remote_copy(
            src_ref=source,
            dst_ref=gather.at[me],
            send_sem=ref.near_send.at[at - 1],
            recv_sem=ref.near_recv.at[at - 1],
            device_id={"tile": beside},
            device_id_type=MESH,
        )
        signs = [1 - 2 * lax.rem(me // 2**bit, 2) for bit in range(bits)]
        others = [
            me + sum(signs[bit] * 2**bit for bit in range(bits) if d // 2**bit % 2)
            for d in range(tiles - 1, 1, -1)
        ]
        return near_copy, Spread(
            "tile", others, source, gather, ref.tile_send.at[at], ref.tile_recv.at[at]
        )

    def slide_copies(at, source, gather):
        return Spread(
            "slide", others_of("slide", slides), source, gather, ref.slide_send.at[at], ref.slide_recv.at[at]
        )

    counts = tile_copies(0, ref.count, ref.count_gather)
    counts.start()
    ref.count_gather[me] = ref.count[...]

    @pl.when(me == 0)
    def _():
        for padded in (fine_pad, coarse_pad):
            padded[0] = jnp.zeros(padded.shape[1:], BF16)

    @pl.when(me == tiles - 1)
    def _():
        for padded in (fine_pad, coarse_pad):
            padded[padded.shape[0] - 1] = jnp.zeros(padded.shape[1:], BF16)

    size, half = 2 * width, width // 2
    levels = (
        (fine_pad, ref.fine_taps, fine_conv, ref.fine_wide, ref.fine_turned, height),
        (coarse_pad, ref.coarse_taps, coarse_conv, ref.coarse_wide, ref.coarse_turned, height // 2),
    )

    def turn(padded, turned, row):
        span = padded.shape[1]
        turned[:, row * span : (row + 1) * span] = padded[row].T

    with jax.named_scope("inner_conv"):
        for at, (padded, taps, out, wide, _, high) in enumerate(levels):
            with jax.named_scope("load_wait"):
                for name in (("fine", "fine_taps"), ("coarse", "coarse_taps"))[at]:
                    loads[name].wait()

            for step in range((high - 2) // PACK):
                total = conv_terms([1 + PACK * step], PACK, padded, taps, range(3))
                conv_finish(total, [1 + PACK * step], padded.shape[1], out, wide, sums, 2 * at)
            span = padded.shape[1]
            ref.begun[at][:span] = conv_terms([0], 1, padded, taps, (1, 2))
            ref.begun[at][span:] = conv_terms([high - 1], 1, padded, taps, (0, 1))

    with jax.named_scope("inner_turn"):
        for padded, _, _, wide, turned, high in levels:
            for row in range(1, high + 1):
                turn(padded, turned, row)
            span = padded.shape[1]

            @pl.loop(0, high)
            def _(row):
                here = pl.ds(pl.multiple_of(row * span, span), span)
                wide[here, 3 * channels :] = ones_of(span, channels, span)

    mine = [lax.rem(me // (2**bit), 2) for bit in range(bits)]
    partners = [{"tile": me + (1 - 2 * mine[bit]) * (2**bit)} for bit in range(bits)]
    plans = [stage_plan(bits, order_of(bits, (piece + 1) % 2)) for piece in range(PIECES)]
    final = ref.final
    across = 3 * channels
    spans = [((piece + 3) % PIECES * across, across) for piece in range(PIECES)]

    def buffer(piece, stage, kind):
        if kind in (SEND, FSEND, COME) or (kind == RECV and stage == 0):
            return ref.parts[kind, 0, stage].at[piece]
        return ref.parts[kind, piece, stage]

    def stage_copy(piece, stage):
        bit, place, left = plans[piece][stage]
        return pltpu.make_async_remote_copy(
            src_ref=buffer(piece, stage, SEND),
            dst_ref=buffer(piece, stage, RECV),
            send_sem=ref.stage_send.at[stage - 1],
            recv_sem=ref.stage_recv.at[piece, stage - 1],
            device_id=partners[bit],
            device_id_type=MESH,
        )

    def piece_copies(piece):
        lanes = pl.ds(*spans[piece])
        return [
            pltpu.make_async_remote_copy(
                src_ref=final.at[slide, :, lanes],
                dst_ref=final.at[slide, :, lanes],
                send_sem=ref.piece_send.at[0],
                recv_sem=ref.piece_recv.at[piece, d - 1],
                device_id={"slide": lax.rem(slide + d, slides)},
                device_id_type=MESH,
            )
            for d in range(1, slides)
        ]

    def first_copy(piece, kind, target):
        bit, place, left = plans[piece][0]
        return pltpu.make_async_remote_copy(
            src_ref=buffer(piece, 0, kind).at[at_bits([(place, 1 - mine[bit])], left + 1)],
            dst_ref=buffer(piece, 0, target),
            send_sem=ref.first_send.at[int(kind == FORM)],
            recv_sem=ref.first_recv.at[int(kind == FORM), piece],
            device_id=partners[bit],
            device_id_type=MESH,
        )

    def fill(piece, stage, part):
        bit, spot, left = plans[piece][stage]
        buffer(piece, stage, SEND)[...] = part(at_bits([(spot, 1 - mine[bit])], left + 1)).astype(BF16)
        buffer(piece, stage, KEPT)[...] = part(at_bits([(spot, mine[bit])], left + 1))

    def pass_on(piece, stage, part):
        fill(piece, stage, part)
        stage_copy(piece, stage).start()

    def own_of(piece, kind):
        bit, place, left = plans[piece][0]
        return buffer(piece, 0, kind).at[at_bits([(place, mine[bit])], left + 1)]

    def halves(piece, stage):
        bit, spot, left = plans[piece][stage]
        return [at_bits([(spot, value)], left + 1) for value in (1 - mine[bit], mine[bit])]

    def form_copy(piece):
        return pltpu.make_async_remote_copy(
            src_ref=buffer(piece, 1, FSEND),
            dst_ref=buffer(piece, 1, FRECV),
            send_sem=ref.form_send.at[0],
            recv_sem=ref.form_recv.at[piece],
            device_id=partners[plans[piece][1][0]],
            device_id_type=MESH,
        )

    def centre_forms(piece, mean):
        away, here = halves(piece, 1)
        own, came = own_of(piece, FORM), buffer(piece, 0, COME)
        windows, send = buffer(piece, 0, WINDOW), buffer(piece, 1, FSEND)

        def centred(at):
            forms = own[at] + came[at]
            window = spread_sums(forms[..., across:], channels)
            windows[at] = window
            return forms[..., :across] - three(mean) * window, forms[..., across:]

        values, ends = centred(away)
        send[..., :across] = values.astype(BF16)
        send[..., across:] = split_sums(ends).astype(BF16)
        buffer(piece, 1, FKEPT)[...] = centred(here)[0]

    def close_forms(piece):
        form_copy(piece).wait_recv()
        kept, came = buffer(piece, 1, FKEPT), buffer(piece, 1, FRECV)
        kept[...] = kept[...] + came[..., :across].astype(F32)
        sums_came = came[..., across:].astype(F32)
        ends = sums_came[..., :3] + sums_came[..., 3:6]
        buffer(piece, 1, OTHER)[...] = spread_sums(ends, channels)

    def centre_grads(piece, gain, near):
        own, came = own_of(piece, GRAD), buffer(piece, 0, RECV)
        windows = buffer(piece, 0, WINDOW)
        wide_gain, wide_near = three(gain), three(near)

        def part(at):
            return wide_gain * (own[at] + came[at]) - wide_near * windows[at]

        fill(piece, 1, part)

    def join(piece, factors):
        stage_copy(piece, 1).wait_recv()
        kept, came = buffer(piece, 1, KEPT), buffer(piece, 1, RECV)
        forms, other = buffer(piece, 1, FKEPT), buffer(piece, 1, OTHER)
        windows = buffer(piece, 0, WINDOW).at[halves(piece, 1)[1]]
        wide = [three(factor) for factor in factors]

        def part(at):
            return (
                wide[0] * (kept[at] + came[at].astype(F32))
                + wide[1] * forms[at]
                + wide[2] * windows[at]
                + wide[3] * other[at]
            )

        pass_on(piece, 2, part)

    def advance(piece, stage):
        stage_copy(piece, stage).wait_recv()
        kept, came = buffer(piece, stage, KEPT), buffer(piece, stage, RECV)

        def part(chosen):
            return kept[chosen] + came[chosen].astype(F32)

        if stage == bits - 1:
            final[slide, :, pl.ds(*spans[piece])] = part(...)
            for copy in piece_copies(piece):
                copy.start()
        else:
            pass_on(piece, stage + 1, part)

    def product(piece, kind, level, a, ranges, more=False):
        padded, _, _, wide, turned, _ = levels[level]
        values = (ref.coarse_shifted if level else ref.fine_shifted) if kind == GRAD else wide
        span = padded.shape[1]
        out = buffer(piece, 0, kind)
        left = [turned[:, (a + first) * span : (a + last) * span] for first, last in ranges]
        right = [values[first * span : last * span, :] for first, last in ranges]
        term = jnp.dot(
            jnp.concatenate(left, axis=1),
            jnp.concatenate(right, axis=0),
            preferred_element_type=F32,
        ).reshape(out.shape)
        out[...] = out[...] + term if more else term

    def send_first(piece, kind):
        first_copy(piece, kind, RECV if kind == GRAD else COME).start()

    def row_copy(stage):
        return pltpu.make_async_remote_copy(
            src_ref=ref.row_sums.at[stage],
            dst_ref=ref.row_gather.at[stage],
            send_sem=ref.row_send.at[stage],
            recv_sem=ref.row_recv.at[stage],
            device_id=partners[stage],
            device_id_type=MESH,
        )

    head_copies = slide_copies(1, ref.row_sums.at[bits], ref.head_gather)

    def advance_rows(stage):
        row_copy(stage).wait()
        ref.row_sums[stage + 1] = ref.row_sums[stage] + ref.row_gather[stage]
        if stage + 1 < bits:
            row_copy(stage + 1).start()
        else:
            head_copies.start()
            ref.head_gather[slide] = ref.row_sums[bits]

    with jax.named_scope("inner_forms"):
        for a in range(3):
            product(3 + a, FORM, 0, a, [(1, height - 1)])

    for at, (padded, taps, out, wide, _, high) in enumerate(levels):
        with jax.named_scope("edge_wait"):

            @pl.when(me < tiles - 1)
            def _():
                down[at].wait_send()
                up[at].wait_recv()

            @pl.when(me > 0)
            def _():
                up[at].wait_send()
                down[at].wait_recv()

        with jax.named_scope("edge_conv"):
            span = padded.shape[1]
            for first, a in ((0, 0), (high - 1, 2)):
                here = slice(span) if first == 0 else slice(span, 2 * span)
                total = ref.begun[at][here] + conv_terms([first], 1, padded, taps, (a,))
                conv_finish(total, [first], span, out, wide, sums, 2 * at)

    ref.stat[...] = sums[0:4]
    near_stat, stat_copies = near_first(1, ref.stat, ref.stat_gather)
    near_stat.start()
    ref.stat_gather[me] = ref.stat[...]
    stat_copies.start()
    counts.wait()
    ref.slide_count[...] = ordered_sum(ref.count_gather, tiles)
    total_copies = slide_copies(0, ref.slide_count, ref.total_gather)
    total_copies.start()
    ref.total_gather[slide] = ref.slide_count[...]

    for padded, _, _, _, turned, high in levels:
        turn(padded, turned, 0)
        turn(padded, turned, high + 1)

    def pair_of(gather, tile):
        return gather[tile] + gather[tile + 1 - 2 * lax.rem(tile, 2)]

    def near_centres(tile):
        pair = pair_of(ref.stat_gather, tile)
        return [
            pair[2 * at : 2 * at + 1] / (numbers[at] * 2 / tiles / (channels // GROUPS))
            for at in range(2)
        ]

    def forms_came(pieces):
        for piece in pieces:
            first_copy(piece, FORM, COME).wait_recv()

    def send_forms(pieces):
        for piece in pieces:
            form_copy(piece).start()

    def form_product(piece):
        if piece < 3:
            product(piece, FORM, 1, piece, [(0, height // 2)])
        else:
            product(piece, FORM, 0, piece - 3, [(0, 1), (height - 1, height)], more=True)

    with jax.named_scope("form_products"):
        for pair in ((0, 1), (2, 3)):
            for piece in pair:
                form_product(piece)
            for piece in pair:
                send_first(piece, FORM)
        near_stat.wait()
        centres = near_centres(me)
        form_product(4)
        send_first(4, FORM)
        forms_came(range(2))
        form_product(5)
        for piece in range(2):
            centre_forms(piece, centres[1])
        send_first(5, FORM)
        send_forms(range(2))
        for piece in range(2, EARLY):
            forms_came([piece])
            centre_forms(piece, centres[1 - piece // 3])
            send_forms([piece])

    scope = jax.named_scope("stat_wait")
    scope.__enter__()
    stat_copies.wait()
    total_copies.wait()
    total = ordered_sum(ref.total_gather, slides)
    count = total[0:1, 0:1]
    scope.__exit__(None, None, None)
    group_sums = group_sums_of(ordered_sum(ref.stat_gather, tiles), channels)

    def terms_of(at, number):
        mean = group_sums[at : at + 1] / number
        variance = group_sums[at + 1 : at + 2] / number - mean * mean
        return mean, lax.rsqrt(variance + EPSILON)

    fine_mean, fine_scale = terms_of(0, numbers[0])
    coarse_mean, coarse_scale = terms_of(2, numbers[1])

    square = (classes, classes)
    offset = jnp.sum(
        jnp.where(
            lanes_of(square) == lanes_of(square, 0),
            jnp.broadcast_to(ref.class_offset[...], square),
            0.0,
        ),
        axis=1,
        keepdims=True,
    )
    rows[...] = jnp.zeros_like(rows)

    forms_came(range(EARLY, PIECES))
    scope = jax.named_scope("head")
    scope.__enter__()
    for piece in range(EARLY, PIECES):
        centre_forms(piece, centres[0])

    for step in range(height // 2):
        widen, fold = ref.widen.at[step], ref.fold.at[step]
        fine_at = pl.ds(step * size, size)
        coarse_at = pl.ds(step * half, half)
        fine_normed = (fine_conv[fine_at, :] - fine_mean) * fine_scale
        fine_pre = fine_normed * fine_gain + fine_offset
        coarse_normed = (coarse_conv[coarse_at, :] - coarse_mean) * coarse_scale
        coarse_pre = coarse_normed * coarse_gain + coarse_offset
        coarse_act = jnp.maximum(coarse_pre, 0.0)
        widen[pl.ds(0, half, stride=2), :] = coarse_act
        widen[pl.ds(1, half, stride=2), :] = coarse_act
        upsampled = widen[...]
        merged = (
            jnp.maximum(fine_pre, 0.0) + jnp.concatenate([upsampled, upsampled], axis=0)
        ).astype(BF16)
        logits = (
            lax.dot_general(
                class_kernel[...], merged, (((1,), (1,)), ((), ())), preferred_element_type=F32
            )
            + offset
        )
        label = jnp.concatenate(
            [labels[pl.ds(2 * step, 1), :], labels[pl.ds(2 * step + 1, 1), :]], axis=1
        )
        onehot = (lanes_of((classes, size), 0) == label).astype(F32)
        tissue = (label >= 0).astype(F32)
        top = jnp.max(logits, axis=0, keepdims=True)
        lse = top + jnp.log(jnp.sum(jnp.exp(logits - top), axis=0, keepdims=True))
        picked = jnp.sum(onehot * logits, axis=0, keepdims=True)
        loss = jnp.sum((lse - picked) * tissue, axis=1, keepdims=True)
        dlogits = ((jnp.exp(logits - lse) - onehot) * tissue / count).astype(BF16)
        dmerged = lax.dot_general(
            dlogits, class_kernel[...], (((0,), (0,)), ((), ())), preferred_element_type=F32
        )
        fine_d = jnp.where(fine_pre > 0, dmerged, 0.0)
        ref.fine_shifted[fine_at, :] = shifts_of(fine_d, width)
        fold[...] = dmerged[:width] + dmerged[width:]
        blocks = fold[pl.ds(0, half, stride=2), :] + fold[pl.ds(1, half, stride=2), :]
        coarse_d = jnp.where(coarse_pre > 0, blocks, 0.0)
        ref.coarse_shifted[coarse_at, :] = shifts_of(coarse_d, half)
        rows[0:1] += jnp.sum(fine_d * fine_normed, axis=0, keepdims=True)
        rows[1:2] += jnp.sum(fine_d, axis=0, keepdims=True)
        rows[2:3] += jnp.sum(coarse_d * coarse_normed, axis=0, keepdims=True)
        rows[3:4] += jnp.sum(coarse_d, axis=0, keepdims=True)
        rows[4 : 4 + classes] += jnp.dot(dlogits, merged, preferred_element_type=F32)
        rows[4 + classes : 5 + classes] += jnp.broadcast_to(loss, (1, channels))

    scope.__exit__(None, None, None)
    gains = jnp.concatenate([fine_gain, fine_gain, coarse_gain, coarse_gain], axis=0)
    ref.back[...] = rows[0:4] * gains
    near_copy, back_copies = near_first(2, ref.back, ref.back_gather)
    near_copy.start()
    back_copies.start()
    ref.back_gather[me] = ref.back[...]
    ref.row_sums[0] = rows[...]
    send_forms(range(EARLY, PIECES))
    row_copy(0).start()
    stats = ((fine_mean, fine_scale), (coarse_mean, coarse_scale))

    def near_means(tile):
        pair = pair_of(ref.back_gather, tile)
        sums_here = group_sums_of(pair, channels)
        return [
            sums_here[2 * at + 1 : 2 * at + 2] / (numbers[at] * 2 / tiles) for at in range(2)
        ]

    def grad_product(piece):
        level = 1 - piece // 3
        product(piece, GRAD, level, piece % 3, [(0, (height, height // 2)[level])])

    def grads_came(pieces):
        for piece in pieces:
            first_copy(piece, GRAD, RECV).wait_recv()

    def centre(pieces):
        for piece in pieces:
            centre_grads(piece, *((coarse_gain, near[1]) if piece < 3 else (fine_gain, near[0])))

    def send(pieces):
        for piece in pieces:
            stage_copy(piece, 1).start()

    with jax.named_scope("grads_a"):
        for piece in range(4):
            grad_product(piece)
            send_first(piece, GRAD)
    with jax.named_scope("grads_wait"):
        near_copy.wait()
        near = near_means(me)
        for piece in range(3):
            grads_came([piece])
            centre([piece])
            send([piece])
        advance_rows(0)
    with jax.named_scope("grads_c"):
        grad_product(4)
        send_first(4, GRAD)
        grads_came([3])
    with jax.named_scope("grads_d"):
        grad_product(5)
        centre([3])
        send_first(5, GRAD)
        send([3])
    with jax.named_scope("close_a"):
        for piece in range(2):
            close_forms(piece)
        grads_came([4])
        centre([4])
        send([4])
        close_forms(2)
        grads_came([5])
        centre([5])
        send([5])
    with jax.named_scope("close_b"):
        for piece in range(3, PIECES):
            close_forms(piece)
    advance_rows(1)
    with jax.named_scope("back_wait"):
        back_copies.wait()
    back = group_sums_of(ordered_sum(ref.back_gather, tiles), channels)
    peers = {
        bit: (near_means(partners[bit]["tile"]), near_centres(partners[bit]["tile"]))
        for bit in {plan[1][0] for plan in plans}
    }

    def factors_of(piece):
        at = 1 - piece // 3
        mean, scale = stats[at]
        first = back[2 * at + 1 : 2 * at + 2] / numbers[at]
        second = back[2 * at : 2 * at + 1] / numbers[at] * scale * scale
        peer_near, peer_centres = peers[plans[piece][1][0]]
        return (
            scale,
            -second,
            scale * (near[at] - first) - second * (centres[at] - mean),
            scale * (peer_near[at] - first) - second * (peer_centres[at] - mean),
        )

    with jax.named_scope("join"):
        for piece in range(3):
            join(piece, factors_of(piece))
    with jax.named_scope("join_fine"):
        for piece in range(3, PIECES):
            join(piece, factors_of(piece))
    advance_rows(2)
    for stage in range(2, bits):
        with jax.named_scope("stage%d" % stage):
            for piece in range(PIECES):
                advance(piece, stage)
                if stage > 2 and piece == 2:
                    advance_rows(stage)
    scope = jax.named_scope("finish")
    scope.__enter__()
    sent = [(ref.parts[SEND, 0, stage], ref.stage_send.at[stage - 1]) for stage in range(1, bits)]
    sent += [(ref.parts[FSEND, 0, 1], ref.form_send.at[0])]
    sent += [(ref.parts[RECV, 0, 0], ref.first_send.at[0])]
    sent += [(ref.parts[COME, 0, 0], ref.first_send.at[1])]
    sent += [(final.at[pl.ds(0, slides - 1)], ref.piece_send.at[0])]
    for buffers, sem in sent:
        pltpu.make_async_copy(buffers, buffers, sem).wait()
    head_copies.wait()
    row_total = ordered_sum(ref.head_gather, slides)
    ref.heads[...] = row_total
    ref.heads[4 + classes : 5 + classes] = row_total[4 + classes : 5 + classes] / count
    for piece in range(PIECES):
        for copy in piece_copies(piece):
            copy.wait_recv()
        level, a = spans[piece][0] // across // 3, spans[piece][0] // across % 3
        whole = ordered_sum(final.at[:, :, pl.ds(*spans[piece])], slides)
        for b in range(3):
            ref.grads[pl.ds(6 * a + 2 * b + level, whole.shape[0], stride=18), :] = whole[
                :, b * channels : (b + 1) * channels
            ]
    scope.__exit__(None, None, None)


def per_device(
    fine_level,
    coarse_level,
    fine_kernel,
    coarse_kernel,
    fine_gain,
    fine_offset,
    coarse_gain,
    coarse_offset,
    class_kernel,
    class_offset,
    tissue_labels,
):
    tiles, slides = lax.axis_size("tile"), lax.axis_size("slide")
    bits = tiles.bit_length() - 1
    in_channels, _, channels = fine_kernel.shape
    classes = class_kernel.shape[0]
    fine, coarse, labels = fine_level[0], coarse_level[0], tissue_labels[0]
    height, width = fine.shape[0], fine.shape[1]
    fine_number = height * tiles * width * (channels // GROUPS)
    numbers = (float(fine_number), float(fine_number // 4))
    pixels, half = height * width, width // 2
    slide_ends = max(slides - 1, 1)
    chunk = in_channels // tiles
    row_count = -(-(5 + classes) // 8) * 8

    inputs = dict(
        fine=fine,
        fine_taps=fine_kernel.transpose(1, 0, 2),
        labels=labels,
        coarse=coarse,
        coarse_taps=coarse_kernel.transpose(1, 0, 2),
        fine_gain=fine_gain[None, :],
        fine_offset=fine_offset[None, :],
        coarse_gain=coarse_gain[None, :],
        coarse_offset=coarse_offset[None, :],
        class_kernel=class_kernel,
        class_offset=class_offset[None, :],
    )
    outputs = dict(
        heads=pltpu.VMEM((row_count, channels), F32),
        grads=pltpu.VMEM((chunk * 18, channels), F32),
    )
    line, lines = (1, channels), (4, channels)
    scratch = {
        name: pltpu.VMEM(value.shape, value.dtype)
        for name, value in inputs.items()
        if name not in ("fine", "coarse")
    }
    scratch |= dict(
        final=pltpu.VMEM((slides, chunk, 18 * channels), F32),
        head_gather=pltpu.VMEM((slides, row_count, channels), F32),
        load_sem=dma_sems(len(inputs)),
        fine_pad=pltpu.VMEM((height + 2, width, in_channels), BF16),
        coarse_pad=pltpu.VMEM((height // 2 + 2, half, in_channels), BF16),
        fine_conv=pltpu.VMEM((pixels, channels), F32),
        coarse_conv=pltpu.VMEM((pixels // 4, channels), F32),
        fine_begun=pltpu.VMEM((2 * width, 3 * channels), F32),
        coarse_begun=pltpu.VMEM((2 * half, 3 * channels), F32),
        fine_wide=pltpu.VMEM((pixels, 4 * channels), BF16),
        coarse_wide=pltpu.VMEM((pixels // 4, 4 * channels), BF16),
        fine_turned=pltpu.VMEM((in_channels, (height + 2) * width), BF16),
        coarse_turned=pltpu.VMEM((in_channels, (height // 2 + 2) * half), BF16),
        fine_shifted=pltpu.VMEM((pixels, 3 * channels), BF16),
        coarse_shifted=pltpu.VMEM((pixels // 4, 3 * channels), BF16),
        widen=pltpu.VMEM((height // 2, width, channels), F32),
        fold=pltpu.VMEM((height // 2, width, channels), F32),
        sums=pltpu.VMEM((8, channels), F32),
        rows=pltpu.VMEM((row_count, channels), F32),
        row_sums=pltpu.VMEM((bits + 1, row_count, channels), F32),
        row_gather=pltpu.VMEM((bits, row_count, channels), F32),
        row_send=dma_sems(bits),
        row_recv=dma_sems(bits),
        count=pltpu.VMEM(line, F32),
        stat=pltpu.VMEM(lines, F32),
        back=pltpu.VMEM(lines, F32),
        slide_count=pltpu.VMEM(line, F32),
        count_gather=pltpu.VMEM((tiles,) + line, F32),
        stat_gather=pltpu.VMEM((tiles,) + lines, F32),
        back_gather=pltpu.VMEM((tiles,) + lines, F32),
        total_gather=pltpu.VMEM((slides,) + line, F32),
        edge_send=dma_sems(2, 2),
        edge_recv=dma_sems(2, 2),
        near_send=dma_sems(2),
        near_recv=dma_sems(2),
        form_send=dma_sems(1),
        form_recv=dma_sems(PIECES),
        tile_send=dma_sems(3),
        tile_recv=dma_sems(3),
        slide_send=dma_sems(2),
        slide_recv=dma_sems(2),
        piece_send=dma_sems(1),
        piece_recv=dma_sems(PIECES, slide_ends),
        first_send=dma_sems(2),
        first_recv=dma_sems(2, PIECES),
        stage_send=dma_sems(bits - 1),
        stage_recv=dma_sems(PIECES, bits - 1),
    )
    parts = {}
    span = 3 * channels
    for piece in range(PIECES):
        parts[GRAD, piece, 0] = pltpu.VMEM((2,) * bits + (chunk, span), F32)
        plan = stage_plan(bits, order_of(bits, (piece + 1) % 2))
        forms = (chunk, 4 * channels)
        parts[FORM, piece, 0] = pltpu.VMEM((2,) * bits + forms, F32)
        parts[WINDOW, piece, 0] = pltpu.VMEM((2,) * (bits - 1) + (chunk, span), F32)
        parts[COME, 0, 0] = pltpu.VMEM((PIECES,) + (2,) * (bits - 1) + forms, F32)
        for stage, (_, _, left) in enumerate(plan):
            below = (2,) * left + (chunk, span)
            if stage:
                parts[RECV, piece, stage] = pltpu.VMEM(below, BF16)
            else:
                parts[RECV, 0, 0] = pltpu.VMEM((PIECES,) + below, F32)
            if stage == 1:
                wider = below[:-1] + (4 * channels,)
                parts[FSEND, 0, 1] = pltpu.VMEM((PIECES,) + wider, BF16)
                parts[FRECV, piece, 1] = pltpu.VMEM(wider, BF16)
                parts[FKEPT, piece, 1] = pltpu.VMEM(below, F32)
                parts[OTHER, piece, 1] = pltpu.VMEM(below, F32)
            if stage:
                parts[SEND, 0, stage] = pltpu.VMEM((PIECES,) + below, BF16)
                parts[KEPT, piece, stage] = pltpu.VMEM(below, F32)
    names = ["far_" + name for name in inputs] + list(outputs) + list(scratch)
    results = call(
        functools.partial(step_kernel, tiles, slides, bits, numbers, names, list(parts)),
        tuple(outputs.values()),
        list(scratch.values()) + list(parts.values()),
        tuple(inputs.values()),
    )
    loss, head, grads = store(*results, classes)
    return (loss[0, 0], head, grads.reshape(chunk, 9, 2, channels).transpose(0, 2, 1, 3))


def solution(mesh):
    return jax.shard_map(
        per_device,
        mesh=mesh,
        in_specs=(
            P("slide", "tile", None, None),
            P("slide", "tile", None, None),
            P(),
            P(),
            P(),
            P(),
            P(),
            P(),
            P(),
            P(),
            P("slide", "tile", None),
        ),
        out_specs=(P(), P(), P("tile", None, None, None)),
        check_vma=False,
    )
```

```python
import functools
import types

import jax
import jax.numpy as jnp
from jax import lax
from jax.experimental import pallas as pl
from jax.experimental.pallas import tpu as pltpu
from jax.sharding import PartitionSpec as P

GROUPS = 32
EPSILON = 1e-05
F32 = jnp.float32
BF16 = jnp.bfloat16
MESH = pl.DeviceIdType.MESH
VMEM = pl.BlockSpec(memory_space=pltpu.VMEM)
ANY = pl.BlockSpec(memory_space=pl.ANY)
LIMIT = 60 * 1024 * 1024
HIGH = lax.Precision.HIGHEST


def call(body, out_shape, scratch, args):
    return pl.pallas_call(
        body,
        out_shape=out_shape,
        in_specs=[ANY] * len(args),
        out_specs=jax.tree.map(lambda _: VMEM, out_shape),
        scratch_shapes=scratch,
        compiler_params=pltpu.CompilerParams(
            vmem_limit_bytes=LIMIT, collective_id=0, has_side_effects=True
        ),
    )(*args)


def store_kernel(classes, rows, grads, loss_out, head_out, grads_out, loss, sems):
    copies = [
        pltpu.make_async_copy(source, target, sems.at[at])
        for at, (source, target) in enumerate(
            ((grads, grads_out), (rows.at[pl.ds(0, 4 + classes)], head_out), (loss, loss_out))
        )
    ]
    for copy in copies[:2]:
        copy.start()
    loss[...] = rows[4 + classes : 5 + classes, 0:1]
    copies[2].start()
    for copy in copies:
        copy.wait()


def store(rows, grads, classes):
    return pl.pallas_call(
        functools.partial(store_kernel, classes),
        out_shape=(
            shape_of((1, 1)),
            shape_of((4 + classes, rows.shape[1])),
            shape_of(grads.shape),
        ),
        in_specs=[VMEM, VMEM],
        out_specs=(ANY, ANY, ANY),
        scratch_shapes=[pltpu.VMEM((1, 1), F32), dma_sems(3)],
    )(*(pltpu.with_memory_space_constraint(value, pltpu.VMEM) for value in (rows, grads)))


def shape_of(dims, dtype=F32):
    return jax.ShapeDtypeStruct(dims, dtype)


def greet(peers, meanwhile):
    barrier = pltpu.get_barrier_semaphore()
    for peer in peers:
        pl.semaphore_signal(barrier, inc=1, device_id=peer, device_id_type=MESH)
    meanwhile()
    pl.semaphore_wait(barrier, len(peers))


def others_of(axis, size):
    me = lax.axis_index(axis)
    return [lax.rem(me + d, size) for d in range(1, size)]


def ring_peers(axis, size):
    return [{axis: peer} for peer in others_of(axis, size)]


class Spread:
    def __init__(self, axis, peers, source, gather, send_sem, recv_sem):
        me = lax.axis_index(axis)
        self.copies = [
            pltpu.make_async_remote_copy(
                src_ref=source,
                dst_ref=gather.at[me],
                send_sem=send_sem,
                recv_sem=recv_sem,
                device_id={axis: peer},
                device_id_type=MESH,
            )
            for peer in peers
        ]
        others = gather.at[pl.ds(0, len(self.copies))]
        self.ends = [pltpu.make_async_copy(others, others, sem) for sem in (send_sem, recv_sem)]

    def start(self):
        for copy in self.copies:
            copy.start()

    def wait(self):
        if self.copies:
            for end in self.ends:
                end.wait()


def ordered_sum(gather, size):
    total = gather[0]
    for index in range(1, size):
        total = total + gather[index]
    return total


def dma_sems(*dims):
    return pltpu.SemaphoreType.DMA(dims)


def column_of(shape, width):
    return lax.rem(lax.broadcasted_iota(jnp.int32, shape, 0), width)


def from_left(values, width):
    moved = pltpu.roll(values, 1, axis=0)
    return jnp.where(column_of(values.shape, width) == 0, 0.0, moved)


def from_right(values, width):
    moved = pltpu.roll(values, values.shape[0] - 1, axis=0)
    return jnp.where(column_of(values.shape, width) == width - 1, 0.0, moved)


def stage_plan(bits, order):
    left = list(reversed(range(bits)))
    plan = []
    for bit in order:
        place = left.index(bit)
        left = [other for other in left if other != bit]
        plan.append((bit, place, len(left)))
    return plan


def at_bits(places, count):
    index = [slice(None)] * count
    for place, value in places:
        index[place] = value
    return tuple(index)


def order_of(bits, turn):
    order = list(range(bits))
    if turn and bits > 2:
        order[1], order[2] = order[2], order[1]
    return order


def lanes_of(shape, dim=1):
    return lax.broadcasted_iota(jnp.int32, shape, dim)


def group_sums_of(rows, channels):
    step = 1
    while step < channels // GROUPS:
        after, before = pltpu.roll(rows, channels - step, axis=1), pltpu.roll(rows, step, axis=1)
        rows = rows + jnp.where(lanes_of(rows.shape) // step % 2 == 0, after, before)
        step *= 2
    return rows


PACK = 2
PIECES = 6
EARLY = 6
GRAD, SEND, RECV, KEPT, FORM, COME, WINDOW, FSEND, FRECV, FKEPT, OTHER = range(11)


def shifts_of(values, width):
    return jnp.concatenate(
        [from_right(values, width), values, from_left(values, width)], axis=1
    ).astype(BF16)


def ones_of(rows, channels, width):
    column = column_of((rows, channels), width)
    lane = lanes_of((rows, channels))
    side = lax.rem(lane, 3)
    outside = ((side == 0) & (column == width - 1)) | ((side == 2) & (column == 0)) | (lane > 5)
    return jnp.where(outside, 0.0, 1.0).astype(BF16)


def split_sums(values):
    high = values.astype(BF16).astype(F32)
    return jnp.where(lanes_of(values.shape, values.ndim - 1) < 3, high, values - high)


def spread_sums(values, channels):
    shape = values.shape[:-1] + (channels,)
    return jnp.concatenate(
        [jnp.broadcast_to(values[..., b : b + 1], shape) for b in range(3)], axis=-1
    )


def three(row):
    return jnp.concatenate([row] * 3, axis=1)


def conv_terms(firsts, count, padded, taps, terms):
    width, depth = padded.shape[1], padded.shape[2]
    total = None
    for a in terms:
        block = jnp.concatenate(
            [padded[pl.ds(first + a, count)].reshape(count * width, depth) for first in firsts],
            axis=0,
        )
        side = jnp.concatenate([taps[3 * a + b] for b in range(3)], axis=1)
        term = jnp.dot(block, side, preferred_element_type=F32)
        total = term if total is None else total + term
    return total


def conv_finish(total, firsts, width, out, wide, sums, at):
    channels = out.shape[1]
    span = total.shape[0] // len(firsts)
    value = (
        from_left(total[:, :channels], width)
        + total[:, channels : 2 * channels]
        + from_right(total[:, 2 * channels :], width)
    )
    for index, first in enumerate(firsts):
        part = value[index * span : (index + 1) * span]
        out[pl.ds(first * width, span), :] = part
        wide[pl.ds(first * width, span), : 3 * channels] = shifts_of(part, width)
    sums[at : at + 1] += jnp.sum(value, axis=0, keepdims=True)
    sums[at + 1 : at + 2] += jnp.sum(value * value, axis=0, keepdims=True)


def step_kernel(tiles, slides, bits, numbers, names, keys, *refs):
    ref = types.SimpleNamespace(**dict(zip(names, refs)))
    ref.parts = dict(zip(keys, refs[len(names) :]))
    ref.begun = (ref.fine_begun, ref.coarse_begun)
    fine, coarse, labels = ref.far_fine, ref.far_coarse, ref.labels
    fine_pad, coarse_pad = ref.fine_pad, ref.coarse_pad
    fine_conv, coarse_conv = ref.fine_conv, ref.coarse_conv
    sums, rows, class_kernel = ref.sums, ref.rows, ref.class_kernel
    me, slide = lax.axis_index("tile"), lax.axis_index("slide")
    height, width, _ = fine.shape
    channels = fine_conv.shape[1]
    classes = class_kernel.shape[0]
    targets = dict(fine=fine_pad.at[pl.ds(1, height)], coarse=coarse_pad.at[pl.ds(1, height // 2)])
    loads = {}
    for at, name in enumerate(names):
        if name.startswith("far_"):
            name = name[4:]
            loads[name] = pltpu.make_async_copy(
                refs[at], targets.get(name, getattr(ref, name, None)), ref.load_sem.at[at]
            )

    def start_loads():
        for copy in loads.values():
            copy.start()

    def prepare():
        for name, copy in loads.items():
            if not name.startswith(("fine", "coarse")) or name.endswith(("gain", "offset")):
                copy.wait()
        tissue_here = (labels[...] >= 0).astype(F32)
        ref.count[...] = jnp.broadcast_to(
            jnp.sum(tissue_here, axis=(0, 1), keepdims=True), ref.count.shape
        )
        sums[...] = jnp.zeros_like(sums)

    with jax.named_scope("greet"):
        greet(ring_peers("tile", tiles) + ring_peers("slide", slides), start_loads)

    def edge_copies(peer, down):
        return [
            pltpu.make_async_remote_copy(
                src_ref=source.at[source.shape[0] - 1 if down else 0],
                dst_ref=target.at[0 if down else target.shape[0] - 1],
                send_sem=ref.edge_send.at[int(down), at],
                recv_sem=ref.edge_recv.at[int(down), at],
                device_id={"tile": peer},
                device_id_type=MESH,
            )
            for at, (source, target) in enumerate(((fine, fine_pad), (coarse, coarse_pad)))
        ]

    down = edge_copies(lax.rem(me + 1, tiles), True)
    up = edge_copies(lax.rem(me + tiles - 1, tiles), False)

    @pl.when(me < tiles - 1)
    def _():
        for copy in down:
            copy.start()

    @pl.when(me > 0)
    def _():
        for copy in up:
            copy.start()

    with jax.named_scope("prepare"):
        prepare()
    fine_gain, fine_offset = ref.fine_gain[...], ref.fine_offset[...]
    coarse_gain, coarse_offset = ref.coarse_gain[...], ref.coarse_offset[...]

    def tile_copies(at, source, gather):
        return Spread(
            "tile", others_of("tile", tiles), source, gather, ref.tile_send.at[at], ref.tile_recv.at[at]
        )

    def near_first(at, source, gather):
        beside = me + 1 - 2 * lax.rem(me, 2)
        near_copy = pltpu.make_async_remote_copy(
            src_ref=source,
            dst_ref=gather.at[me],
            send_sem=ref.near_send.at[at - 1],
            recv_sem=ref.near_recv.at[at - 1],
            device_id={"tile": beside},
            device_id_type=MESH,
        )
        signs = [1 - 2 * lax.rem(me // 2**bit, 2) for bit in range(bits)]
        others = [
            me + sum(signs[bit] * 2**bit for bit in range(bits) if d // 2**bit % 2)
            for d in range(tiles - 1, 1, -1)
        ]
        return near_copy, Spread(
            "tile", others, source, gather, ref.tile_send.at[at], ref.tile_recv.at[at]
        )

    def slide_copies(at, source, gather):
        return Spread(
            "slide", others_of("slide", slides), source, gather, ref.slide_send.at[at], ref.slide_recv.at[at]
        )

    counts = tile_copies(0, ref.count, ref.count_gather)
    counts.start()
    ref.count_gather[me] = ref.count[...]

    @pl.when(me == 0)
    def _():
        for padded in (fine_pad, coarse_pad):
            padded[0] = jnp.zeros(padded.shape[1:], BF16)

    @pl.when(me == tiles - 1)
    def _():
        for padded in (fine_pad, coarse_pad):
            padded[padded.shape[0] - 1] = jnp.zeros(padded.shape[1:], BF16)

    size, half = 2 * width, width // 2
    levels = (
        (fine_pad, ref.fine_taps, fine_conv, ref.fine_wide, ref.fine_turned, height),
        (coarse_pad, ref.coarse_taps, coarse_conv, ref.coarse_wide, ref.coarse_turned, height // 2),
    )

    def turn(padded, turned, row):
        span = padded.shape[1]
        turned[:, row * span : (row + 1) * span] = padded[row].T

    with jax.named_scope("inner_conv"):
        for at, (padded, taps, out, wide, _, high) in enumerate(levels):
            with jax.named_scope("load_wait"):
                for name in (("fine", "fine_taps"), ("coarse", "coarse_taps"))[at]:
                    loads[name].wait()

            for step in range((high - 2) // PACK):
                total = conv_terms([1 + PACK * step], PACK, padded, taps, range(3))
                conv_finish(total, [1 + PACK * step], padded.shape[1], out, wide, sums, 2 * at)
            span = padded.shape[1]
            ref.begun[at][:span] = conv_terms([0], 1, padded, taps, (1, 2))
            ref.begun[at][span:] = conv_terms([high - 1], 1, padded, taps, (0, 1))

    with jax.named_scope("inner_turn"):
        for padded, _, _, wide, turned, high in levels:
            for row in range(1, high + 1):
                turn(padded, turned, row)
            span = padded.shape[1]

            @pl.loop(0, high)
            def _(row):
                here = pl.ds(pl.multiple_of(row * span, span), span)
                wide[here, 3 * channels :] = ones_of(span, channels, span)

    mine = [lax.rem(me // (2**bit), 2) for bit in range(bits)]
    partners = [{"tile": me + (1 - 2 * mine[bit]) * (2**bit)} for bit in range(bits)]
    plans = [stage_plan(bits, order_of(bits, (piece + 1) % 2)) for piece in range(PIECES)]
    final = ref.final
    across = 3 * channels
    spans = [((piece + 3) % PIECES * across, across) for piece in range(PIECES)]

    def buffer(piece, stage, kind):
        if kind in (SEND, FSEND, COME) or (kind == RECV and stage == 0):
            return ref.parts[kind, 0, stage].at[piece]
        return ref.parts[kind, piece, stage]

    def stage_copy(piece, stage):
        bit, place, left = plans[piece][stage]
        return pltpu.make_async_remote_copy(
            src_ref=buffer(piece, stage, SEND),
            dst_ref=buffer(piece, stage, RECV),
            send_sem=ref.stage_send.at[stage - 1],
            recv_sem=ref.stage_recv.at[piece, stage - 1],
            device_id=partners[bit],
            device_id_type=MESH,
        )

    def piece_copies(piece):
        lanes = pl.ds(*spans[piece])
        return [
            pltpu.make_async_remote_copy(
                src_ref=final.at[slide, :, lanes],
                dst_ref=final.at[slide, :, lanes],
                send_sem=ref.piece_send.at[0],
                recv_sem=ref.piece_recv.at[piece, d - 1],
                device_id={"slide": lax.rem(slide + d, slides)},
                device_id_type=MESH,
            )
            for d in range(1, slides)
        ]

    def first_copy(piece, kind, target):
        bit, place, left = plans[piece][0]
        return pltpu.make_async_remote_copy(
            src_ref=buffer(piece, 0, kind).at[at_bits([(place, 1 - mine[bit])], left + 1)],
            dst_ref=buffer(piece, 0, target),
            send_sem=ref.first_send.at[int(kind == FORM)],
            recv_sem=ref.first_recv.at[int(kind == FORM), piece],
            device_id=partners[bit],
            device_id_type=MESH,
        )

    def fill(piece, stage, part):
        bit, spot, left = plans[piece][stage]
        buffer(piece, stage, SEND)[...] = part(at_bits([(spot, 1 - mine[bit])], left + 1)).astype(BF16)
        buffer(piece, stage, KEPT)[...] = part(at_bits([(spot, mine[bit])], left + 1))

    def pass_on(piece, stage, part):
        fill(piece, stage, part)
        stage_copy(piece, stage).start()

    def own_of(piece, kind):
        bit, place, left = plans[piece][0]
        return buffer(piece, 0, kind).at[at_bits([(place, mine[bit])], left + 1)]

    def halves(piece, stage):
        bit, spot, left = plans[piece][stage]
        return [at_bits([(spot, value)], left + 1) for value in (1 - mine[bit], mine[bit])]

    def form_copy(piece):
        return pltpu.make_async_remote_copy(
            src_ref=buffer(piece, 1, FSEND),
            dst_ref=buffer(piece, 1, FRECV),
            send_sem=ref.form_send.at[0],
            recv_sem=ref.form_recv.at[piece],
            device_id=partners[plans[piece][1][0]],
            device_id_type=MESH,
        )

    def centre_forms(piece, mean):
        away, here = halves(piece, 1)
        own, came = own_of(piece, FORM), buffer(piece, 0, COME)
        windows, send = buffer(piece, 0, WINDOW), buffer(piece, 1, FSEND)

        def centred(at):
            forms = own[at] + came[at]
            window = spread_sums(forms[..., across:], channels)
            windows[at] = window
            return forms[..., :across] - three(mean) * window, forms[..., across:]

        values, ends = centred(away)
        send[..., :across] = values.astype(BF16)
        send[..., across:] = split_sums(ends).astype(BF16)
        buffer(piece, 1, FKEPT)[...] = centred(here)[0]

    def close_forms(piece):
        form_copy(piece).wait_recv()
        kept, came = buffer(piece, 1, FKEPT), buffer(piece, 1, FRECV)
        kept[...] = kept[...] + came[..., :across].astype(F32)
        sums_came = came[..., across:].astype(F32)
        ends = sums_came[..., :3] + sums_came[..., 3:6]
        buffer(piece, 1, OTHER)[...] = spread_sums(ends, channels)

    def centre_grads(piece, gain, near):
        own, came = own_of(piece, GRAD), buffer(piece, 0, RECV)
        windows = buffer(piece, 0, WINDOW)
        wide_gain, wide_near = three(gain), three(near)

        def part(at):
            return wide_gain * (own[at] + came[at]) - wide_near * windows[at]

        fill(piece, 1, part)

    def join(piece, factors):
        stage_copy(piece, 1).wait_recv()
        kept, came = buffer(piece, 1, KEPT), buffer(piece, 1, RECV)
        forms, other = buffer(piece, 1, FKEPT), buffer(piece, 1, OTHER)
        windows = buffer(piece, 0, WINDOW).at[halves(piece, 1)[1]]
        wide = [three(factor) for factor in factors]

        def part(at):
            return (
                wide[0] * (kept[at] + came[at].astype(F32))
                + wide[1] * forms[at]
                + wide[2] * windows[at]
                + wide[3] * other[at]
            )

        pass_on(piece, 2, part)

    def advance(piece, stage):
        stage_copy(piece, stage).wait_recv()
        kept, came = buffer(piece, stage, KEPT), buffer(piece, stage, RECV)

        def part(chosen):
            return kept[chosen] + came[chosen].astype(F32)

        if stage == bits - 1:
            final[slide, :, pl.ds(*spans[piece])] = part(...)
            for copy in piece_copies(piece):
                copy.start()
        else:
            pass_on(piece, stage + 1, part)

    def product(piece, kind, level, a, ranges, more=False):
        padded, _, _, wide, turned, _ = levels[level]
        values = (ref.coarse_shifted if level else ref.fine_shifted) if kind == GRAD else wide
        span = padded.shape[1]
        out = buffer(piece, 0, kind)
        left = [turned[:, (a + first) * span : (a + last) * span] for first, last in ranges]
        right = [values[first * span : last * span, :] for first, last in ranges]
        term = jnp.dot(
            jnp.concatenate(left, axis=1),
            jnp.concatenate(right, axis=0),
            preferred_element_type=F32,
        ).reshape(out.shape)
        out[...] = out[...] + term if more else term

    def send_first(piece, kind):
        first_copy(piece, kind, RECV if kind == GRAD else COME).start()

    def row_copy(stage):
        return pltpu.make_async_remote_copy(
            src_ref=ref.row_sums.at[stage],
            dst_ref=ref.row_gather.at[stage],
            send_sem=ref.row_send.at[stage],
            recv_sem=ref.row_recv.at[stage],
            device_id=partners[stage],
            device_id_type=MESH,
        )

    head_copies = slide_copies(1, ref.row_sums.at[bits], ref.head_gather)

    def advance_rows(stage):
        row_copy(stage).wait()
        ref.row_sums[stage + 1] = ref.row_sums[stage] + ref.row_gather[stage]
        if stage + 1 < bits:
            row_copy(stage + 1).start()
        else:
            head_copies.start()
            ref.head_gather[slide] = ref.row_sums[bits]

    with jax.named_scope("inner_forms"):
        for a in range(3):
            product(3 + a, FORM, 0, a, [(1, height - 1)])

    for at, (padded, taps, out, wide, _, high) in enumerate(levels):
        with jax.named_scope("edge_wait"):

            @pl.when(me < tiles - 1)
            def _():
                down[at].wait_send()
                up[at].wait_recv()

            @pl.when(me > 0)
            def _():
                up[at].wait_send()
                down[at].wait_recv()

        with jax.named_scope("edge_conv"):
            span = padded.shape[1]
            for first, a in ((0, 0), (high - 1, 2)):
                here = slice(span) if first == 0 else slice(span, 2 * span)
                total = ref.begun[at][here] + conv_terms([first], 1, padded, taps, (a,))
                conv_finish(total, [first], span, out, wide, sums, 2 * at)

    ref.stat[...] = sums[0:4]
    near_stat, stat_copies = near_first(1, ref.stat, ref.stat_gather)
    near_stat.start()
    ref.stat_gather[me] = ref.stat[...]
    stat_copies.start()
    counts.wait()
    ref.slide_count[...] = ordered_sum(ref.count_gather, tiles)
    total_copies = slide_copies(0, ref.slide_count, ref.total_gather)
    total_copies.start()
    ref.total_gather[slide] = ref.slide_count[...]

    for padded, _, _, _, turned, high in levels:
        turn(padded, turned, 0)
        turn(padded, turned, high + 1)

    def pair_of(gather, tile):
        return gather[tile] + gather[tile + 1 - 2 * lax.rem(tile, 2)]

    def near_centres(tile):
        pair = pair_of(ref.stat_gather, tile)
        return [
            pair[2 * at : 2 * at + 1] / (numbers[at] * 2 / tiles / (channels // GROUPS))
            for at in range(2)
        ]

    def forms_came(pieces):
        for piece in pieces:
            first_copy(piece, FORM, COME).wait_recv()

    def send_forms(pieces):
        for piece in pieces:
            form_copy(piece).start()

    def form_product(piece):
        if piece < 3:
            product(piece, FORM, 1, piece, [(0, height // 2)])
        else:
            product(piece, FORM, 0, piece - 3, [(0, 1), (height - 1, height)], more=True)

    with jax.named_scope("form_products"):
        for pair in ((0, 1), (2, 3)):
            for piece in pair:
                form_product(piece)
            for piece in pair:
                send_first(piece, FORM)
        near_stat.wait()
        centres = near_centres(me)
        form_product(4)
        send_first(4, FORM)
        forms_came(range(2))
        form_product(5)
        for piece in range(2):
            centre_forms(piece, centres[1])
        send_first(5, FORM)
        send_forms(range(2))
        for piece in range(2, EARLY):
            forms_came([piece])
            centre_forms(piece, centres[1 - piece // 3])
            send_forms([piece])

    scope = jax.named_scope("stat_wait")
    scope.__enter__()
    stat_copies.wait()
    total_copies.wait()
    total = ordered_sum(ref.total_gather, slides)
    count = total[0:1, 0:1]
    scope.__exit__(None, None, None)
    group_sums = group_sums_of(ordered_sum(ref.stat_gather, tiles), channels)

    def terms_of(at, number):
        mean = group_sums[at : at + 1] / number
        variance = group_sums[at + 1 : at + 2] / number - mean * mean
        return mean, lax.rsqrt(variance + EPSILON)

    fine_mean, fine_scale = terms_of(0, numbers[0])
    coarse_mean, coarse_scale = terms_of(2, numbers[1])

    square = (classes, classes)
    offset = jnp.sum(
        jnp.where(
            lanes_of(square) == lanes_of(square, 0),
            jnp.broadcast_to(ref.class_offset[...], square),
            0.0,
        ),
        axis=1,
        keepdims=True,
    )
    rows[...] = jnp.zeros_like(rows)

    forms_came(range(EARLY, PIECES))
    scope = jax.named_scope("head")
    scope.__enter__()
    for piece in range(EARLY, PIECES):
        centre_forms(piece, centres[0])

    for step in range(height // 2):
        widen, fold = ref.widen.at[step], ref.fold.at[step]
        fine_at = pl.ds(step * size, size)
        coarse_at = pl.ds(step * half, half)
        fine_normed = (fine_conv[fine_at, :] - fine_mean) * fine_scale
        fine_pre = fine_normed * fine_gain + fine_offset
        coarse_normed = (coarse_conv[coarse_at, :] - coarse_mean) * coarse_scale
        coarse_pre = coarse_normed * coarse_gain + coarse_offset
        coarse_act = jnp.maximum(coarse_pre, 0.0)
        widen[pl.ds(0, half, stride=2), :] = coarse_act
        widen[pl.ds(1, half, stride=2), :] = coarse_act
        upsampled = widen[...]
        merged = (
            jnp.maximum(fine_pre, 0.0) + jnp.concatenate([upsampled, upsampled], axis=0)
        ).astype(BF16)
        logits = (
            lax.dot_general(
                class_kernel[...], merged, (((1,), (1,)), ((), ())), preferred_element_type=F32
            )
            + offset
        )
        label = jnp.concatenate(
            [labels[pl.ds(2 * step, 1), :], labels[pl.ds(2 * step + 1, 1), :]], axis=1
        )
        onehot = (lanes_of((classes, size), 0) == label).astype(F32)
        tissue = (label >= 0).astype(F32)
        top = jnp.max(logits, axis=0, keepdims=True)
        lse = top + jnp.log(jnp.sum(jnp.exp(logits - top), axis=0, keepdims=True))
        picked = jnp.sum(onehot * logits, axis=0, keepdims=True)
        loss = jnp.sum((lse - picked) * tissue, axis=1, keepdims=True)
        dlogits = ((jnp.exp(logits - lse) - onehot) * tissue / count).astype(BF16)
        dmerged = lax.dot_general(
            dlogits, class_kernel[...], (((0,), (0,)), ((), ())), preferred_element_type=F32
        )
        fine_d = jnp.where(fine_pre > 0, dmerged, 0.0)
        ref.fine_shifted[fine_at, :] = shifts_of(fine_d, width)
        fold[...] = dmerged[:width] + dmerged[width:]
        blocks = fold[pl.ds(0, half, stride=2), :] + fold[pl.ds(1, half, stride=2), :]
        coarse_d = jnp.where(coarse_pre > 0, blocks, 0.0)
        ref.coarse_shifted[coarse_at, :] = shifts_of(coarse_d, half)
        rows[0:1] += jnp.sum(fine_d * fine_normed, axis=0, keepdims=True)
        rows[1:2] += jnp.sum(fine_d, axis=0, keepdims=True)
        rows[2:3] += jnp.sum(coarse_d * coarse_normed, axis=0, keepdims=True)
        rows[3:4] += jnp.sum(coarse_d, axis=0, keepdims=True)
        rows[4 : 4 + classes] += jnp.dot(dlogits, merged, preferred_element_type=F32)
        rows[4 + classes : 5 + classes] += jnp.broadcast_to(loss, (1, channels))

    scope.__exit__(None, None, None)
    gains = jnp.concatenate([fine_gain, fine_gain, coarse_gain, coarse_gain], axis=0)
    ref.back[...] = rows[0:4] * gains
    near_copy, back_copies = near_first(2, ref.back, ref.back_gather)
    near_copy.start()
    back_copies.start()
    ref.back_gather[me] = ref.back[...]
    ref.row_sums[0] = rows[...]
    send_forms(range(EARLY, PIECES))
    row_copy(0).start()
    stats = ((fine_mean, fine_scale), (coarse_mean, coarse_scale))

    def near_means(tile):
        pair = pair_of(ref.back_gather, tile)
        sums_here = group_sums_of(pair, channels)
        return [
            sums_here[2 * at + 1 : 2 * at + 2] / (numbers[at] * 2 / tiles) for at in range(2)
        ]

    def grad_product(piece):
        level = 1 - piece // 3
        product(piece, GRAD, level, piece % 3, [(0, (height, height // 2)[level])])

    def grads_came(pieces):
        for piece in pieces:
            first_copy(piece, GRAD, RECV).wait_recv()

    def centre(pieces):
        for piece in pieces:
            centre_grads(piece, *((coarse_gain, near[1]) if piece < 3 else (fine_gain, near[0])))

    def send(pieces):
        for piece in pieces:
            stage_copy(piece, 1).start()

    with jax.named_scope("grads_a"):
        for piece in range(4):
            grad_product(piece)
            send_first(piece, GRAD)
    with jax.named_scope("grads_wait"):
        near_copy.wait()
        near = near_means(me)
        for piece in range(3):
            grads_came([piece])
            centre([piece])
            send([piece])
        advance_rows(0)
    with jax.named_scope("grads_c"):
        grad_product(4)
        send_first(4, GRAD)
        grads_came([3])
    with jax.named_scope("grads_d"):
        grad_product(5)
        centre([3])
        send_first(5, GRAD)
        send([3])
    with jax.named_scope("close_a"):
        for piece in range(2):
            close_forms(piece)
        grads_came([4])
        centre([4])
        send([4])
        close_forms(2)
        grads_came([5])
        centre([5])
        send([5])
    with jax.named_scope("close_b"):
        for piece in range(3, PIECES):
            close_forms(piece)
    advance_rows(1)
    with jax.named_scope("back_wait"):
        back_copies.wait()
    back = group_sums_of(ordered_sum(ref.back_gather, tiles), channels)
    peers = {
        bit: (near_means(partners[bit]["tile"]), near_centres(partners[bit]["tile"]))
        for bit in {plan[1][0] for plan in plans}
    }

    def factors_of(piece):
        at = 1 - piece // 3
        mean, scale = stats[at]
        first = back[2 * at + 1 : 2 * at + 2] / numbers[at]
        second = back[2 * at : 2 * at + 1] / numbers[at] * scale * scale
        peer_near, peer_centres = peers[plans[piece][1][0]]
        return (
            scale,
            -second,
            scale * (near[at] - first) - second * (centres[at] - mean),
            scale * (peer_near[at] - first) - second * (peer_centres[at] - mean),
        )

    with jax.named_scope("join"):
        for piece in range(3):
            join(piece, factors_of(piece))
    with jax.named_scope("join_fine"):
        for piece in range(3, PIECES):
            join(piece, factors_of(piece))
    advance_rows(2)
    for stage in range(2, bits):
        with jax.named_scope("stage%d" % stage):
            for piece in range(PIECES):
                advance(piece, stage)
                if stage > 2 and piece == 4:
                    advance_rows(stage)
    scope = jax.named_scope("finish")
    scope.__enter__()
    sent = [(ref.parts[SEND, 0, stage], ref.stage_send.at[stage - 1]) for stage in range(1, bits)]
    sent += [(ref.parts[FSEND, 0, 1], ref.form_send.at[0])]
    sent += [(ref.parts[RECV, 0, 0], ref.first_send.at[0])]
    sent += [(ref.parts[COME, 0, 0], ref.first_send.at[1])]
    sent += [(final.at[pl.ds(0, slides - 1)], ref.piece_send.at[0])]
    for buffers, sem in sent:
        pltpu.make_async_copy(buffers, buffers, sem).wait()
    head_copies.wait()
    row_total = ordered_sum(ref.head_gather, slides)
    ref.heads[...] = row_total
    ref.heads[4 + classes : 5 + classes] = row_total[4 + classes : 5 + classes] / count
    for piece in range(PIECES):
        for copy in piece_copies(piece):
            copy.wait_recv()
        level, a = spans[piece][0] // across // 3, spans[piece][0] // across % 3
        whole = ordered_sum(final.at[:, :, pl.ds(*spans[piece])], slides)
        for b in range(3):
            ref.grads[pl.ds(6 * a + 2 * b + level, whole.shape[0], stride=18), :] = whole[
                :, b * channels : (b + 1) * channels
            ]
    scope.__exit__(None, None, None)


def per_device(
    fine_level,
    coarse_level,
    fine_kernel,
    coarse_kernel,
    fine_gain,
    fine_offset,
    coarse_gain,
    coarse_offset,
    class_kernel,
    class_offset,
    tissue_labels,
):
    tiles, slides = lax.axis_size("tile"), lax.axis_size("slide")
    bits = tiles.bit_length() - 1
    in_channels, _, channels = fine_kernel.shape
    classes = class_kernel.shape[0]
    fine, coarse, labels = fine_level[0], coarse_level[0], tissue_labels[0]
    height, width = fine.shape[0], fine.shape[1]
    fine_number = height * tiles * width * (channels // GROUPS)
    numbers = (float(fine_number), float(fine_number // 4))
    pixels, half = height * width, width // 2
    slide_ends = max(slides - 1, 1)
    chunk = in_channels // tiles
    row_count = -(-(5 + classes) // 8) * 8

    inputs = dict(
        fine=fine,
        fine_taps=fine_kernel.transpose(1, 0, 2),
        labels=labels,
        coarse=coarse,
        coarse_taps=coarse_kernel.transpose(1, 0, 2),
        fine_gain=fine_gain[None, :],
        fine_offset=fine_offset[None, :],
        coarse_gain=coarse_gain[None, :],
        coarse_offset=coarse_offset[None, :],
        class_kernel=class_kernel,
        class_offset=class_offset[None, :],
    )
    outputs = dict(
        heads=pltpu.VMEM((row_count, channels), F32),
        grads=pltpu.VMEM((chunk * 18, channels), F32),
    )
    line, lines = (1, channels), (4, channels)
    scratch = {
        name: pltpu.VMEM(value.shape, value.dtype)
        for name, value in inputs.items()
        if name not in ("fine", "coarse")
    }
    scratch |= dict(
        final=pltpu.VMEM((slides, chunk, 18 * channels), F32),
        head_gather=pltpu.VMEM((slides, row_count, channels), F32),
        load_sem=dma_sems(len(inputs)),
        fine_pad=pltpu.VMEM((height + 2, width, in_channels), BF16),
        coarse_pad=pltpu.VMEM((height // 2 + 2, half, in_channels), BF16),
        fine_conv=pltpu.VMEM((pixels, channels), F32),
        coarse_conv=pltpu.VMEM((pixels // 4, channels), F32),
        fine_begun=pltpu.VMEM((2 * width, 3 * channels), F32),
        coarse_begun=pltpu.VMEM((2 * half, 3 * channels), F32),
        fine_wide=pltpu.VMEM((pixels, 4 * channels), BF16),
        coarse_wide=pltpu.VMEM((pixels // 4, 4 * channels), BF16),
        fine_turned=pltpu.VMEM((in_channels, (height + 2) * width), BF16),
        coarse_turned=pltpu.VMEM((in_channels, (height // 2 + 2) * half), BF16),
        fine_shifted=pltpu.VMEM((pixels, 3 * channels), BF16),
        coarse_shifted=pltpu.VMEM((pixels // 4, 3 * channels), BF16),
        widen=pltpu.VMEM((height // 2, width, channels), F32),
        fold=pltpu.VMEM((height // 2, width, channels), F32),
        sums=pltpu.VMEM((8, channels), F32),
        rows=pltpu.VMEM((row_count, channels), F32),
        row_sums=pltpu.VMEM((bits + 1, row_count, channels), F32),
        row_gather=pltpu.VMEM((bits, row_count, channels), F32),
        row_send=dma_sems(bits),
        row_recv=dma_sems(bits),
        count=pltpu.VMEM(line, F32),
        stat=pltpu.VMEM(lines, F32),
        back=pltpu.VMEM(lines, F32),
        slide_count=pltpu.VMEM(line, F32),
        count_gather=pltpu.VMEM((tiles,) + line, F32),
        stat_gather=pltpu.VMEM((tiles,) + lines, F32),
        back_gather=pltpu.VMEM((tiles,) + lines, F32),
        total_gather=pltpu.VMEM((slides,) + line, F32),
        edge_send=dma_sems(2, 2),
        edge_recv=dma_sems(2, 2),
        near_send=dma_sems(2),
        near_recv=dma_sems(2),
        form_send=dma_sems(1),
        form_recv=dma_sems(PIECES),
        tile_send=dma_sems(3),
        tile_recv=dma_sems(3),
        slide_send=dma_sems(2),
        slide_recv=dma_sems(2),
        piece_send=dma_sems(1),
        piece_recv=dma_sems(PIECES, slide_ends),
        first_send=dma_sems(2),
        first_recv=dma_sems(2, PIECES),
        stage_send=dma_sems(bits - 1),
        stage_recv=dma_sems(PIECES, bits - 1),
    )
    parts = {}
    span = 3 * channels
    for piece in range(PIECES):
        parts[GRAD, piece, 0] = pltpu.VMEM((2,) * bits + (chunk, span), F32)
        plan = stage_plan(bits, order_of(bits, (piece + 1) % 2))
        forms = (chunk, 4 * channels)
        parts[FORM, piece, 0] = pltpu.VMEM((2,) * bits + forms, F32)
        parts[WINDOW, piece, 0] = pltpu.VMEM((2,) * (bits - 1) + (chunk, span), F32)
        parts[COME, 0, 0] = pltpu.VMEM((PIECES,) + (2,) * (bits - 1) + forms, F32)
        for stage, (_, _, left) in enumerate(plan):
            below = (2,) * left + (chunk, span)
            if stage:
                parts[RECV, piece, stage] = pltpu.VMEM(below, BF16)
            else:
                parts[RECV, 0, 0] = pltpu.VMEM((PIECES,) + below, F32)
            if stage == 1:
                wider = below[:-1] + (4 * channels,)
                parts[FSEND, 0, 1] = pltpu.VMEM((PIECES,) + wider, BF16)
                parts[FRECV, piece, 1] = pltpu.VMEM(wider, BF16)
                parts[FKEPT, piece, 1] = pltpu.VMEM(below, F32)
                parts[OTHER, piece, 1] = pltpu.VMEM(below, F32)
            if stage:
                parts[SEND, 0, stage] = pltpu.VMEM((PIECES,) + below, BF16)
                parts[KEPT, piece, stage] = pltpu.VMEM(below, F32)
    names = ["far_" + name for name in inputs] + list(outputs) + list(scratch)
    results = call(
        functools.partial(step_kernel, tiles, slides, bits, numbers, names, list(parts)),
        tuple(outputs.values()),
        list(scratch.values()) + list(parts.values()),
        tuple(inputs.values()),
    )
    loss, head, grads = store(*results, classes)
    return (loss[0, 0], head, grads.reshape(chunk, 9, 2, channels).transpose(0, 2, 1, 3))


def solution(mesh):
    return jax.shard_map(
        per_device,
        mesh=mesh,
        in_specs=(
            P("slide", "tile", None, None),
            P("slide", "tile", None, None),
            P(),
            P(),
            P(),
            P(),
            P(),
            P(),
            P(),
            P(),
            P("slide", "tile", None),
        ),
        out_specs=(P(), P(), P("tile", None, None, None)),
        check_vma=False,
    )
```
